32 devices in a mesh: section: 4 (over x, core), dp: 8 (over z, y).
Axes of the slice: x: 2, y: 2, z: 4, core: 2. Of those that a mesh axis runs over, the one named last changes fastest.
Arguments:
- activations: bfloat16 [4, 4, 2048, 1024], P('section', None, 'dp'), may hold values from -6 to 6
- section_weights: bfloat16 [4, 1024, 1024], P('section'), may hold values from -0.1875 to 0.1875
- cand_table: bfloat16 [128, 2048], replicated, may hold values from -6 to 6
- cand_index: int32 [4, 8, 64], P(None, 'dp'), may hold values from 0 to 127
- cand_count: int32 [4, 8], P(None, 'dp'), may hold values from 1 to 64, as said below
- pooled_cotangent: bfloat16 [4, 8, 1024], P(None, 'dp'), may hold values from -6 to 6
Outputs:
- weight_grads: float32 [4, 1024, 1024], P('section', 'dp')
- table_grads: float32 [128, 2048], P('dp', 'section')
The draws below stay inside these ranges and needn't reach their ends.
Inputs may be any that keep to these rules, and one draw needn't show every extreme that they name: `cand_count`: the first sample of every micro-batch has all 64 candidates valid.
All inputs are finite; a program needn't handle non-finite values.
Results may differ from the reference program's by a relative error of at most 0.014.
Values may be sent and summed in bfloat16 or wider, within the bound.
No kernel may reach another device: no remote copies, remote signals or barrier semaphores. Data moves between devices by JAX's collectives and lax.ppermute only.
A program may use at most 64 MiB of HBM per device.

```python
import math
import jax
import jax.numpy as jnp
from jax import lax

D = 1024
HEADS = 16
HEAD = 64
PATCH = 256
CAND = 64
MICRO = 4
SAMP = 1
NCAND = 128
SAMPLES = 8
ROWS = 2048
N_SECTION = 4
N_DP = 8


def draw_cand_count(key, part):
    counted = jax.random.randint(key, (MICRO, SAMPLES), 1, CAND + 1)
    return counted.at[:, 0].set(CAND).astype(jnp.int32)


def shared_pattern(key):
    anchor = jax.random.fold_in(key, 9173)
    head_pick = jax.random.randint(jax.random.fold_in(anchor, 1), (), 0, HEADS)
    sign_bits = jax.random.randint(jax.random.fold_in(anchor, 2), (HEAD,), 0, 2)
    signs = (2 * sign_bits - 1).astype(jnp.float32)
    column = jnp.arange(D, dtype=jnp.int32)
    inside = column // HEAD == head_pick
    tiled = jnp.tile(signs, HEADS)
    return (inside, tiled)


def base_noise(key, shape):
    values = jax.random.truncated_normal(jax.random.fold_in(key, 33), -6.0, 6.0, shape, jnp.float32)
    return jnp.clip(values, -6.0, 6.0)


def draw_activations(key, part):
    base = base_noise(jax.random.fold_in(key, 41), (N_SECTION, MICRO, ROWS, D))
    inside, signs = shared_pattern(key)
    level = jax.random.randint(jax.random.fold_in(key, 42), (MICRO, ROWS), 0, 16)
    strength = jnp.where(level == 0, 5.8, jnp.where(level == 1, 4.6, jnp.where(level == 2, 3.4, 0.0))).astype(jnp.float32)
    planted = (level < 3)[:, :, None] & inside[None, None, :]
    last_section = jnp.where(planted, strength[:, :, None] * signs[None, None, :], base[N_SECTION - 1])
    whole = jnp.concatenate([base[:N_SECTION - 1], last_section[None]], axis=0)
    return jnp.clip(whole, -6.0, 6.0).astype(jnp.bfloat16)


def draw_cand_table(key, part):
    base = base_noise(jax.random.fold_in(key, 51), (NCAND, 2 * D))
    inside, signs = shared_pattern(key)
    wobble = jnp.clip(0.4 * jax.random.normal(jax.random.fold_in(key, 52), (NCAND, D), jnp.float32), -1.0, 1.0)
    key_half = jnp.where(inside[None, :], signs[None, :] * (5.0 + wobble), base[:, :D])
    whole = jnp.concatenate([key_half, base[:, D:]], axis=1)
    return jnp.clip(whole, -6.0, 6.0).astype(jnp.bfloat16)


def set_ends(array, key, low, high):
    extent = array.shape
    place = [jax.random.randint(jax.random.fold_in(key, axis), (), 0, extent[axis]) for axis in range(len(extent))]
    array = array.at[tuple(place)].set(low)
    longest = extent.index(max(extent))
    place[longest] = (place[longest] + 1) % extent[longest]
    return array.at[tuple(place)].set(high)


def block_scale(own_key, shape, split, low, largest):
    factor_of = 1.0
    for axis_at, shards_of in split:
        steps = jax.random.uniform(jax.random.fold_in(jax.random.fold_in(own_key, 6), axis_at), (shards_of,), jnp.float32, low / len(split), largest / len(split))
        factor_of = factor_of * jnp.repeat(jnp.exp(steps), shape[axis_at] // shards_of).reshape((-1,) + (1,) * (len(shape) - 1 - axis_at))
    return factor_of


def scatter_about(own_key, extent, scale, reach, shards=(), held_as=jnp.bfloat16):
    entries = jax.random.normal(own_key, extent, jnp.float32) * scale
    if len(shards) > 0:
        entries = block_scale(own_key, extent, shards, -0.22, 0.18) * entries
    return jnp.clip(entries, min=-reach, max=reach).astype(held_as)


def setup_inputs(seed: int = 0) -> dict:
    key_of = jax.random.split(jax.random.key(seed), 7)
    activations = draw_activations(jax.random.fold_in(key_of[6], 71), 0)
    section_weights = scatter_about(key_of[1], (N_SECTION, D, D), D ** -0.5, 0.1875, ((0, 4),))
    cand_table = draw_cand_table(jax.random.fold_in(key_of[6], 71), 0)
    cand_index = set_ends(jax.random.randint(key_of[3], (MICRO, SAMPLES, CAND), 0, NCAND), jax.random.fold_in(key_of[3], 1), 0, NCAND - 1).astype(jnp.int32)
    cand_count = draw_cand_count(jax.random.fold_in(key_of[6], 71), 0)
    pooled_cotangent = scatter_about(key_of[5], (MICRO, SAMPLES, D), 1.0, 6.0, ((1, 8),))
    return {"activations": activations, "section_weights": section_weights, "cand_table": cand_table, "cand_index": cand_index, "cand_count": cand_count, "pooled_cotangent": pooled_cotangent}


def attend(outputs, keys_values, allowed):
    samples, cands, double = keys_values.shape
    model_width = double // 2
    heads = model_width // HEAD
    queries = outputs.reshape(samples, -1, heads, HEAD)
    keys = keys_values[:, :, :model_width].reshape(samples, cands, heads, HEAD)
    values = keys_values[:, :, model_width:].reshape(samples, cands, heads, HEAD)
    scores = jnp.einsum('nphd,nchd->nhpc', queries, keys) / math.sqrt(HEAD)
    scores = jnp.where(allowed[:, None, None, :], scores, -1e+30)
    attention = jax.nn.softmax(scores, axis=-1)
    mixed = jnp.einsum('nhpc,nchd->nphd', attention, values)
    return mixed.reshape(outputs.shape)

def section_back(inputs, weight, keys_values, allowed, upstream, is_final):
    hidden = jnp.dot(inputs, weight, preferred_element_type=jnp.float32)
    outputs = inputs.astype(jnp.float32) + jax.nn.gelu(hidden)
    if is_final:
        samples = keys_values.shape[0]

        def branch_fn(rows, table_rows):
            shaped = rows.reshape(samples, -1, rows.shape[1])
            return attend(shaped, table_rows, allowed).reshape(rows.shape)
        _, pull = jax.vjp(branch_fn, outputs, keys_values.astype(jnp.float32))
        extra_grad, kv_grad = pull(upstream)
        total_grad = upstream + extra_grad
    else:
        kv_grad = jnp.zeros(keys_values.shape, jnp.float32)
        total_grad = upstream
    _, gelu_pull = jax.vjp(jax.nn.gelu, hidden)
    delta_rows = gelu_pull(total_grad)[0].astype(jnp.bfloat16)
    input_grad = (total_grad + jnp.dot(delta_rows, weight.T, preferred_element_type=jnp.float32)).astype(jnp.bfloat16)
    return (input_grad, delta_rows, kv_grad)

def reference(activations, section_weights, cand_table, cand_index, cand_count, pooled_cotangent):
    row_count = SAMP * PATCH

    def replica(state_carry, replica_id):
        weight_sum, table_sum = state_carry
        weight_terms = jnp.zeros((N_SECTION, D, D), jnp.float32)
        table_terms = jnp.zeros((NCAND, 2 * D), jnp.float32)
        first_sample = (replica_id * SAMP).astype(jnp.int32)
        first_row = (first_sample * PATCH).astype(jnp.int32)
        for micro_id in range(MICRO):
            picked = lax.dynamic_slice_in_dim(cand_index[micro_id], first_sample, SAMP, 0)
            counted = lax.dynamic_slice_in_dim(cand_count[micro_id], first_sample, SAMP, 0)
            allowed = jnp.arange(CAND, dtype=jnp.int32)[None, :] < counted[:, None]
            keys_values = jnp.take(cand_table, picked, axis=0)
            pooled = lax.dynamic_slice_in_dim(pooled_cotangent[micro_id], first_sample, SAMP, 0)
            upstream = jnp.repeat(pooled.astype(jnp.float32) / PATCH, PATCH, axis=0)
            inputs = lax.dynamic_slice_in_dim(activations[N_SECTION - 1, micro_id], first_row, row_count, 0)
            input_grad, delta_rows, kv_grad = section_back(inputs, section_weights[N_SECTION - 1], keys_values, allowed, upstream, True)
            weight_terms = weight_terms.at[N_SECTION - 1].add(jnp.dot(inputs.T, delta_rows, preferred_element_type=jnp.float32))
            table_terms = table_terms.at[picked.reshape(-1)].add(kv_grad.reshape(-1, 2 * D))

            def descend(grad_in, section_id):
                rows_in = lax.dynamic_slice_in_dim(activations[section_id, micro_id], first_row, row_count, 0)
                grad_out, delta_section, _ = section_back(rows_in, section_weights[section_id], keys_values, allowed, grad_in, False)
                return (grad_out.astype(jnp.float32), jnp.dot(rows_in.T, delta_section, preferred_element_type=jnp.float32))
            _, lower_terms = lax.scan(descend, input_grad.astype(jnp.float32), jnp.arange(N_SECTION - 2, -1, -1, dtype=jnp.int32))
            weight_terms = weight_terms.at[:N_SECTION - 1].add(lower_terms[::-1])
        rounded = lax.optimization_barrier(weight_terms.astype(jnp.bfloat16))
        return ((weight_sum + rounded.astype(jnp.float32), table_sum + table_terms), None)
    initial = (jnp.zeros((N_SECTION, D, D), jnp.float32), jnp.zeros((NCAND, 2 * D), jnp.float32))
    (weight_sum, table_sum), _ = lax.scan(replica, initial, jnp.arange(N_DP, dtype=jnp.int32))
    return (weight_sum, table_sum)
```

```python
import math

import jax
import jax.numpy as jnp
from jax import lax
from jax.sharding import PartitionSpec as P

HEAD = 64
CHUNKS = 2


def attend(outputs, keys_values, allowed):
    samples, cands, double = keys_values.shape
    model_width = double // 2
    heads = model_width // HEAD
    queries = outputs.reshape(samples, -1, heads, HEAD)
    keys = keys_values[:, :, :model_width].reshape(samples, cands, heads, HEAD)
    values = keys_values[:, :, model_width:].reshape(samples, cands, heads, HEAD)
    scores = jnp.einsum("nphd,nchd->nhpc", queries, keys) / math.sqrt(HEAD)
    scores = jnp.where(allowed[:, None, None, :], scores, -1e30)
    attention = jax.nn.softmax(scores, axis=-1)
    mixed = jnp.einsum("nhpc,nchd->nphd", attention, values)
    return mixed.reshape(outputs.shape)


def halve(block, bit, axes, pairs_of):
    mine = (lax.axis_index("dp") >> bit) & 1
    keep = lax.dynamic_index_in_dim(block, mine, 0, keepdims=False)
    send = lax.dynamic_index_in_dim(block, 1 - mine, 0, keepdims=False)
    got = lax.ppermute(send.astype(jnp.bfloat16), axes, pairs_of(bit))
    return keep.astype(jnp.float32) + got.astype(jnp.float32)


def scatter_sum(block, replicas, axes, pairs_of):
    steps = replicas.bit_length() - 1
    rows, columns = block.shape
    block = block.reshape((2,) * steps + (rows // replicas, columns))
    for bit in range(steps):
        block = jnp.moveaxis(block, steps - bit - 1, 0)
        block = halve(block, bit, axes, pairs_of)
    return block


def body(activations, section_weights, cand_table, cand_index, cand_count, pooled_cotangent):
    sections = lax.axis_size("section")
    replicas = lax.axis_size("dp")
    position = lax.axis_index("section")
    last = sections - 1
    final_flag = position == last
    acts = activations[0]
    weight = section_weights[0]
    micro_count, row_count, model_width = acts.shape
    samples = cand_index.shape[1]
    cands = cand_index.shape[2]
    patches = row_count // samples
    table_rows = cand_table.shape[0]

    def first(m):
        inputs = acts[m]

        def forward():
            hidden = jnp.dot(inputs, weight, preferred_element_type=jnp.float32)
            return hidden, jax.vjp(jax.nn.gelu, hidden)

        def final_back():
            hidden, (gelu, gelu_pull) = forward()
            outputs = inputs.astype(jnp.float32) + gelu
            picked = cand_index[m]
            allowed = jnp.arange(cands, dtype=jnp.int32)[None, :] < cand_count[m][:, None]
            keys_values = jnp.take(cand_table, picked, axis=0)
            upstream = jnp.repeat(pooled_cotangent[m].astype(jnp.float32) / patches, patches, axis=0)

            def branch_fn(rows, taken):
                shaped = rows.reshape(samples, -1, rows.shape[1])
                return attend(shaped, taken, allowed).reshape(rows.shape)

            _, pull = jax.vjp(branch_fn, outputs, keys_values.astype(jnp.float32))
            extra_grad, kv_grad = pull(upstream)
            total_grad = upstream + extra_grad
            delta = gelu_pull(total_grad)[0].astype(jnp.bfloat16)
            grad = total_grad + jnp.dot(delta, weight.T, preferred_element_type=jnp.float32)
            onehot = (
                picked.reshape(-1)[:, None] == jnp.arange(table_rows, dtype=jnp.int32)[None, :]
            ).astype(jnp.float32)
            part = jnp.dot(
                onehot.T,
                kv_grad.reshape(-1, 2 * model_width),
                precision=lax.Precision.HIGHEST,
                preferred_element_type=jnp.float32,
            )
            return grad.astype(jnp.bfloat16), delta.astype(jnp.float32), part

        def plain():
            hidden, (_, gelu_pull) = forward()
            slope = gelu_pull(jnp.ones_like(hidden))[0]
            return inputs, slope, jnp.zeros((table_rows, 2 * model_width), jnp.float32)

        return lax.cond(final_flag, final_back, plain)

    grads, aux, table_part = [], [], jnp.zeros((table_rows, 2 * model_width), jnp.float32)
    for m in range(micro_count):
        grad, extra, part = first(m)
        grads.append(grad)
        aux.append(extra)
        table_part = table_part + part

    arrived = [jnp.zeros((row_count, model_width), jnp.bfloat16)] * micro_count
    for hop in range(last):
        source = last - hop
        received = [lax.ppermute(g, "section", [(source, source - 1)]) for g in grads]
        arrived = [a + r for a, r in zip(arrived, received)]
        if hop + 1 < last:

            def back(m):
                def active():
                    total = received[m].astype(jnp.float32)
                    delta = (total * aux[m]).astype(jnp.bfloat16)
                    grad = total + jnp.dot(delta, weight.T, preferred_element_type=jnp.float32)
                    return grad.astype(jnp.bfloat16)

                return lax.cond(position == source - 1, active, lambda: received[m])

            grads = [back(m) for m in range(micro_count)]

    def table_pairs(bit):
        return [(last * replicas + i, last * replicas + (i ^ (1 << bit))) for i in range(replicas)]

    own_table = scatter_sum(table_part, replicas, ("section", "dp"), table_pairs)
    width = 2 * model_width // sections
    spread = jnp.zeros((table_rows // replicas, width), jnp.float32)
    for s in range(last):
        piece = own_table[:, s * width : (s + 1) * width].astype(jnp.bfloat16)
        spread = spread + lax.ppermute(piece, "section", [(last, s)]).astype(jnp.float32)
    table_sum = jnp.where(final_flag, own_table[:, last * width :], spread)

    def delta_of(m):
        return lax.cond(
            final_flag,
            lambda: aux[m].astype(jnp.bfloat16),
            lambda: (arrived[m].astype(jnp.float32) * aux[m]).astype(jnp.bfloat16),
        )

    delta = jnp.concatenate([delta_of(m) for m in range(micro_count)], axis=0)
    inputs = acts.reshape(micro_count * row_count, model_width)

    def pairs(bit):
        return [(i, i ^ (1 << bit)) for i in range(replicas)]

    sums = []
    step = model_width // CHUNKS
    for c in range(CHUNKS):
        part = jnp.dot(inputs.T, delta[:, c * step : (c + 1) * step], preferred_element_type=jnp.float32)
        part = part.astype(jnp.bfloat16)
        sums.append(scatter_sum(part, replicas, "dp", pairs))
    return jnp.concatenate(sums, axis=1)[None], table_sum


def solution(mesh):
    in_specs = (
        P("section", None, "dp", None),
        P("section", None, None),
        P(),
        P(None, "dp", None),
        P(None, "dp"),
        P(None, "dp", None),
    )
    out_specs = (P("section", "dp", None), P("dp", "section"))
    return jax.shard_map(body, mesh=mesh, in_specs=in_specs, out_specs=out_specs, check_vma=False)
```

```python
import functools
import math

import jax
import jax.numpy as jnp
from jax import lax
from jax.experimental import pallas as pl
from jax.experimental.pallas import tpu as pltpu
from jax.sharding import PartitionSpec as P

HEAD = 64
PAIR = 2 * HEAD
TILE = 256
CHUNKS = (0.5, 0.25, 0.25)
MIB = 1024 * 1024
ANY = pl.BlockSpec(memory_space=pl.ANY)
VMEM = pl.BlockSpec(memory_space=pltpu.VMEM)
SMEM = pl.BlockSpec(memory_space=pltpu.SMEM)
BF16 = jnp.bfloat16
F32 = jnp.float32

NN = (((1,), (0,)), ((), ()))
NT = (((1,), (1,)), ((), ()))
TN = (((0,), (0,)), ((), ()))


def dot(left, right, dims):
    return lax.dot_general(left, right, dims, preferred_element_type=F32)


def gelu_parts(hidden):
    root = math.sqrt(2.0 / math.pi)
    square = hidden * hidden
    bent = jnp.tanh(root * hidden * (1.0 + 0.044715 * square))
    share = 0.5 + 0.5 * bent
    slope = share + (0.5 * root) * hidden * (1.0 - bent * bent) * (1.0 + (3 * 0.044715) * square)
    return hidden * share, slope


def high_low(values):
    high = values.astype(BF16)
    return high, (values - high.astype(F32)).astype(BF16)


def first_kernel(
    flag_ref, count_ref, index_ref, acts_ref, weight_ref, table_ref, pooled_ref,
    grad_ref, aux_ref, turned_ref, kv_ref, total_ref,
):
    rows, width = acts_ref.shape
    table_rows = table_ref.shape[0]
    tiles = width // TILE

    @pl.when(flag_ref[0] == 0)
    def _():
        @pl.loop(0, tiles)
        def _(q):
            cols = pl.ds(pl.multiple_of(q * TILE, TILE), TILE)
            hidden = dot(acts_ref[...], weight_ref[:, cols], NN)
            aux_ref[:, cols] = gelu_parts(hidden)[1].astype(BF16)

    @pl.when(flag_ref[0] == 1)
    def _():
        onehot = (lax.broadcasted_iota(jnp.int32, (table_rows, PAIR), 0) == index_ref[...]).astype(BF16)
        own = (
            lax.broadcasted_iota(jnp.int32, (PAIR, PAIR), 0) // HEAD
            == lax.broadcasted_iota(jnp.int32, (PAIR, PAIR), 1) // HEAD
        )
        allowed = lax.broadcasted_iota(jnp.int32, (2, HEAD, rows), 1) < count_ref[0]
        left_half = lax.broadcasted_iota(jnp.int32, (HEAD, PAIR), 1) < HEAD

        @pl.loop(0, tiles)
        def _(q):
            base = pl.multiple_of(q * TILE, TILE)
            cols = pl.ds(base, TILE)
            hidden = dot(acts_ref[...], weight_ref[:, cols], NN)
            bent, slope = gelu_parts(hidden)
            outputs = acts_ref[:, cols].astype(F32) + bent
            high, low = high_low(outputs)
            keys = dot(onehot, table_ref[:, cols], TN)
            values = dot(onehot, table_ref[:, pl.ds(pl.multiple_of(width + q * TILE, TILE), TILE)], TN)
            pooled = jnp.broadcast_to(pooled_ref[:, cols].astype(F32), (rows, TILE))
            for j in range(TILE // PAIR):
                here = slice(j * PAIR, (j + 1) * PAIR)
                key = jnp.where(own, keys[:, here], 0.0).astype(BF16)
                value = jnp.where(own, values[:, here], 0.0).astype(BF16)
                given = pooled[:, here]
                scores = dot(
                    jnp.concatenate([key, key], axis=1),
                    jnp.concatenate([high[:, here], low[:, here]], axis=1),
                    NT,
                ).reshape(2, HEAD, rows)
                scores = jnp.where(allowed, scores * (1.0 / math.sqrt(HEAD)), -1e30)
                raised = jnp.exp(scores - jnp.max(scores, axis=1, keepdims=True))
                share = raised / jnp.sum(raised, axis=1, keepdims=True)
                worth = dot(value, given.astype(BF16), NT).reshape(2, HEAD, rows)
                centre = jnp.sum(share * worth, axis=1, keepdims=True)
                slant = share * (worth - centre) * (1.0 / (rows * math.sqrt(HEAD)))
                slant = slant.reshape(PAIR, rows).astype(BF16)
                share = share.reshape(PAIR, rows).astype(BF16)
                total = given * (1.0 / rows) + dot(slant, key, TN)
                there = pl.ds(pl.multiple_of(base + j * PAIR, PAIR), PAIR)
                total_ref[:, there] = total
                aux_ref[:, there] = (total * slope[:, here]).astype(BF16)
                key_grad = dot(slant, high[:, here], NN)
                value_grad = dot(share, given.astype(BF16), NN) * (1.0 / rows)
                kv_ref[:, there] = jnp.where(left_half, key_grad[:HEAD], key_grad[HEAD:])
                kv_ref[:, pl.ds(pl.multiple_of(width + base + j * PAIR, PAIR), PAIR)] = jnp.where(
                    left_half, value_grad[:HEAD], value_grad[HEAD:]
                )

        @pl.loop(0, tiles)
        def _(q):
            cols = pl.ds(pl.multiple_of(q * TILE, TILE), TILE)
            grad_ref[:, cols] = (total_ref[:, cols] + dot(aux_ref[...], weight_ref[cols, :], NT)).astype(BF16)

    turned_ref[...] = acts_ref[...].T


def first_call(flag, count, index, acts, weight, table, pooled):
    rows, width = acts.shape
    cands = index.shape[1] // 2
    shape = jax.ShapeDtypeStruct
    return pl.pallas_call(
        first_kernel,
        out_shape=(
            shape((rows, width), BF16),
            shape((rows, width), BF16),
            shape((width, rows), BF16),
            shape((cands, 2 * width), F32),
        ),
        in_specs=[SMEM, SMEM] + [VMEM] * 5,
        out_specs=(VMEM,) * 4,
        scratch_shapes=[pltpu.VMEM((rows, width), F32)],
        compiler_params=pltpu.CompilerParams(vmem_limit_bytes=24 * MIB),
        cost_estimate=pl.CostEstimate(flops=8 * rows * width * width, bytes_accessed=6 * MIB, transcendentals=0),
        name="first",
    )(flag, count, index, acts, weight, table, pooled)


def hop_kernel(with_grad, flag_ref, came_hbm, aux_hbm, weight_hbm, *rest):
    if with_grad:
        grad_hbm, aux_out, came, aux, weight, grad, sems = rest
    else:
        aux_out, came, aux, sems = rest
    width = came.shape[1]
    tiles = width // TILE

    @pl.when(flag_ref[0] == 1)
    def _():
        first = pltpu.make_async_copy(came_hbm, came, sems.at[0])
        second = pltpu.make_async_copy(aux_hbm, aux, sems.at[1])
        first.start()
        second.start()
        loads, stores = [], []
        if with_grad:
            for n in range(tiles):
                part = pl.ds(n * TILE, TILE)
                loads.append(pltpu.make_async_copy(weight_hbm.at[part], weight.at[part], sems.at[3 + n]))
                stores.append(
                    pltpu.make_async_copy(grad.at[:, part], grad_hbm.at[:, part], sems.at[3 + tiles + n])
                )
                loads[n].start()
        first.wait()
        second.wait()
        aux[...] = (came[...].astype(F32) * aux[...].astype(F32)).astype(BF16)
        back = pltpu.make_async_copy(aux, aux_out, sems.at[2])
        back.start()
        for n in range(len(loads)):
            part = pl.ds(n * TILE, TILE)
            loads[n].wait()
            grad[:, part] = (came[:, part].astype(F32) + dot(aux[...], weight[part, :], NT)).astype(BF16)
            stores[n].start()
        for store in stores:
            store.wait()
        back.wait()


def hop_call(flag, came, aux, weight, with_grad):
    rows, width = came.shape
    tiles = width // TILE
    block = jax.ShapeDtypeStruct((rows, width), BF16)
    scratch = [pltpu.VMEM((rows, width), BF16)] * 2
    if with_grad:
        scratch += [pltpu.VMEM((width, width), BF16), pltpu.VMEM((rows, width), BF16)]
    scratch.append(pltpu.SemaphoreType.DMA((3 + 2 * tiles,)))
    outs = (block, block) if with_grad else (block,)
    return pl.pallas_call(
        functools.partial(hop_kernel, with_grad),
        out_shape=outs,
        in_specs=[SMEM, ANY, ANY, ANY],
        out_specs=(ANY,) * len(outs),
        scratch_shapes=scratch,
        input_output_aliases={2: len(outs) - 1},
        compiler_params=pltpu.CompilerParams(vmem_limit_bytes=16 * MIB),
        cost_estimate=pl.CostEstimate(flops=2 * rows * width * width, bytes_accessed=4 * MIB, transcendentals=0),
        name="hop" if with_grad else "end",
    )(flag, came, aux, weight)


def block_order(replicas):
    steps = replicas.bit_length() - 1
    order = []
    for i in range(replicas // 2):
        bits = [(i >> (steps - 2 - k)) & 1 for k in range(steps - 1)]
        order.append(sum(bit << (k + 1) for k, bit in enumerate(bits)))
    return order


def weight_kernel(replicas, widths, parity_ref, *refs):
    count = (len(refs) - 3 - 2 * len(widths)) // 2
    turned_hbm, delta_hbm = refs[:count], refs[count : 2 * count]
    outs = refs[2 * count : 2 * count + 2 * len(widths)]
    turned, delta, sems = refs[-3:]
    width = delta.shape[1]
    rows = delta.shape[0] // count
    size = width // replicas
    half = width // 2
    order = block_order(replicas)
    mine = parity_ref[0]
    copies = []
    for m in range(count):
        copies.append(
            pltpu.make_async_copy(delta_hbm[m], delta.at[pl.ds(m * rows, rows)], sems.at[len(copies)])
        )
        for which in range(2):
            low_bit = 1 - mine if which == 0 else mine
            for i, block in enumerate(order):
                source = pl.ds(pl.multiple_of((block + low_bit) * size, size), size)
                target = pl.ds(which * half + i * size, size)
                copies.append(
                    pltpu.make_async_copy(
                        turned_hbm[m].at[source],
                        turned.at[target, pl.ds(m * rows, rows)],
                        sems.at[len(copies)],
                    )
                )
    for copy in copies:
        copy.start()
    for copy in copies:
        copy.wait()
    for which in range(2):
        begin = 0
        for c, span in enumerate(widths):
            out = outs[2 * c + which]
            for at in range(0, span, TILE):
                cols = slice(begin + at, begin + at + TILE)
                product = dot(turned[which * half : (which + 1) * half], delta[:, cols], NN)
                out[:, at : at + TILE] = product.astype(out.dtype)
            begin += span


def weight_call(parity, turned, deltas, replicas, widths):
    rows, width = deltas[0].shape
    count = len(deltas)
    outs = []
    for span in widths:
        outs += [jax.ShapeDtypeStruct((width // 2, span), BF16), jax.ShapeDtypeStruct((width // 2, span), F32)]
    return pl.pallas_call(
        functools.partial(weight_kernel, replicas, widths),
        out_shape=tuple(outs),
        in_specs=[SMEM] + [ANY] * (2 * count),
        out_specs=(VMEM,) * len(outs),
        scratch_shapes=[
            pltpu.VMEM((width, count * rows), BF16),
            pltpu.VMEM((count * rows, width), BF16),
            pltpu.SemaphoreType.DMA((count * (replicas + 1),)),
        ],
        compiler_params=pltpu.CompilerParams(vmem_limit_bytes=32 * MIB),
        cost_estimate=pl.CostEstimate(
            flops=2 * count * rows * width * width, bytes_accessed=8 * MIB, transcendentals=0
        ),
        name="weight",
    )(parity, *turned, *deltas)


def own_half(keep, got, bit):
    mine = (lax.axis_index("dp") >> bit) & 1

    def pick(which):
        return lax.dynamic_index_in_dim(keep, which, 0, keepdims=False) + lax.dynamic_index_in_dim(
            got, which, 0, keepdims=False
        ).astype(F32)

    return pick(1 - mine).astype(BF16), pick(mine)


def finish_scatter(send, keep, replicas, axes, pairs_of):
    steps = replicas.bit_length() - 1
    rows, columns = keep.shape
    for bit in range(steps):
        got = lax.ppermute(send, axes, pairs_of(bit))
        if bit + 1 < steps:
            lead = (2, keep.shape[0] // 2, columns)
            send, keep = own_half(keep.reshape(lead), got.reshape(lead), bit + 1)
    return keep + got.astype(F32)


def body(activations, section_weights, cand_table, cand_index, cand_count, pooled_cotangent):
    sections = lax.axis_size("section")
    replicas = lax.axis_size("dp")
    position = lax.axis_index("section")
    replica = lax.axis_index("dp")
    last = sections - 1
    final_flag = position == last
    acts = activations[0]
    weight = section_weights[0]
    micro_count, row_count, model_width = acts.shape
    table_rows = cand_table.shape[0]

    def flag(truth):
        return truth.astype(jnp.int32).reshape(1)

    index = jnp.concatenate([cand_index, cand_index], axis=2)
    grads, aux, turned, kv = [], [], [], []
    for m in range(micro_count):
        out = first_call(
            flag(final_flag), cand_count[m], index[m], acts[m], weight, cand_table, pooled_cotangent[m]
        )
        for kept, item in zip((grads, aux, turned, kv), out):
            kept.append(item)

    for hop in range(last):
        source = last - hop
        received = [lax.ppermute(g, "section", [(source, source - 1)]) for g in grads]
        active = flag(position == source - 1)
        for m in range(micro_count):
            if hop + 1 < last:
                grads[m], aux[m] = hop_call(active, received[m], aux[m], weight, True)
            else:
                (aux[m],) = hop_call(active, received[m], aux[m], weight, False)

    def table_pairs(bit):
        return [(last * replicas + i, last * replicas + (i ^ (1 << bit))) for i in range(replicas)]

    def pairs(bit):
        return [(i, i ^ (1 << bit)) for i in range(replicas)]

    def table_parts():
        onehot = (
            cand_index.reshape(-1)[:, None] == jnp.arange(table_rows, dtype=jnp.int32)[None, :]
        ).astype(BF16)
        high, low = high_low(jnp.concatenate(kv, axis=0))
        part = dot(onehot, high, TN) + dot(onehot, low, TN)
        blocks = part.reshape(replicas, -1)[jnp.array([b + bit for bit in (0, 1) for b in block_order(replicas)])]
        return blocks.reshape(2, table_rows // 2, 2 * model_width)

    parts = lax.cond(
        final_flag, table_parts, lambda: jnp.zeros((2, table_rows // 2, 2 * model_width), F32)
    )
    table_send = lax.dynamic_index_in_dim(parts, 1 - (replica & 1), 0, keepdims=False).astype(BF16)
    table_keep = lax.dynamic_index_in_dim(parts, replica & 1, 0, keepdims=False)
    own_table = finish_scatter(table_send, table_keep, replicas, ("section", "dp"), table_pairs)
    width = 2 * model_width // sections
    spread = jnp.zeros((table_rows // replicas, width), F32)
    for s in range(last):
        piece = own_table[:, s * width : (s + 1) * width].astype(BF16)
        spread = spread + lax.ppermute(piece, "section", [(last, s)]).astype(F32)
    table_sum = jnp.where(final_flag, own_table[:, last * width :], spread)

    widths = tuple(int(part * model_width) for part in CHUNKS)
    pieces = weight_call((replica & 1).reshape(1), turned, aux, replicas, widths)
    sums = [
        finish_scatter(pieces[2 * c], pieces[2 * c + 1], replicas, "dp", pairs) for c in range(len(widths))
    ]
    return jnp.concatenate(sums, axis=1)[None], table_sum


def solution(mesh):
    in_specs = (
        P("section", None, "dp", None),
        P("section", None, None),
        P(),
        P(None, "dp", None),
        P(None, "dp"),
        P(None, "dp", None),
    )
    out_specs = (P("section", "dp", None), P("dp", "section"))
    return jax.shard_map(body, mesh=mesh, in_specs=in_specs, out_specs=out_specs, check_vma=False)
```

```python
import functools
import math

import jax
import jax.numpy as jnp
from jax import lax
from jax.experimental import pallas as pl
from jax.experimental.pallas import tpu as pltpu
from jax.sharding import PartitionSpec as P

HEAD = 64
PAIR = 2 * HEAD
TILE = 256
CHUNKS = (0.5, 0.25, 0.25)
MIB = 1024 * 1024
ANY = pl.BlockSpec(memory_space=pl.ANY)
VMEM = pl.BlockSpec(memory_space=pltpu.VMEM)
SMEM = pl.BlockSpec(memory_space=pltpu.SMEM)
BF16 = jnp.bfloat16
F32 = jnp.float32

NN = (((1,), (0,)), ((), ()))
NT = (((1,), (1,)), ((), ()))
TN = (((0,), (0,)), ((), ()))


def dot(left, right, dims):
    return lax.dot_general(left, right, dims, preferred_element_type=F32)


def gelu_parts(hidden):
    root = math.sqrt(2.0 / math.pi)
    square = hidden * hidden
    bent = jnp.tanh(root * hidden * (1.0 + 0.044715 * square))
    share = 0.5 + 0.5 * bent
    slope = share + (0.5 * root) * hidden * (1.0 - bent * bent) * (1.0 + (3 * 0.044715) * square)
    return hidden * share, slope


def high_low(values):
    high = values.astype(BF16)
    return high, (values - high.astype(F32)).astype(BF16)


def first_kernel(
    m, flag_ref, count_ref, acts_hbm, weight_ref, table_ref, index_ref, pooled_ref,
    grad_ref, aux_ref, slant_hbm, share_hbm, high_hbm, acts, slant_ref, share_ref, high_ref, sems,
):
    rows, width = acts.shape
    table_rows = table_ref.shape[0]
    pairs = width // PAIR
    load = pltpu.make_async_copy(acts_hbm.at[m], acts, sems.at[0])
    load.start()

    @pl.when(flag_ref[0] == 0)
    def _():
        load.wait()
        for q in range(width // TILE):
            cols = slice(q * TILE, (q + 1) * TILE)
            hidden = dot(acts[...], weight_ref[:, cols], NN)
            aux_ref[:, cols] = gelu_parts(hidden)[1].astype(BF16)

    @pl.when(flag_ref[0] == 1)
    def _():
        index = index_ref[m]
        index = jnp.concatenate([index, index], axis=1)
        onehot = (lax.broadcasted_iota(jnp.int32, (table_rows, PAIR), 0) == index).astype(BF16)
        gathered = dot(onehot, table_ref[...], TN)
        own = (
            lax.broadcasted_iota(jnp.int32, (PAIR, width), 0) // HEAD
            == lax.broadcasted_iota(jnp.int32, (PAIR, width), 1) // HEAD % 2
        )
        keys = jnp.where(own, gathered[:, :width] * (1.0 / math.sqrt(HEAD)), 0.0).astype(BF16)
        values = jnp.where(own, gathered[:, width:], 0.0).astype(BF16)
        allowed = lax.broadcasted_iota(jnp.int32, (2, HEAD, rows), 1) < count_ref[m, 0]
        given_row = pooled_ref[m].astype(F32) * (1.0 / rows)
        given = jnp.broadcast_to(given_row, (rows, width)).astype(BF16)
        worths = [
            dot(values[:, j * PAIR : (j + 1) * PAIR], given[:, j * PAIR : (j + 1) * PAIR], NT)
            for j in range(pairs)
        ]
        load.wait()
        slopes, scores = [], []
        for q in range(width // TILE):
            cols = slice(q * TILE, (q + 1) * TILE)
            hidden = dot(acts[...], weight_ref[:, cols], NN)
            bent, slope = gelu_parts(hidden)
            high, low = high_low(acts[:, cols].astype(F32) + bent)
            high_ref[:, cols] = high
            slopes.append(slope)
            for j in range(TILE // PAIR):
                here = slice(j * PAIR, (j + 1) * PAIR)
                key = keys[:, q * TILE + j * PAIR : q * TILE + (j + 1) * PAIR]
                scores.append(
                    dot(
                        jnp.concatenate([key, key], axis=1),
                        jnp.concatenate([high[:, here], low[:, here]], axis=1),
                        NT,
                    )
                )
        stores = [pltpu.make_async_copy(high_ref, high_hbm, sems.at[1])]
        stores[0].start()
        slants = []
        for j in range(pairs):
            score = jnp.where(allowed, scores[j].reshape(2, HEAD, rows), -1e30)
            raised = jnp.exp(score - jnp.max(score, axis=1, keepdims=True))
            share = raised * (1.0 / jnp.sum(raised, axis=1, keepdims=True))
            worth = worths[j].reshape(2, HEAD, rows)
            centre = jnp.sum(share * worth, axis=1, keepdims=True)
            slant = (share * (worth - centre)).reshape(PAIR, rows).astype(BF16)
            slants.append(slant)
            slant_ref[j * PAIR : (j + 1) * PAIR] = slant
            share_ref[j * PAIR : (j + 1) * PAIR] = share.reshape(PAIR, rows).astype(BF16)
        stores.append(pltpu.make_async_copy(slant_ref, slant_hbm, sems.at[2]))
        stores.append(pltpu.make_async_copy(share_ref, share_hbm, sems.at[3]))
        stores[1].start()
        stores[2].start()
        totals = []
        for j in range(pairs):
            here = slice(j * PAIR, (j + 1) * PAIR)
            part = slice(j * PAIR % TILE, j * PAIR % TILE + PAIR)
            total = given_row[:, here] + dot(slants[j], keys[:, here], TN)
            totals.append(total)
            aux_ref[:, here] = (total * slopes[j * PAIR // TILE][:, part]).astype(BF16)
        for j in range(pairs):
            here = slice(j * PAIR, (j + 1) * PAIR)
            grad_ref[:, here] = (totals[j] + dot(aux_ref[...], weight_ref[here, :], NT)).astype(BF16)
        for store in stores:
            store.wait()


def first_call(m, flag, count, acts, weight, table, index, pooled):
    rows, width = acts.shape[1:]
    heads_rows = width // HEAD * index.shape[2]
    block = jax.ShapeDtypeStruct((rows, width), BF16)
    turned = jax.ShapeDtypeStruct((heads_rows, rows), BF16)
    return pl.pallas_call(
        functools.partial(first_kernel, m),
        out_shape=(block, block, turned, turned, block),
        in_specs=[SMEM, SMEM, ANY] + [VMEM] * 4,
        out_specs=(VMEM, VMEM, ANY, ANY, ANY),
        scratch_shapes=[
            pltpu.VMEM((rows, width), BF16),
            pltpu.VMEM((heads_rows, rows), BF16),
            pltpu.VMEM((heads_rows, rows), BF16),
            pltpu.VMEM((rows, width), BF16),
            pltpu.SemaphoreType.DMA((4,)),
        ],
        compiler_params=pltpu.CompilerParams(vmem_limit_bytes=28 * MIB),
        cost_estimate=pl.CostEstimate(flops=8 * rows * width * width, bytes_accessed=6 * MIB, transcendentals=0),
        name="first",
    )(flag, count, acts, weight, table, index, pooled)


def table_kernel(replicas, flag_ref, parity_ref, index_ref, pooled_ref, *refs):
    count = (len(refs) - 7) // 3
    sources = refs[: 3 * count]
    send_ref, keep_ref, slant, share, high, kv, sems = refs[3 * count :]
    width = high.shape[2]
    rows = high.shape[1]
    table_rows = 2 * keep_ref.shape[0]
    cands = index_ref.shape[2]

    @pl.when(flag_ref[0] == 1)
    def _():
        loads = []
        for m in range(count):
            for k, target in enumerate((slant, share, high)):
                loads.append(pltpu.make_async_copy(sources[k * count + m], target.at[m], sems.at[3 * m + k]))
        for load in loads:
            load.start()
        steps = replicas.bit_length() - 1
        shift = (table_rows // replicas).bit_length() - 1
        spot = lax.broadcasted_iota(jnp.int32, (table_rows, cands), 0)
        block = spot >> shift
        low_bit = jnp.where(block < replicas // 2, 1 - parity_ref[0], parity_ref[0])
        for k in range(steps - 1):
            low_bit = low_bit + (((block >> (steps - 2 - k)) & 1) << (k + 1))
        row = (low_bit << shift) + (spot & ((1 << shift) - 1))
        left_half = lax.broadcasted_iota(jnp.int32, (HEAD, PAIR), 1) < HEAD
        onehots = []
        for m in range(count):
            onehots.append((row == index_ref[m]).astype(BF16))
            given = jnp.broadcast_to(pooled_ref[m].astype(F32) * (1.0 / rows), (rows, width)).astype(BF16)
            for k in range(3):
                loads[3 * m + k].wait()
            for j in range(width // PAIR):
                here = slice(j * PAIR, (j + 1) * PAIR)
                key = dot(slant[m, here], high[m, :, here], NN) * (1.0 / math.sqrt(HEAD))
                value = dot(share[m, here], given[:, here], NN)
                lines = slice(m * cands, (m + 1) * cands)
                kv[lines, here] = jnp.where(left_half, key[:HEAD], key[HEAD:])
                kv[lines, width + j * PAIR : width + (j + 1) * PAIR] = jnp.where(
                    left_half, value[:HEAD], value[HEAD:]
                )
        onehot = jnp.concatenate(onehots, axis=1)
        for at in range(0, 2 * width, 2 * TILE):
            cols = slice(at, at + 2 * TILE)
            kv_high, kv_low = high_low(kv[:, cols])
            part = dot(onehot, kv_high, NN) + dot(onehot, kv_low, NN)
            send_ref[:, cols] = part[: table_rows // 2].astype(BF16)
            keep_ref[:, cols] = part[table_rows // 2 :]


def table_call(flag, parity, index, pooled, slants, shares, highs, replicas, table_rows):
    rows, width = highs[0].shape
    count = len(highs)
    half = (table_rows // 2, 2 * width)
    return pl.pallas_call(
        functools.partial(table_kernel, replicas),
        out_shape=(jax.ShapeDtypeStruct(half, BF16), jax.ShapeDtypeStruct(half, F32)),
        in_specs=[SMEM, SMEM, VMEM, VMEM] + [ANY] * (3 * count),
        out_specs=(VMEM, VMEM),
        scratch_shapes=[
            pltpu.VMEM((count,) + slants[0].shape, BF16),
            pltpu.VMEM((count,) + shares[0].shape, BF16),
            pltpu.VMEM((count,) + highs[0].shape, BF16),
            pltpu.VMEM((count * index.shape[2], 2 * width), F32),
            pltpu.SemaphoreType.DMA((3 * count,)),
        ],
        compiler_params=pltpu.CompilerParams(vmem_limit_bytes=28 * MIB),
        cost_estimate=pl.CostEstimate(flops=rows * width * width, bytes_accessed=6 * MIB, transcendentals=0),
        name="table",
    )(flag, parity, index, pooled, *slants, *shares, *highs)


def hop_kernel(with_grad, flag_ref, came_hbm, aux_hbm, weight_ref, *rest):
    if with_grad:
        grad_hbm, aux_out, came, aux, grad, sems = rest
    else:
        aux_out, came, aux, sems = rest
    width = came.shape[1]

    @pl.when(flag_ref[0] == 1)
    def _():
        first = pltpu.make_async_copy(came_hbm, came, sems.at[0])
        second = pltpu.make_async_copy(aux_hbm, aux, sems.at[1])
        first.start()
        second.start()
        first.wait()
        second.wait()
        aux[...] = (came[...].astype(F32) * aux[...].astype(F32)).astype(BF16)
        stores = [pltpu.make_async_copy(aux, aux_out, sems.at[2])]
        stores[0].start()
        if with_grad:
            for n in range(width // TILE):
                part = slice(n * TILE, (n + 1) * TILE)
                grad[:, part] = (came[:, part].astype(F32) + dot(aux[...], weight_ref[part, :], NT)).astype(BF16)
                stores.append(
                    pltpu.make_async_copy(grad.at[:, part], grad_hbm.at[:, part], sems.at[3 + n])
                )
                stores[-1].start()
        for store in stores:
            store.wait()


def hop_call(flag, came, aux, weight, with_grad):
    rows, width = came.shape
    block = jax.ShapeDtypeStruct((rows, width), BF16)
    scratch = [pltpu.VMEM((rows, width), BF16)] * (3 if with_grad else 2)
    scratch.append(pltpu.SemaphoreType.DMA((3 + width // TILE,)))
    outs = (block, block) if with_grad else (block,)
    return pl.pallas_call(
        functools.partial(hop_kernel, with_grad),
        out_shape=outs,
        in_specs=[SMEM, ANY, ANY, VMEM if with_grad else ANY],
        out_specs=(ANY,) * len(outs),
        scratch_shapes=scratch,
        input_output_aliases={2: len(outs) - 1},
        compiler_params=pltpu.CompilerParams(vmem_limit_bytes=12 * MIB),
        cost_estimate=pl.CostEstimate(flops=2 * rows * width * width, bytes_accessed=4 * MIB, transcendentals=0),
        name="hop" if with_grad else "end",
    )(flag, came, aux, weight)


def block_order(replicas):
    steps = replicas.bit_length() - 1
    order = []
    for i in range(replicas // 2):
        bits = [(i >> (steps - 2 - k)) & 1 for k in range(steps - 1)]
        order.append(sum(bit << (k + 1) for k, bit in enumerate(bits)))
    return order


def turn_kernel(replicas, parity_ref, acts_hbm, after_hbm, out_ref, acts, turned, sems):
    count, rows, width = acts.shape
    size = width // replicas
    half = width // 2
    mine = parity_ref[0]
    loads = [pltpu.make_async_copy(acts_hbm.at[m], acts.at[m], sems.at[m]) for m in range(count)]
    for load in loads:
        load.start()
    for m in range(count):
        loads[m].wait()
        turned[...] = acts[m].T
        for which in range(2):
            low_bit = 1 - mine if which == 0 else mine
            for i, block in enumerate(block_order(replicas)):
                source = pl.ds(pl.multiple_of((block + low_bit) * size, size), size)
                out_ref[which * half + i * size : which * half + (i + 1) * size, m * rows : (m + 1) * rows] = turned[
                    source
                ]


def turn_call(parity, acts, after, replicas):
    count, rows, width = acts.shape
    return pl.pallas_call(
        functools.partial(turn_kernel, replicas),
        out_shape=jax.ShapeDtypeStruct((width, count * rows), BF16),
        in_specs=[SMEM, ANY, ANY],
        out_specs=VMEM,
        scratch_shapes=[
            pltpu.VMEM(acts.shape, BF16),
            pltpu.VMEM((width, rows), BF16),
            pltpu.SemaphoreType.DMA((count,)),
        ],
        compiler_params=pltpu.CompilerParams(vmem_limit_bytes=16 * MIB),
        cost_estimate=pl.CostEstimate(flops=rows * width, bytes_accessed=4 * MIB, transcendentals=0),
        name="turn",
    )(parity, acts, after)


def weight_kernel(widths, turned, *refs):
    count = len(refs) - 2 - 2 * len(widths)
    delta_hbm = refs[:count]
    outs = refs[count : count + 2 * len(widths)]
    delta, sems = refs[-2:]
    width = delta.shape[1]
    rows = delta.shape[0] // count
    half = width // 2
    copies = [
        pltpu.make_async_copy(delta_hbm[m], delta.at[pl.ds(m * rows, rows)], sems.at[m]) for m in range(count)
    ]
    for copy in copies:
        copy.start()
    for copy in copies:
        copy.wait()
    for which in range(2):
        begin = 0
        for c, span in enumerate(widths):
            out = outs[2 * c + which]
            for at in range(0, span, TILE):
                cols = slice(begin + at, begin + at + TILE)
                product = dot(turned[which * half : (which + 1) * half], delta[:, cols], NN)
                out[:, at : at + TILE] = product.astype(out.dtype)
            begin += span


def weight_call(turned, deltas, widths):
    rows, width = deltas[0].shape
    count = len(deltas)
    outs = []
    for span in widths:
        outs += [jax.ShapeDtypeStruct((width // 2, span), BF16), jax.ShapeDtypeStruct((width // 2, span), F32)]
    return pl.pallas_call(
        functools.partial(weight_kernel, widths),
        out_shape=tuple(outs),
        in_specs=[VMEM] + [ANY] * count,
        out_specs=(VMEM,) * len(outs),
        scratch_shapes=[pltpu.VMEM((count * rows, width), BF16), pltpu.SemaphoreType.DMA((count,))],
        compiler_params=pltpu.CompilerParams(vmem_limit_bytes=28 * MIB),
        cost_estimate=pl.CostEstimate(
            flops=2 * count * rows * width * width, bytes_accessed=8 * MIB, transcendentals=0
        ),
        name="weight",
    )(turned, *deltas)


def own_half(keep, got, bit):
    mine = (lax.axis_index("dp") >> bit) & 1

    def pick(which):
        return lax.dynamic_index_in_dim(keep, which, 0, keepdims=False) + lax.dynamic_index_in_dim(
            got, which, 0, keepdims=False
        ).astype(F32)

    return pick(1 - mine).astype(BF16), pick(mine)


def finish_scatter(send, keep, replicas, axes, pairs_of):
    steps = replicas.bit_length() - 1
    rows, columns = keep.shape
    for bit in range(steps):
        got = lax.ppermute(send, axes, pairs_of(bit))
        if bit + 1 < steps:
            lead = (2, keep.shape[0] // 2, columns)
            send, keep = own_half(keep.reshape(lead), got.reshape(lead), bit + 1)
    return keep + got.astype(F32)


def body(activations, section_weights, cand_table, cand_index, cand_count, pooled_cotangent):
    sections = lax.axis_size("section")
    replicas = lax.axis_size("dp")
    position = lax.axis_index("section")
    replica = lax.axis_index("dp")
    last = sections - 1
    final_flag = position == last
    acts = activations[0]
    weight = section_weights[0]
    micro_count, row_count, model_width = acts.shape
    table_rows = cand_table.shape[0]

    def flag(truth):
        return truth.astype(jnp.int32).reshape(1)

    parity = (replica & 1).reshape(1)
    pooled = pooled_cotangent
    grads, aux, slants, shares, highs = [], [], [], [], []
    for m in range(micro_count):
        out = first_call(m, flag(final_flag), cand_count, acts, weight, cand_table, cand_index, pooled)
        for kept, item in zip((grads, aux, slants, shares, highs), out):
            kept.append(item)

    for hop in range(last):
        source = last - hop
        received = [lax.ppermute(g, "section", [(source, source - 1)]) for g in grads]
        active = flag(position == source - 1)
        if hop + 1 == last:
            turned = turn_call(parity, acts, received[0], replicas)
        for m in range(micro_count):
            if hop + 1 < last:
                grads[m], aux[m] = hop_call(active, received[m], aux[m], weight, True)
            else:
                (aux[m],) = hop_call(active, received[m], aux[m], weight, False)

    def table_pairs(bit):
        return [(last * replicas + i, last * replicas + (i ^ (1 << bit))) for i in range(replicas)]

    def pairs(bit):
        return [(i, i ^ (1 << bit)) for i in range(replicas)]

    table_send, table_keep = table_call(
        flag(final_flag), parity, cand_index, pooled, slants, shares, highs, replicas, table_rows
    )
    own_table = finish_scatter(table_send, table_keep, replicas, ("section", "dp"), table_pairs)
    width = 2 * model_width // sections
    spread = [
        lax.ppermute(own_table[:, s * width : (s + 1) * width].astype(BF16), "section", [(last, s)])
        for s in range(last)
    ]

    widths = tuple(int(part * model_width) for part in CHUNKS)
    pieces = weight_call(turned, aux, widths)
    sums = [
        finish_scatter(pieces[2 * c], pieces[2 * c + 1], replicas, "dp", pairs) for c in range(len(widths))
    ]
    late_flag, sums = lax.optimization_barrier((flag(final_flag), sums))
    table_sum = jnp.where(
        late_flag[0] == 1, own_table[:, last * width :], sum(piece.astype(F32) for piece in spread)
    )
    return jnp.concatenate(sums, axis=1)[None], table_sum


def solution(mesh):
    in_specs = (
        P("section", None, "dp", None),
        P("section", None, None),
        P(),
        P(None, "dp", None),
        P(None, "dp"),
        P(None, "dp", None),
    )
    out_specs = (P("section", "dp", None), P("dp", "section"))
    return jax.shard_map(body, mesh=mesh, in_specs=in_specs, out_specs=out_specs, check_vma=False)
```

```python
import functools
import math

import jax
import jax.numpy as jnp
from jax import lax
from jax.experimental import pallas as pl
from jax.experimental.pallas import tpu as pltpu
from jax.sharding import PartitionSpec as P

HEAD = 64
PAIR = 2 * HEAD
TILE = 256
CHUNKS = (0.25, 0.25, 0.25, 0.25)
MIB = 1024 * 1024
HBM = pl.BlockSpec(memory_space=pltpu.HBM)
VMEM = pl.BlockSpec(memory_space=pltpu.VMEM)
SMEM = pl.BlockSpec(memory_space=pltpu.SMEM)
BF16 = jnp.bfloat16
F32 = jnp.float32

NN = (((1,), (0,)), ((), ()))
NT = (((1,), (1,)), ((), ()))
TN = (((0,), (0,)), ((), ()))


def dot(left, right, dims):
    return lax.dot_general(left, right, dims, preferred_element_type=F32)


def gelu_parts(hidden):
    root = math.sqrt(2.0 / math.pi)
    square = hidden * hidden
    bent = jnp.tanh(root * hidden * (1.0 + 0.044715 * square))
    share = 0.5 + 0.5 * bent
    slope = share + (0.5 * root) * hidden * (1.0 - bent * bent) * (1.0 + (3 * 0.044715) * square)
    return hidden * share, slope


def high_low(values):
    high = values.astype(BF16)
    return high, (values - high.astype(F32)).astype(BF16)


def first_kernel(
    m, flag_ref, count_ref, acts_hbm, weight_hbm, table_hbm, index_ref, pooled_ref,
    grad_hbm, aux_hbm, share_hbm, high_hbm, acts, weight, table, grad, aux, share_ref, high_ref, sems,
):
    rows, width = acts.shape
    table_rows = table.shape[0]
    pairs = width // PAIR
    tiles = width // TILE
    tile = [slice(q * TILE, (q + 1) * TILE) for q in range(tiles)]
    used = []

    def copy(source, target):
        used.append(pltpu.make_async_copy(source, target, sems.at[len(used)]))
        used[-1].start()
        return used[-1]

    load = copy(acts_hbm.at[m], acts)
    load_weight = [copy(weight_hbm.at[:, cols], weight.at[:, cols]) for cols in tile]

    @pl.when(flag_ref[0] == 0)
    def _():
        load.wait()
        stores = []
        for q, cols in enumerate(tile):
            load_weight[q].wait()
            hidden = dot(acts[...], weight[:, cols], NN)
            aux[:, cols] = gelu_parts(hidden)[1].astype(BF16)
            stores.append(copy(aux.at[:, cols], aux_hbm.at[:, cols]))
        for store in stores:
            store.wait()

    @pl.when(flag_ref[0] == 1)
    def _():
        copy(table_hbm, table).wait()
        index = index_ref[m]
        index = jnp.concatenate([index, index], axis=1)
        onehot = (lax.broadcasted_iota(jnp.int32, (table_rows, PAIR), 0) == index).astype(BF16)
        gathered = dot(onehot, table[...], TN)
        own = (
            lax.broadcasted_iota(jnp.int32, (PAIR, width), 0) // HEAD
            == lax.broadcasted_iota(jnp.int32, (PAIR, width), 1) // HEAD % 2
        )
        keys = jnp.where(own, gathered[:, :width] * (1.0 / math.sqrt(HEAD)), 0.0).astype(BF16)
        values = jnp.where(own, gathered[:, width:], 0.0).astype(BF16)
        allowed = lax.broadcasted_iota(jnp.int32, (2, HEAD, rows), 1) < count_ref[m, 0]
        given_row = pooled_ref[m].astype(F32) * (1.0 / rows)
        given = jnp.broadcast_to(given_row, (rows, width)).astype(BF16)
        load.wait()
        stores, totals = [], []
        for q, cols in enumerate(tile):
            load_weight[q].wait()
            hidden = dot(acts[...], weight[:, cols], NN)
            bent, slope = gelu_parts(hidden)
            high, low = high_low(acts[:, cols].astype(F32) + bent)
            high_ref[:, cols] = high
            stores.append(copy(high_ref.at[:, cols], high_hbm.at[:, cols]))
            for j in range(TILE // PAIR):
                here = slice(j * PAIR, (j + 1) * PAIR)
                there = slice(q * TILE + j * PAIR, q * TILE + (j + 1) * PAIR)
                key = keys[:, there]
                score = dot(
                    jnp.concatenate([key, key], axis=1),
                    jnp.concatenate([high[:, here], low[:, here]], axis=1),
                    NT,
                )
                share, slant = soften(score, dot(values[:, there], given[:, there], NT), allowed)
                share_ref[there] = share
                total = given_row[:, there] + dot(slant, key, TN)
                totals.append(total)
                aux[:, there] = (total * slope[:, here]).astype(BF16)
            stores.append(copy(aux.at[:, cols], aux_hbm.at[:, cols]))
        stores.append(copy(share_ref, share_hbm))
        for q, cols in enumerate(tile):
            total = jnp.concatenate(totals[q * TILE // PAIR : (q + 1) * TILE // PAIR], axis=1)
            grad[:, cols] = (total + dot(aux[...], weight[cols, :], NT)).astype(BF16)
            stores.append(copy(grad.at[:, cols], grad_hbm.at[:, cols]))
        for store in stores:
            store.wait()


def lean(share, worth):
    worth = worth.reshape(share.shape)
    centre = jnp.sum(share * worth, axis=1, keepdims=True)
    return (share * (worth - centre)).reshape(worth.shape[0] * worth.shape[1], -1).astype(BF16)


def soften(score, worth, allowed):
    score = jnp.where(allowed, score.reshape(allowed.shape), -1e30)
    raised = jnp.exp(score - jnp.max(score, axis=1, keepdims=True))
    share = raised * (1.0 / jnp.sum(raised, axis=1, keepdims=True))
    return share.reshape(worth.shape).astype(BF16), lean(share, worth)


def first_call(m, flag, count, acts, weight, table, index, pooled):
    rows, width = acts.shape[1:]
    tiles = width // TILE
    block = jax.ShapeDtypeStruct((rows, width), BF16)
    turned = (width // HEAD * index.shape[2], rows)
    return pl.pallas_call(
        functools.partial(first_kernel, m),
        out_shape=(block, block, jax.ShapeDtypeStruct(turned, BF16), block),
        in_specs=[SMEM, SMEM, HBM, HBM, HBM, VMEM, VMEM],
        out_specs=(HBM,) * 4,
        scratch_shapes=[
            pltpu.VMEM((rows, width), BF16),
            pltpu.VMEM((width, width), BF16),
            pltpu.VMEM(table.shape, BF16),
            pltpu.VMEM((rows, width), BF16),
            pltpu.VMEM((rows, width), BF16),
            pltpu.VMEM(turned, BF16),
            pltpu.VMEM((rows, width), BF16),
            pltpu.SemaphoreType.DMA((6 + 5 * tiles,)),
        ],
        compiler_params=pltpu.CompilerParams(vmem_limit_bytes=28 * MIB),
        cost_estimate=pl.CostEstimate(flops=8 * rows * width * width, bytes_accessed=6 * MIB, transcendentals=0),
        name="first",
    )(flag, count, acts, weight, table, index, pooled)


def table_kernel(replicas, flag_ref, parity_ref, index_ref, pooled_ref, table_hbm, *refs):
    count = (len(refs) - 7) // 2
    sources = refs[: 2 * count]
    send_ref, keep_ref, table, share, high, kv, sems = refs[2 * count :]
    width = high.shape[2]
    rows = high.shape[1]
    table_rows = 2 * keep_ref.shape[0]
    cands = index_ref.shape[2]

    @pl.when(flag_ref[0] == 1)
    def _():
        loads = []
        for m in range(count):
            for k, target in enumerate((share, high)):
                loads.append(pltpu.make_async_copy(sources[k * count + m], target.at[m], sems.at[2 * m + k]))
        loads.append(pltpu.make_async_copy(table_hbm, table, sems.at[2 * count]))
        for load in loads:
            load.start()
        steps = replicas.bit_length() - 1
        shift = (table_rows // replicas).bit_length() - 1
        spot = lax.broadcasted_iota(jnp.int32, (table_rows, cands), 0)
        block = spot >> shift
        low_bit = jnp.where(block < replicas // 2, 1 - parity_ref[0], parity_ref[0])
        for k in range(steps - 1):
            low_bit = low_bit + (((block >> (steps - 2 - k)) & 1) << (k + 1))
        row = (low_bit << shift) + (spot & ((1 << shift) - 1))
        left_half = lax.broadcasted_iota(jnp.int32, (HEAD, PAIR), 1) < HEAD
        own = (
            lax.broadcasted_iota(jnp.int32, (PAIR, width), 0) // HEAD
            == lax.broadcasted_iota(jnp.int32, (PAIR, width), 1) // HEAD % 2
        )
        loads[-1].wait()
        onehots = []
        for m in range(count):
            onehots.append((row == index_ref[m]).astype(BF16))
            given = jnp.broadcast_to(pooled_ref[m].astype(F32) * (1.0 / rows), (rows, width)).astype(BF16)
            index = jnp.concatenate([index_ref[m], index_ref[m]], axis=1)
            onehot = (lax.broadcasted_iota(jnp.int32, (table_rows, PAIR), 0) == index).astype(BF16)
            values = jnp.where(own, dot(onehot, table[:, width:], TN), 0.0).astype(BF16)
            for k in range(2):
                loads[2 * m + k].wait()
            for j in range(width // PAIR):
                here = slice(j * PAIR, (j + 1) * PAIR)
                slant = lean(
                    share[m, here].astype(F32).reshape(2, HEAD, rows), dot(values[:, here], given[:, here], NT)
                )
                key = dot(slant, high[m, :, here], NN) * (1.0 / math.sqrt(HEAD))
                value = dot(share[m, here], given[:, here], NN)
                lines = slice(m * cands, (m + 1) * cands)
                kv[lines, here] = jnp.where(left_half, key[:HEAD], key[HEAD:])
                kv[lines, width + j * PAIR : width + (j + 1) * PAIR] = jnp.where(
                    left_half, value[:HEAD], value[HEAD:]
                )
        onehot = jnp.concatenate(onehots, axis=1)
        for at in range(0, 2 * width, 2 * TILE):
            cols = slice(at, at + 2 * TILE)
            kv_high, kv_low = high_low(kv[:, cols])
            part = dot(onehot, kv_high, NN) + dot(onehot, kv_low, NN)
            send_ref[:, cols] = part[: table_rows // 2].astype(BF16)
            keep_ref[:, cols] = part[table_rows // 2 :]


def table_call(flag, parity, index, pooled, table, shares, highs, replicas):
    rows, width = highs[0].shape
    count = len(highs)
    half = (table.shape[0] // 2, 2 * width)
    return pl.pallas_call(
        functools.partial(table_kernel, replicas),
        out_shape=(jax.ShapeDtypeStruct(half, BF16), jax.ShapeDtypeStruct(half, F32)),
        in_specs=[SMEM, SMEM, VMEM, VMEM, HBM] + [HBM] * (2 * count),
        out_specs=(VMEM, VMEM),
        scratch_shapes=[
            pltpu.VMEM(table.shape, BF16),
            pltpu.VMEM((count,) + shares[0].shape, BF16),
            pltpu.VMEM((count,) + highs[0].shape, BF16),
            pltpu.VMEM((count * index.shape[2], 2 * width), F32),
            pltpu.SemaphoreType.DMA((2 * count + 1,)),
        ],
        compiler_params=pltpu.CompilerParams(vmem_limit_bytes=28 * MIB),
        cost_estimate=pl.CostEstimate(flops=rows * width * width, bytes_accessed=6 * MIB, transcendentals=0),
        name="table",
    )(flag, parity, index, pooled, table, *shares, *highs)


def hop_kernel(with_grad, flag_ref, came_hbm, aux_hbm, weight_ref, *rest):
    if with_grad:
        grad_hbm, aux_out, came, aux, grad, sems = rest
    else:
        aux_out, came, aux, sems = rest
    width = came.shape[1]

    @pl.when(flag_ref[0] == 1)
    def _():
        first = pltpu.make_async_copy(came_hbm, came, sems.at[0])
        second = pltpu.make_async_copy(aux_hbm, aux, sems.at[1])
        first.start()
        second.start()
        first.wait()
        second.wait()
        aux[...] = (came[...].astype(F32) * aux[...].astype(F32)).astype(BF16)
        stores = [pltpu.make_async_copy(aux, aux_out, sems.at[2])]
        stores[0].start()
        if with_grad:
            for n in range(width // TILE):
                part = slice(n * TILE, (n + 1) * TILE)
                grad[:, part] = (came[:, part].astype(F32) + dot(aux[...], weight_ref[part, :], NT)).astype(BF16)
                stores.append(
                    pltpu.make_async_copy(grad.at[:, part], grad_hbm.at[:, part], sems.at[3 + n])
                )
                stores[-1].start()
        for store in stores:
            store.wait()


def hop_call(flag, came, aux, weight, with_grad):
    rows, width = came.shape
    block = jax.ShapeDtypeStruct((rows, width), BF16)
    scratch = [pltpu.VMEM((rows, width), BF16)] * (3 if with_grad else 2)
    scratch.append(pltpu.SemaphoreType.DMA((3 + width // TILE,)))
    outs = (block, block) if with_grad else (block,)
    return pl.pallas_call(
        functools.partial(hop_kernel, with_grad),
        out_shape=outs,
        in_specs=[SMEM, HBM, HBM, VMEM if with_grad else HBM],
        out_specs=(HBM,) * len(outs),
        scratch_shapes=scratch,
        input_output_aliases={2: len(outs) - 1},
        compiler_params=pltpu.CompilerParams(vmem_limit_bytes=12 * MIB),
        cost_estimate=pl.CostEstimate(flops=2 * rows * width * width, bytes_accessed=4 * MIB, transcendentals=0),
        name="hop" if with_grad else "end",
    )(flag, came, aux, weight)


def block_order(replicas):
    steps = replicas.bit_length() - 1
    order = []
    for i in range(replicas // 2):
        bits = [(i >> (steps - 2 - k)) & 1 for k in range(steps - 1)]
        order.append(sum(bit << (k + 1) for k, bit in enumerate(bits)))
    return order


def turn_kernel(replicas, parity_ref, acts_hbm, after_hbm, out_ref, acts, turned, sems):
    count, rows, width = acts.shape
    size = width // replicas
    half = width // 2
    mine = parity_ref[0]
    loads = [pltpu.make_async_copy(acts_hbm.at[m], acts.at[m], sems.at[m]) for m in range(count)]
    for load in loads:
        load.start()
    for m in range(count):
        loads[m].wait()
        turned[...] = acts[m].T
        for which in range(2):
            low_bit = 1 - mine if which == 0 else mine
            for i, block in enumerate(block_order(replicas)):
                source = pl.ds(pl.multiple_of((block + low_bit) * size, size), size)
                out_ref[which * half + i * size : which * half + (i + 1) * size, m * rows : (m + 1) * rows] = turned[
                    source
                ]


def turn_call(parity, acts, after, replicas):
    count, rows, width = acts.shape
    return pl.pallas_call(
        functools.partial(turn_kernel, replicas),
        out_shape=jax.ShapeDtypeStruct((width, count * rows), BF16),
        in_specs=[SMEM, HBM, HBM],
        out_specs=VMEM,
        scratch_shapes=[
            pltpu.VMEM(acts.shape, BF16),
            pltpu.VMEM((width, rows), BF16),
            pltpu.SemaphoreType.DMA((count,)),
        ],
        compiler_params=pltpu.CompilerParams(vmem_limit_bytes=16 * MIB),
        cost_estimate=pl.CostEstimate(flops=rows * width, bytes_accessed=4 * MIB, transcendentals=0),
        name="turn",
    )(parity, acts, after)


def weight_kernel(widths, turned, *refs):
    count = len(refs) - 2 - 2 * len(widths)
    delta_hbm = refs[:count]
    outs = refs[count : count + 2 * len(widths)]
    delta, sems = refs[-2:]
    width = delta.shape[1]
    rows = delta.shape[0] // count
    half = width // 2
    copies = [
        pltpu.make_async_copy(delta_hbm[m], delta.at[pl.ds(m * rows, rows)], sems.at[m]) for m in range(count)
    ]
    for copy in copies:
        copy.start()
    for copy in copies:
        copy.wait()
    for which in range(2):
        begin = 0
        for c, span in enumerate(widths):
            out = outs[2 * c + which]
            for at in range(0, span, TILE):
                cols = slice(begin + at, begin + at + TILE)
                product = dot(turned[which * half : (which + 1) * half], delta[:, cols], NN)
                out[:, at : at + TILE] = product.astype(out.dtype)
            begin += span


def weight_call(turned, deltas, widths):
    rows, width = deltas[0].shape
    count = len(deltas)
    outs = []
    for span in widths:
        outs += [jax.ShapeDtypeStruct((width // 2, span), BF16), jax.ShapeDtypeStruct((width // 2, span), F32)]
    return pl.pallas_call(
        functools.partial(weight_kernel, widths),
        out_shape=tuple(outs),
        in_specs=[VMEM] + [HBM] * count,
        out_specs=(VMEM,) * len(outs),
        scratch_shapes=[pltpu.VMEM((count * rows, width), BF16), pltpu.SemaphoreType.DMA((count,))],
        compiler_params=pltpu.CompilerParams(vmem_limit_bytes=28 * MIB),
        cost_estimate=pl.CostEstimate(
            flops=2 * count * rows * width * width, bytes_accessed=8 * MIB, transcendentals=0
        ),
        name="weight",
    )(turned, *deltas)


def own_half(keep, got, bit):
    mine = (lax.axis_index("dp") >> bit) & 1

    def pick(which):
        return lax.dynamic_index_in_dim(keep, which, 0, keepdims=False) + lax.dynamic_index_in_dim(
            got, which, 0, keepdims=False
        ).astype(F32)

    return pick(1 - mine).astype(BF16), pick(mine)


def finish_scatter(sends, keeps, replicas, axes, pairs_of):
    steps = replicas.bit_length() - 1
    sends = list(sends)
    sums = []
    for c in range(len(sends)):
        send, keep = sends[c], keeps[c]
        for bit in range(steps):
            got = lax.ppermute(send, axes, pairs_of(bit))
            if bit + 1 < steps:
                lead = (2, keep.shape[0] // 2, keep.shape[1])
                send, keep = own_half(keep.reshape(lead), got.reshape(lead), bit + 1)
                if bit == 0 and c + 2 < len(sends):
                    send, sends[c + 2] = lax.optimization_barrier((send, sends[c + 2]))
        sums.append(keep + got.astype(F32))
    return sums


def body(activations, section_weights, cand_table, cand_index, cand_count, pooled_cotangent):
    sections = lax.axis_size("section")
    replicas = lax.axis_size("dp")
    position = lax.axis_index("section")
    replica = lax.axis_index("dp")
    last = sections - 1
    final_flag = position == last
    acts = activations[0]
    weight = section_weights[0]
    micro_count, row_count, model_width = acts.shape

    def flag(truth):
        return truth.astype(jnp.int32).reshape(1)

    parity = (replica & 1).reshape(1)
    pooled = pooled_cotangent
    grads, aux, shares, highs = [], [], [], []
    for m in range(micro_count):
        out = first_call(m, flag(final_flag), cand_count, acts, weight, cand_table, cand_index, pooled)
        for kept, item in zip((grads, aux, shares, highs), out):
            kept.append(item)

    for hop in range(last):
        source = last - hop
        received = [lax.ppermute(g, "section", [(source, source - 1)]) for g in grads]
        active = flag(position == source - 1)
        if hop + 1 == last:
            turned = turn_call(parity, acts, received[0], replicas)
        for m in range(micro_count):
            if hop + 1 < last:
                grads[m], aux[m] = hop_call(active, received[m], aux[m], weight, True)
            else:
                (aux[m],) = hop_call(active, received[m], aux[m], weight, False)

    def table_pairs(bit):
        return [(last * replicas + i, last * replicas + (i ^ (1 << bit))) for i in range(replicas)]

    def pairs(bit):
        return [(i, i ^ (1 << bit)) for i in range(replicas)]

    table_send, table_keep = table_call(
        flag(final_flag), parity, cand_index, pooled, cand_table, shares, highs, replicas
    )
    (own_table,) = finish_scatter([table_send], [table_keep], replicas, ("section", "dp"), table_pairs)
    width = 2 * model_width // sections
    spread = [
        lax.ppermute(own_table[:, s * width : (s + 1) * width].astype(BF16), "section", [(last, s)])
        for s in range(last)
    ]

    widths = tuple(int(part * model_width) for part in CHUNKS)
    pieces = weight_call(turned, aux, widths)
    sums = finish_scatter(pieces[::2], pieces[1::2], replicas, "dp", pairs)
    late_flag, sums = lax.optimization_barrier((flag(final_flag), sums))
    table_sum = jnp.where(
        late_flag[0] == 1, own_table[:, last * width :], sum(piece.astype(F32) for piece in spread)
    )
    return jnp.concatenate(sums, axis=1)[None], table_sum


def solution(mesh):
    in_specs = (
        P("section", None, "dp", None),
        P("section", None, None),
        P(),
        P(None, "dp", None),
        P(None, "dp"),
        P(None, "dp", None),
    )
    out_specs = (P("section", "dp", None), P("dp", "section"))
    return jax.shard_map(body, mesh=mesh, in_specs=in_specs, out_specs=out_specs, check_vma=False)
```

```python
import functools
import math

import jax
import jax.numpy as jnp
from jax import lax
from jax.experimental import pallas as pl
from jax.experimental.pallas import tpu as pltpu
from jax.sharding import PartitionSpec as P

HEAD = 64
PAIR = 2 * HEAD
TILE = 256
MIB = 1024 * 1024
HBM = pl.BlockSpec(memory_space=pltpu.HBM)
VMEM = pl.BlockSpec(memory_space=pltpu.VMEM)
SMEM = pl.BlockSpec(memory_space=pltpu.SMEM)
BF16 = jnp.bfloat16
F32 = jnp.float32
LIGHT = pl.CostEstimate(flops=1024, bytes_accessed=1024, transcendentals=0)

NN = (((1,), (0,)), ((), ()))
NT = (((1,), (1,)), ((), ()))
TN = (((0,), (0,)), ((), ()))


def dot(left, right, dims):
    return lax.dot_general(left, right, dims, preferred_element_type=F32)


def gelu_parts(hidden):
    root = math.sqrt(2.0 / math.pi)
    square = hidden * hidden
    bent = jnp.tanh(root * hidden * (1.0 + 0.044715 * square))
    share = 0.5 + 0.5 * bent
    slope = share + (0.5 * root) * hidden * (1.0 - bent * bent) * (1.0 + (3 * 0.044715) * square)
    return hidden * share, slope


def high_low(values):
    high = values.astype(BF16)
    return high, (values - high.astype(F32)).astype(BF16)


def stay(array):
    return pltpu.with_memory_space_constraint(array, pltpu.HBM)


def first_kernel(
    m, flag_ref, count_ref, acts_hbm, weight, table_hbm, index_hbm, pooled_hbm, after_hbm,
    grad_hbm, aux_hbm, share_hbm, high_hbm, acts, table, index_ref, pooled_ref, grad, aux, share_ref, high_ref, sems,
):
    rows, width = acts.shape
    table_rows = table.shape[0]
    pairs = width // PAIR
    tiles = width // TILE
    tile = [slice(q * TILE, (q + 1) * TILE) for q in range(tiles)]
    pair = [slice(j * PAIR, (j + 1) * PAIR) for j in range(pairs)]
    load = pltpu.make_async_copy(acts_hbm.at[m], acts, sems.at[0])
    load.start()
    store_aux = pltpu.make_async_copy(aux, aux_hbm, sems.at[1])

    @pl.when(flag_ref[0] == 0)
    def _():
        load.wait()
        for cols in tile:
            hidden = dot(acts[...], weight[:, cols], NN)
            aux[:, cols] = gelu_parts(hidden)[1].astype(BF16)
        store_aux.start()
        store_aux.wait()

    @pl.when(flag_ref[0] == 1)
    def _():
        load_index = pltpu.make_async_copy(index_hbm, index_ref, sems.at[6])
        load_pooled = pltpu.make_async_copy(pooled_hbm, pooled_ref, sems.at[7])
        load_table = pltpu.make_async_copy(table_hbm, table, sems.at[2])
        load_index.start()
        load_pooled.start()
        load_table.start()
        load.wait()
        slopes, highs, lows = [], [], []
        for cols in tile:
            hidden = dot(acts[...], weight[:, cols], NN)
            bent, slope = gelu_parts(hidden)
            high, low = high_low(acts[:, cols].astype(F32) + bent)
            high_ref[:, cols] = high
            slopes.append(slope)
            lows.append(low)
        store_high = pltpu.make_async_copy(high_ref, high_hbm, sems.at[3])
        store_high.start()
        load_table.wait()
        load_index.wait()
        load_pooled.wait()
        index = index_ref[m]
        index = jnp.concatenate([index, index], axis=1)
        onehot = (lax.broadcasted_iota(jnp.int32, (table_rows, PAIR), 0) == index).astype(BF16)
        gathered = dot(onehot, table[...], TN)
        own = (
            lax.broadcasted_iota(jnp.int32, (PAIR, width), 0) // HEAD
            == lax.broadcasted_iota(jnp.int32, (PAIR, width), 1) // HEAD % 2
        )
        keys = jnp.where(own, gathered[:, :width] * (1.0 / math.sqrt(HEAD)), 0.0).astype(BF16)
        values = jnp.where(own, gathered[:, width:], 0.0).astype(BF16)
        allowed = lax.broadcasted_iota(jnp.int32, (2, HEAD, rows), 1) < count_ref[0, m]
        given_row = pooled_ref[m : m + 1].astype(F32) * (1.0 / rows)
        given = jnp.broadcast_to(given_row, (rows, width)).astype(BF16)
        scores = []
        for j, here in enumerate(pair):
            part = slice(j * PAIR % TILE, j * PAIR % TILE + PAIR)
            scores.append(
                dot(
                    jnp.concatenate([keys[:, here], keys[:, here]], axis=1),
                    jnp.concatenate([high_ref[:, here], lows[j * PAIR // TILE][:, part]], axis=1),
                    NT,
                )
            )
        slants = []
        for j, here in enumerate(pair):
            share, slant = soften(scores[j], dot(values[:, here], given[:, here], NT), allowed)
            share_ref[here] = share
            slants.append(slant)
        store_share = pltpu.make_async_copy(share_ref, share_hbm, sems.at[4])
        store_share.start()
        totals = []
        for j, here in enumerate(pair):
            part = slice(j * PAIR % TILE, j * PAIR % TILE + PAIR)
            total = given_row[:, here] + dot(slants[j], keys[:, here], TN)
            totals.append(total)
            aux[:, here] = (total * slopes[j * PAIR // TILE][:, part]).astype(BF16)
        store_aux.start()
        for q, cols in enumerate(tile):
            total = jnp.concatenate(totals[q * TILE // PAIR : (q + 1) * TILE // PAIR], axis=1)
            grad[:, cols] = (total + dot(aux[...], weight[cols, :], NT)).astype(BF16)
        store_grad = pltpu.make_async_copy(grad, grad_hbm, sems.at[5])
        store_grad.start()
        store_high.wait()
        store_share.wait()
        store_aux.wait()
        store_grad.wait()


def lean(share, worth):
    worth = worth.reshape(share.shape)
    centre = jnp.sum(share * worth, axis=1, keepdims=True)
    return (share * (worth - centre)).reshape(worth.shape[0] * worth.shape[1], -1).astype(BF16)


def soften(score, worth, allowed):
    score = jnp.where(allowed, score.reshape(allowed.shape), -1e30)
    raised = jnp.exp(score - jnp.max(score, axis=1, keepdims=True))
    share = raised * (1.0 / jnp.sum(raised, axis=1, keepdims=True))
    return share.reshape(worth.shape).astype(BF16), lean(share, worth)


def first_call(m, flag, count, acts, weight, table, index, pooled, after):
    rows, width = acts.shape[1:]
    turned = (width // HEAD * index.shape[2], rows)
    block = pltpu.HBM((rows, width), BF16)
    return pl.pallas_call(
        functools.partial(first_kernel, m),
        out_shape=(block, block, pltpu.HBM(turned, BF16), block),
        in_specs=[SMEM, SMEM, HBM, VMEM, HBM, HBM, HBM, HBM],
        out_specs=(HBM,) * 4,
        scratch_shapes=[
            pltpu.VMEM((rows, width), BF16),
            pltpu.VMEM(table.shape, BF16),
            pltpu.VMEM(index.shape, jnp.int32),
            pltpu.VMEM(pooled.shape, BF16),
            pltpu.VMEM((rows, width), BF16),
            pltpu.VMEM((rows, width), BF16),
            pltpu.VMEM(turned, BF16),
            pltpu.VMEM((rows, width), BF16),
            pltpu.SemaphoreType.DMA((8,)),
        ],
        compiler_params=pltpu.CompilerParams(vmem_limit_bytes=28 * MIB),
        cost_estimate=LIGHT,
        name="first",
    )(flag, count, stay(acts), weight, stay(table), stay(index), stay(pooled), stay(after))


def table_kernel(replicas, flag_ref, parity_ref, index_ref, pooled_ref, table_hbm, *refs):
    count = (len(refs) - 7) // 2
    sources = refs[: 2 * count]
    send_ref, keep_ref, table, share, high, kv, sems = refs[2 * count :]
    width = high.shape[2]
    rows = high.shape[1]
    table_rows = 2 * keep_ref.shape[0]
    cands = index_ref.shape[2]

    @pl.when(flag_ref[0] == 1)
    def _():
        loads = []
        for m in range(count):
            for k, target in enumerate((share, high)):
                loads.append(pltpu.make_async_copy(sources[k * count + m], target.at[m], sems.at[2 * m + k]))
        loads.append(pltpu.make_async_copy(table_hbm, table, sems.at[2 * count]))
        for load in loads:
            load.start()
        steps = replicas.bit_length() - 1
        shift = (table_rows // replicas).bit_length() - 1
        spot = lax.broadcasted_iota(jnp.int32, (table_rows, cands), 0)
        block = spot >> shift
        low_bit = jnp.where(block < replicas // 2, 1 - parity_ref[0], parity_ref[0])
        for k in range(steps - 1):
            low_bit = low_bit + (((block >> (steps - 2 - k)) & 1) << (k + 1))
        row = (low_bit << shift) + (spot & ((1 << shift) - 1))
        left_half = lax.broadcasted_iota(jnp.int32, (HEAD, PAIR), 1) < HEAD
        own = (
            lax.broadcasted_iota(jnp.int32, (PAIR, width), 0) // HEAD
            == lax.broadcasted_iota(jnp.int32, (PAIR, width), 1) // HEAD % 2
        )
        loads[-1].wait()
        onehots = []
        for m in range(count):
            onehots.append((row == index_ref[m]).astype(BF16))
            given = jnp.broadcast_to(pooled_ref[m : m + 1].astype(F32) * (1.0 / rows), (rows, width)).astype(BF16)
            index = jnp.concatenate([index_ref[m], index_ref[m]], axis=1)
            onehot = (lax.broadcasted_iota(jnp.int32, (table_rows, PAIR), 0) == index).astype(BF16)
            values = jnp.where(own, dot(onehot, table[:, width:], TN), 0.0).astype(BF16)
            for k in range(2):
                loads[2 * m + k].wait()
            for j in range(width // PAIR):
                here = slice(j * PAIR, (j + 1) * PAIR)
                slant = lean(
                    share[m, here].astype(F32).reshape(2, HEAD, rows), dot(values[:, here], given[:, here], NT)
                )
                key = dot(slant, high[m, :, here], NN) * (1.0 / math.sqrt(HEAD))
                value = dot(share[m, here], given[:, here], NN)
                lines = slice(m * cands, (m + 1) * cands)
                kv[lines, here] = jnp.where(left_half, key[:HEAD], key[HEAD:])
                kv[lines, width + j * PAIR : width + (j + 1) * PAIR] = jnp.where(
                    left_half, value[:HEAD], value[HEAD:]
                )
        onehot = jnp.concatenate(onehots, axis=1)
        for at in range(0, 2 * width, 2 * TILE):
            cols = slice(at, at + 2 * TILE)
            kv_high, kv_low = high_low(kv[:, cols])
            part = dot(onehot, kv_high, NN) + dot(onehot, kv_low, NN)
            send_ref[:, cols] = part[: table_rows // 2].astype(BF16)
            keep_ref[:, cols] = part[table_rows // 2 :]


def table_call(flag, parity, index, pooled, table, shares, highs, replicas):
    rows, width = highs[0].shape
    count = len(highs)
    half = (table.shape[0] // 2, 2 * width)
    return pl.pallas_call(
        functools.partial(table_kernel, replicas),
        out_shape=(jax.ShapeDtypeStruct(half, BF16), jax.ShapeDtypeStruct(half, F32)),
        in_specs=[SMEM, SMEM, VMEM, VMEM, HBM] + [HBM] * (2 * count),
        out_specs=(VMEM, VMEM),
        scratch_shapes=[
            pltpu.VMEM(table.shape, BF16),
            pltpu.VMEM((count,) + shares[0].shape, BF16),
            pltpu.VMEM((count,) + highs[0].shape, BF16),
            pltpu.VMEM((count * index.shape[2], 2 * width), F32),
            pltpu.SemaphoreType.DMA((2 * count + 1,)),
        ],
        compiler_params=pltpu.CompilerParams(vmem_limit_bytes=28 * MIB),
        cost_estimate=LIGHT,
        name="table",
    )(flag, parity, index, pooled, stay(table), *map(stay, shares), *map(stay, highs))


def hop_kernel(with_grad, flag_ref, came_hbm, aux_hbm, weight, after_hbm, *rest):
    if with_grad:
        grad_hbm, aux_out, came, aux, grad, sems = rest
    else:
        aux_out, came, aux, sems = rest
    rows, width = came.shape

    @pl.when(flag_ref[0] == 1)
    def _():
        first = pltpu.make_async_copy(came_hbm, came, sems.at[0])
        second = pltpu.make_async_copy(aux_hbm, aux, sems.at[1])
        first.start()
        second.start()
        first.wait()
        second.wait()
        aux[...] = (came[...].astype(F32) * aux[...].astype(F32)).astype(BF16)
        stores = [pltpu.make_async_copy(aux, aux_out, sems.at[2])]
        stores[0].start()
        if with_grad:
            for n in range(width // TILE):
                part = slice(n * TILE, (n + 1) * TILE)
                grad[:, part] = (came[:, part].astype(F32) + dot(aux[...], weight[part, :], NT)).astype(BF16)
            stores.append(pltpu.make_async_copy(grad, grad_hbm, sems.at[3]))
            stores[-1].start()
        for store in stores:
            store.wait()


def hop_call(flag, came, aux, weight, after, with_grad):
    rows, width = came.shape
    block = pltpu.HBM((rows, width), BF16)
    scratch = [pltpu.VMEM((rows, width), BF16)] * (3 if with_grad else 2)
    scratch.append(pltpu.SemaphoreType.DMA((4,)))
    outs = (block, block) if with_grad else (block,)
    return pl.pallas_call(
        functools.partial(hop_kernel, with_grad),
        out_shape=outs,
        in_specs=[SMEM, HBM, HBM, VMEM if with_grad else HBM, HBM],
        out_specs=(HBM,) * len(outs),
        scratch_shapes=scratch,
        input_output_aliases={2: len(outs) - 1},
        compiler_params=pltpu.CompilerParams(vmem_limit_bytes=12 * MIB),
        cost_estimate=LIGHT,
        name="hop" if with_grad else "end",
    )(flag, came, stay(aux), weight if with_grad else stay(weight), stay(after))


def bit_orders(replicas):
    bits = list(range(replicas.bit_length() - 1))
    return [bits, bits[1::-1] + bits[2:]]


def block_order(bits):
    rest = bits[1:]
    order = []
    for i in range(1 << len(rest)):
        order.append(sum(((i >> (len(rest) - 1 - k)) & 1) << bit for k, bit in enumerate(rest)))
    return order


def turn_kernel(replicas, number_ref, acts_hbm, after_hbm, *refs):
    outs = refs[:2]
    acts, turned, sems = refs[2:]
    count, rows, width = acts.shape
    size = width // replicas
    loads = [pltpu.make_async_copy(acts_hbm.at[m], acts.at[m], sems.at[m]) for m in range(count)]
    for load in loads:
        load.start()
    for m in range(count):
        loads[m].wait()
        turned[...] = acts[m].T
        for out, bits in zip(outs, bit_orders(replicas)):
            order = block_order(bits)
            mine = (number_ref[0] >> bits[0]) & 1
            for i, block in enumerate(order + order):
                bit = 1 - mine if i < len(order) else mine
                source = pl.ds(pl.multiple_of((block + (bit << bits[0])) * size, size), size)
                out[i * size : (i + 1) * size, m * rows : (m + 1) * rows] = turned[source]


def turn_call(number, acts, after, replicas):
    count, rows, width = acts.shape
    return pl.pallas_call(
        functools.partial(turn_kernel, replicas),
        out_shape=(jax.ShapeDtypeStruct((width, count * rows), BF16),) * 2,
        in_specs=[SMEM, HBM, HBM],
        out_specs=(VMEM, VMEM),
        scratch_shapes=[
            pltpu.VMEM(acts.shape, BF16),
            pltpu.VMEM((width, rows), BF16),
            pltpu.SemaphoreType.DMA((count,)),
        ],
        compiler_params=pltpu.CompilerParams(vmem_limit_bytes=24 * MIB),
        cost_estimate=LIGHT,
        name="turn",
    )(number, stay(acts), after)


def weight_kernel(flag_ref, *refs):
    turned, refs = refs[:2], refs[2:]
    count = len(refs) - 7
    delta_hbm, came, outs = refs[:count], refs[count], refs[count + 1 : count + 5]
    delta, sems = refs[count + 5 :]
    width = delta.shape[1]
    rows = delta.shape[0] // count
    half = width // 2
    copies = [
        pltpu.make_async_copy(delta_hbm[m], delta.at[pl.ds(m * rows, rows)], sems.at[m]) for m in range(count)
    ]
    for copy in copies:
        copy.start()
    for copy in copies:
        copy.wait()

    @pl.when(flag_ref[0] == 1)
    def _():
        tail = pl.ds((count - 1) * rows, rows)
        delta[tail] = (came[...].astype(F32) * delta[tail].astype(F32)).astype(BF16)

    for which in range(2):
        for c in range(2):
            out = outs[2 * c + which]
            for at in range(0, half, TILE):
                cols = slice(c * half + at, c * half + at + TILE)
                product = dot(turned[c][which * half : (which + 1) * half], delta[:, cols], NN)
                out[:, at : at + TILE] = product.astype(out.dtype)


def weight_call(flag, turned, deltas, came):
    rows, width = deltas[0].shape
    count = len(deltas)
    half = (width // 2, width // 2)
    return pl.pallas_call(
        weight_kernel,
        out_shape=(pltpu.HBM(half, BF16), jax.ShapeDtypeStruct(half, F32)) * 2,
        in_specs=[SMEM, VMEM, VMEM] + [HBM] * count + [VMEM],
        out_specs=(VMEM,) * 4,
        scratch_shapes=[
            pltpu.VMEM((count * rows, width), BF16),
            pltpu.SemaphoreType.DMA((count,)),
        ],
        compiler_params=pltpu.CompilerParams(vmem_limit_bytes=28 * MIB),
        cost_estimate=LIGHT,
        name="weight",
    )(flag, *turned, *map(stay, deltas), came)


def own_half(keep, got, bit):
    mine = (lax.axis_index("dp") >> bit) & 1

    def pick(which):
        return lax.dynamic_index_in_dim(keep, which, 0, keepdims=False) + lax.dynamic_index_in_dim(
            got, which, 0, keepdims=False
        ).astype(F32)

    return pick(1 - mine).astype(BF16), pick(mine)


def finish_scatter(send, keep, bits, axes, pairs_of):
    for n, bit in enumerate(bits):
        got = lax.ppermute(send, axes, pairs_of(bit))
        if n + 1 < len(bits):
            lead = (2, keep.shape[0] // 2, keep.shape[1])
            send, keep = own_half(keep.reshape(lead), got.reshape(lead), bits[n + 1])
    return keep + got.astype(F32)


def body(activations, section_weights, cand_table, cand_index, cand_count, pooled_cotangent):
    sections = lax.axis_size("section")
    replicas = lax.axis_size("dp")
    position = lax.axis_index("section")
    replica = lax.axis_index("dp")
    last = sections - 1
    final_flag = position == last
    acts = activations[0]
    weight = section_weights[0]
    micro_count, row_count, model_width = acts.shape

    def flag(truth):
        return truth.astype(jnp.int32).reshape(1)

    number = replica.reshape(1)
    count = cand_count.reshape(1, micro_count)
    pooled = pooled_cotangent.reshape(micro_count, model_width)
    final = flag(final_flag)
    grads, aux, shares, highs = [], [], [], []
    for m in range(micro_count):
        after = aux[m - 1] if m else acts
        out = first_call(m, final, count, acts, weight, cand_table, cand_index, pooled, after)
        for kept, item in zip((grads, aux, shares, highs), out):
            kept.append(item)

    def table_pairs(bit):
        return [(last * replicas + i, last * replicas + (i ^ (1 << bit))) for i in range(replicas)]

    def pairs(bit):
        return [(i, i ^ (1 << bit)) for i in range(replicas)]

    orders = bit_orders(replicas)
    table_send, table_keep = table_call(
        final, number & 1, cand_index, pooled, cand_table, shares, highs, replicas
    )
    own_table = finish_scatter(table_send, table_keep, orders[0], ("section", "dp"), table_pairs)
    for hop in range(last):
        source = last - hop
        received = [lax.ppermute(g, "section", [(source, source - 1)]) for g in grads]
        active = flag(position == source - 1)
        if hop + 1 == last:
            turned = turn_call(number, acts, received[0], replicas)
        for m in range(micro_count):
            after = aux[m - 1] if m else acts
            if hop + 1 == last and m + 2 == micro_count:
                after = own_table
            if hop + 1 < last:
                grads[m], aux[m] = hop_call(active, received[m], aux[m], weight, after, True)
            elif m + 1 < micro_count:
                (aux[m],) = hop_call(active, received[m], aux[m], weight, after, False)

    width = 2 * model_width // sections
    spread = [
        lax.ppermute(own_table[:, s * width : (s + 1) * width].astype(BF16), "section", [(last, s)])
        for s in range(last)
    ]

    pieces = weight_call(active, turned, aux, received[-1])
    sums = [finish_scatter(pieces[2 * c], pieces[2 * c + 1], orders[c], "dp", pairs) for c in range(2)]
    late_flag, sums = lax.optimization_barrier((flag(final_flag), sums))
    table_sum = jnp.where(
        late_flag[0] == 1, own_table[:, last * width :], sum(piece.astype(F32) for piece in spread)
    )
    return jnp.concatenate(sums, axis=1)[None], table_sum


def solution(mesh):
    in_specs = (
        P("section", None, "dp", None),
        P("section", None, None),
        P(),
        P(None, "dp", None),
        P(None, "dp"),
        P(None, "dp", None),
    )
    out_specs = (P("section", "dp", None), P("dp", "section"))
    return jax.shard_map(body, mesh=mesh, in_specs=in_specs, out_specs=out_specs, check_vma=False)
```

```python
import functools
import math

import jax
import jax.numpy as jnp
from jax import lax
from jax.experimental import pallas as pl
from jax.experimental.pallas import tpu as pltpu
from jax.sharding import PartitionSpec as P

HEAD = 64
PAIR = 2 * HEAD
TILE = 256
MIB = 1024 * 1024
HBM = pl.BlockSpec(memory_space=pltpu.HBM)
VMEM = pl.BlockSpec(memory_space=pltpu.VMEM)
SMEM = pl.BlockSpec(memory_space=pltpu.SMEM)
BF16 = jnp.bfloat16
F32 = jnp.float32
LIGHT = pl.CostEstimate(flops=1024, bytes_accessed=1024, transcendentals=0)

NN = (((1,), (0,)), ((), ()))
NT = (((1,), (1,)), ((), ()))
TN = (((0,), (0,)), ((), ()))


def dot(left, right, dims):
    return lax.dot_general(left, right, dims, preferred_element_type=F32)


def gelu_parts(hidden):
    root = math.sqrt(2.0 / math.pi)
    square = hidden * hidden
    bent = jnp.tanh(root * hidden * (1.0 + 0.044715 * square))
    share = 0.5 + 0.5 * bent
    slope = share + (0.5 * root) * hidden * (1.0 - bent * bent) * (1.0 + (3 * 0.044715) * square)
    return hidden * share, slope


def high_low(values):
    high = values.astype(BF16)
    return high, (values - high.astype(F32)).astype(BF16)


def stay(array):
    return pltpu.with_memory_space_constraint(array, pltpu.HBM)


def own_heads(width):
    shift = HEAD.bit_length() - 1
    row = lax.broadcasted_iota(jnp.int32, (PAIR, width), 0) >> shift
    return row == ((lax.broadcasted_iota(jnp.int32, (PAIR, width), 1) >> shift) & 1)


def first_kernel(
    m, flag_ref, count_hbm, acts_in, weight_in, table_in, index_hbm, pooled_hbm, delta_in,
    grad_hbm, delta_hbm, share_hbm, high_hbm,
    count_ref, acts_buf, weight_buf, table_buf, index_ref, pooled_ref, grad, aux, share_ref, high_ref, sems,
):
    micros, rows, width = acts_in.shape
    table_rows = table_in.shape[0]
    pairs = width // PAIR
    tiles = width // TILE
    tile = [slice(q * TILE, (q + 1) * TILE) for q in range(tiles)]
    pair = [slice(j * PAIR, (j + 1) * PAIR) for j in range(pairs)]

    def copy(source, target, at):
        started = pltpu.make_async_copy(source, target, sems.at[at])
        started.start()
        return started

    if m == 0:
        acts_ref, weight, table = acts_buf, weight_buf, table_buf

        @pl.when(flag_ref[0] == 0)
        def _():
            load_weight = copy(weight_in, weight, 0)
            loads = [copy(acts_in.at[k], acts_ref.at[k], 1 + k) for k in range(micros)]
            load_weight.wait()
            stores = []
            for k in range(micros):
                loads[k].wait()
                for cols in tile:
                    hidden = dot(acts_ref[k], weight[:, cols], NN)
                    aux[k, :, cols] = gelu_parts(hidden)[1].astype(BF16)
                stores.append(copy(aux.at[k], delta_hbm.at[k], 1 + micros + k))
            for store in stores:
                store.wait()

    else:
        acts_ref, weight, table = acts_in, weight_in, table_in

    @pl.when(flag_ref[0] == 1)
    def _():
        loads = [copy(index_hbm, index_ref, 0), copy(pooled_hbm, pooled_ref, 1), copy(count_hbm, count_ref, 2)]
        if m == 0:
            loads.append(copy(table_in, table, 3))
            load_weight = copy(weight_in, weight, 4)
            load_acts = copy(acts_in.at[0], acts_ref.at[0], 5)
            load_acts.wait()
            load_weight.wait()
        acts = acts_ref.at[m]
        slopes, lows = [], []
        for cols in tile:
            hidden = dot(acts[...], weight[:, cols], NN)
            bent, slope = gelu_parts(hidden)
            high, low = high_low(acts[:, cols].astype(F32) + bent)
            high_ref[:, cols] = high
            slopes.append(slope)
            lows.append(low)
        store_high = copy(high_ref, high_hbm, 6)
        for load in loads:
            load.wait()
        index = index_ref[m]
        index = jnp.concatenate([index, index], axis=1)
        onehot = (lax.broadcasted_iota(jnp.int32, (table_rows, PAIR), 0) == index).astype(BF16)
        gathered = dot(onehot, table[...], TN)
        own = own_heads(width)
        keys = jnp.where(own, gathered[:, :width] * (1.0 / math.sqrt(HEAD)), 0.0).astype(BF16)
        values = jnp.where(own, gathered[:, width:], 0.0).astype(BF16)
        allowed = lax.broadcasted_iota(jnp.int32, (2, HEAD, rows), 1) < count_ref[0, m]
        given_row = pooled_ref[m : m + 1].astype(F32) * (1.0 / rows)
        given = jnp.broadcast_to(given_row, (rows, width)).astype(BF16)
        scores = []
        for j, here in enumerate(pair):
            part = slice(j * PAIR % TILE, j * PAIR % TILE + PAIR)
            scores.append(
                dot(
                    jnp.concatenate([keys[:, here], keys[:, here]], axis=1),
                    jnp.concatenate([high_ref[:, here], lows[j * PAIR // TILE][:, part]], axis=1),
                    NT,
                )
            )
        slants = []
        for j, here in enumerate(pair):
            share, slant = soften(scores[j], dot(values[:, here], given[:, here], NT), allowed)
            share_ref[here] = share
            slants.append(slant)
        store_share = copy(share_ref, share_hbm, 7)
        totals = []
        for j, here in enumerate(pair):
            part = slice(j * PAIR % TILE, j * PAIR % TILE + PAIR)
            total = given_row[:, here] + dot(slants[j], keys[:, here], TN)
            totals.append(total)
            aux[0, :, here] = (total * slopes[j * PAIR // TILE][:, part]).astype(BF16)
        store_aux = copy(aux.at[0], delta_hbm.at[m], 8)
        for q, cols in enumerate(tile):
            total = jnp.concatenate(totals[q * TILE // PAIR : (q + 1) * TILE // PAIR], axis=1)
            grad[:, cols] = (total + dot(aux[0], weight[cols, :], NT)).astype(BF16)
        store_grad = copy(grad, grad_hbm, 9)
        store_high.wait()
        store_share.wait()
        store_aux.wait()
        store_grad.wait()


def lean(share, worth):
    worth = worth.reshape(share.shape)
    centre = jnp.sum(share * worth, axis=1, keepdims=True)
    return (share * (worth - centre)).reshape(worth.shape[0] * worth.shape[1], -1).astype(BF16)


def soften(score, worth, allowed):
    score = jnp.where(allowed, score.reshape(allowed.shape), -1e30)
    raised = jnp.exp(score - jnp.max(score, axis=1, keepdims=True))
    share = raised * (1.0 / jnp.sum(raised, axis=1, keepdims=True))
    return share.reshape(worth.shape).astype(BF16), lean(share, worth)


def first_call(m, flag, count, acts, weight, table, index, pooled, delta):
    micros, rows, width = acts.shape
    turned = (width // HEAD * index.shape[2], rows)
    block = pltpu.HBM((rows, width), BF16)
    big = HBM if m == 0 else VMEM
    small = pltpu.VMEM((8, 128), BF16)
    return pl.pallas_call(
        functools.partial(first_kernel, m),
        out_shape=(block, pltpu.HBM(acts.shape, BF16), pltpu.HBM(turned, BF16), block),
        in_specs=[SMEM, HBM, big, big, big, HBM, HBM, HBM],
        out_specs=(HBM,) * 4,
        scratch_shapes=[
            pltpu.SMEM(count.shape, jnp.int32),
            pltpu.VMEM(acts.shape, BF16) if m == 0 else small,
            pltpu.VMEM(weight.shape, BF16) if m == 0 else small,
            pltpu.VMEM(table.shape, BF16) if m == 0 else small,
            pltpu.VMEM(index.shape, jnp.int32),
            pltpu.VMEM(pooled.shape, BF16),
            pltpu.VMEM((rows, width), BF16),
            pltpu.VMEM((micros if m == 0 else 1, rows, width), BF16),
            pltpu.VMEM(turned, BF16),
            pltpu.VMEM((rows, width), BF16),
            pltpu.SemaphoreType.DMA((max(10, 1 + 2 * micros),)),
        ],
        input_output_aliases={} if m == 0 else {7: 1},
        compiler_params=pltpu.CompilerParams(vmem_limit_bytes=28 * MIB),
        cost_estimate=LIGHT,
        name="first",
    )(
        flag,
        stay(count),
        *(stay(array) if m == 0 else array for array in (acts, weight, table)),
        stay(index),
        stay(pooled),
        stay(delta),
    )


def table_kernel(replicas, flag_ref, parity_ref, index_ref, pooled_ref, table_hbm, *refs):
    count = (len(refs) - 7) // 2
    sources = refs[: 2 * count]
    send_ref, keep_ref, table, share, high, kv, sems = refs[2 * count :]
    width = high.shape[2]
    rows = high.shape[1]
    table_rows = 2 * keep_ref.shape[0]
    cands = index_ref.shape[2]

    @pl.when(flag_ref[0] == 1)
    def _():
        loads = []
        for m in range(count):
            for k, target in enumerate((share, high)):
                loads.append(pltpu.make_async_copy(sources[k * count + m], target.at[m], sems.at[2 * m + k]))
        loads.append(pltpu.make_async_copy(table_hbm, table, sems.at[2 * count]))
        for load in loads:
            load.start()
        steps = replicas.bit_length() - 1
        shift = (table_rows // replicas).bit_length() - 1
        spot = lax.broadcasted_iota(jnp.int32, (table_rows, cands), 0)
        block = spot >> shift
        low_bit = jnp.where(block < replicas // 2, 1 - parity_ref[0], parity_ref[0])
        for k in range(steps - 1):
            low_bit = low_bit + (((block >> (steps - 2 - k)) & 1) << (k + 1))
        row = (low_bit << shift) + (spot & ((1 << shift) - 1))
        left_half = lax.broadcasted_iota(jnp.int32, (HEAD, PAIR), 1) < HEAD
        own = own_heads(width)
        loads[-1].wait()
        onehots = []
        for m in range(count):
            onehots.append((row == index_ref[m]).astype(BF16))
            given = jnp.broadcast_to(pooled_ref[m : m + 1].astype(F32) * (1.0 / rows), (rows, width)).astype(BF16)
            index = jnp.concatenate([index_ref[m], index_ref[m]], axis=1)
            onehot = (lax.broadcasted_iota(jnp.int32, (table_rows, PAIR), 0) == index).astype(BF16)
            values = jnp.where(own, dot(onehot, table[:, width:], TN), 0.0).astype(BF16)
            for k in range(2):
                loads[2 * m + k].wait()
            for j in range(width // PAIR):
                here = slice(j * PAIR, (j + 1) * PAIR)
                slant = lean(
                    share[m, here].astype(F32).reshape(2, HEAD, rows), dot(values[:, here], given[:, here], NT)
                )
                key = dot(slant, high[m, :, here], NN) * (1.0 / math.sqrt(HEAD))
                value = dot(share[m, here], given[:, here], NN)
                lines = slice(m * cands, (m + 1) * cands)
                kv[lines, here] = jnp.where(left_half, key[:HEAD], key[HEAD:])
                kv[lines, width + j * PAIR : width + (j + 1) * PAIR] = jnp.where(
                    left_half, value[:HEAD], value[HEAD:]
                )
        onehot = jnp.concatenate(onehots, axis=1)
        for at in range(0, 2 * width, 2 * TILE):
            cols = slice(at, at + 2 * TILE)
            kv_high, kv_low = high_low(kv[:, cols])
            part = dot(onehot, kv_high, NN) + dot(onehot, kv_low, NN)
            send_ref[:, cols] = part[: table_rows // 2].astype(BF16)
            keep_ref[:, cols] = part[table_rows // 2 :]


def table_call(flag, parity, index, pooled, table, shares, highs, replicas):
    rows, width = highs[0].shape
    count = len(highs)
    half = (table.shape[0] // 2, 2 * width)
    return pl.pallas_call(
        functools.partial(table_kernel, replicas),
        out_shape=(jax.ShapeDtypeStruct(half, BF16), jax.ShapeDtypeStruct(half, F32)),
        in_specs=[SMEM, SMEM, VMEM, VMEM, HBM] + [HBM] * (2 * count),
        out_specs=(VMEM, VMEM),
        scratch_shapes=[
            pltpu.VMEM(table.shape, BF16),
            pltpu.VMEM((count,) + shares[0].shape, BF16),
            pltpu.VMEM((count,) + highs[0].shape, BF16),
            pltpu.VMEM((count * index.shape[2], 2 * width), F32),
            pltpu.SemaphoreType.DMA((2 * count + 1,)),
        ],
        compiler_params=pltpu.CompilerParams(vmem_limit_bytes=28 * MIB),
        cost_estimate=LIGHT,
        name="table",
    )(flag, parity, index, pooled, stay(table), *map(stay, shares), *map(stay, highs))


def hop_kernel(m, with_grad, flag_ref, came_hbm, delta_in, weight, after_hbm, *rest):
    if with_grad:
        grad_hbm, delta_hbm, came, aux, grad, sems = rest
    else:
        delta_hbm, came, aux, sems = rest
    width = came.shape[1]

    @pl.when(flag_ref[0] == 1)
    def _():
        first = pltpu.make_async_copy(came_hbm, came, sems.at[0])
        second = pltpu.make_async_copy(delta_in.at[m], aux, sems.at[1])
        first.start()
        second.start()
        first.wait()
        second.wait()
        aux[...] = (came[...].astype(F32) * aux[...].astype(F32)).astype(BF16)
        stores = [pltpu.make_async_copy(aux, delta_hbm.at[m], sems.at[2])]
        stores[0].start()
        if with_grad:
            for n in range(width // TILE):
                part = slice(n * TILE, (n + 1) * TILE)
                grad[:, part] = (came[:, part].astype(F32) + dot(aux[...], weight[part, :], NT)).astype(BF16)
            stores.append(pltpu.make_async_copy(grad, grad_hbm, sems.at[3]))
            stores[-1].start()
        for store in stores:
            store.wait()


def hop_call(m, flag, came, delta, weight, after, with_grad):
    rows, width = came.shape
    scratch = [pltpu.VMEM((rows, width), BF16)] * (3 if with_grad else 2)
    scratch.append(pltpu.SemaphoreType.DMA((4,)))
    outs = (pltpu.HBM(delta.shape, BF16),)
    if with_grad:
        outs = (pltpu.HBM((rows, width), BF16),) + outs
    return pl.pallas_call(
        functools.partial(hop_kernel, m, with_grad),
        out_shape=outs,
        in_specs=[SMEM, HBM, HBM, VMEM if with_grad else HBM, HBM],
        out_specs=(HBM,) * len(outs),
        scratch_shapes=scratch,
        input_output_aliases={2: len(outs) - 1},
        compiler_params=pltpu.CompilerParams(vmem_limit_bytes=12 * MIB),
        cost_estimate=LIGHT,
        name="hop" if with_grad else "end",
    )(flag, came, stay(delta), weight if with_grad else stay(weight), stay(after))


def bit_orders(replicas):
    bits = list(range(replicas.bit_length() - 1))
    return [bits, bits[1::-1] + bits[2:]]


def block_order(bits):
    rest = bits[1:]
    order = []
    for i in range(1 << len(rest)):
        order.append(sum(((i >> (len(rest) - 1 - k)) & 1) << bit for k, bit in enumerate(rest)))
    return order


def turn_kernel(replicas, number_ref, acts_hbm, after_hbm, *refs):
    outs, token_ref = refs[:2], refs[2]
    acts, turned, sems = refs[3:]
    token_ref[...] = jnp.zeros_like(token_ref)
    count, rows, width = acts.shape
    size = width // replicas
    loads = [pltpu.make_async_copy(acts_hbm.at[m], acts.at[m], sems.at[m]) for m in range(count)]
    for load in loads:
        load.start()
    for m in range(count):
        loads[m].wait()
        turned[...] = acts[m].T
        for out, bits in zip(outs, bit_orders(replicas)):
            order = block_order(bits)
            mine = (number_ref[0] >> bits[0]) & 1
            for i, block in enumerate(order + order):
                bit = 1 - mine if i < len(order) else mine
                source = pl.ds(pl.multiple_of((block + (bit << bits[0])) * size, size), size)
                out[i * size : (i + 1) * size, m * rows : (m + 1) * rows] = turned[source]


def turn_call(number, acts, after, replicas):
    count, rows, width = acts.shape
    return pl.pallas_call(
        functools.partial(turn_kernel, replicas),
        out_shape=(jax.ShapeDtypeStruct((width, count * rows), BF16),) * 2 + (pltpu.HBM((16, 128), BF16),),
        in_specs=[SMEM, HBM, HBM],
        out_specs=(VMEM,) * 3,
        scratch_shapes=[
            pltpu.VMEM(acts.shape, BF16),
            pltpu.VMEM((width, rows), BF16),
            pltpu.SemaphoreType.DMA((count,)),
        ],
        compiler_params=pltpu.CompilerParams(vmem_limit_bytes=24 * MIB),
        cost_estimate=LIGHT,
        name="turn",
    )(number, stay(acts), after)


def early_kernel(turned_first, turned_second, delta_hbm, *refs):
    outs, (delta, sems) = refs[:4], refs[4:]
    micros, rows, width = delta.shape
    half = width // 2
    loads = [pltpu.make_async_copy(delta_hbm.at[m], delta.at[m], sems.at[m]) for m in range(micros)]
    for load in loads:
        load.start()
    for load in loads:
        load.wait()
    flat = delta.reshape(micros * rows, width)
    for c, turned in enumerate((turned_first, turned_second)):
        for which in range(2):
            for at in range(0, half, TILE):
                outs[2 * c + which][:, at : at + TILE] = dot(
                    turned[which * half : (which + 1) * half, : micros * rows],
                    flat[:, c * half + at : c * half + at + TILE],
                    NN,
                )


def early_call(turned, delta):
    micros, rows, width = delta.shape
    half = jax.ShapeDtypeStruct((width // 2, width // 2), F32)
    return pl.pallas_call(
        early_kernel,
        out_shape=(half,) * 4,
        in_specs=[VMEM, VMEM, HBM],
        out_specs=(VMEM,) * 4,
        scratch_shapes=[
            pltpu.VMEM((micros - 1, rows, width), BF16),
            pltpu.SemaphoreType.DMA((micros - 1,)),
        ],
        compiler_params=pltpu.CompilerParams(vmem_limit_bytes=28 * MIB),
        cost_estimate=LIGHT,
        name="early",
    )(*turned, stay(delta))


def weight_kernel(which, flag_ref, turned_first, turned_second, delta_hbm, came, early_first, early_second, *refs):
    outs, (delta, sem) = refs[:2], refs[2:]
    rows, width = delta.shape
    half = width // 2
    last = delta_hbm.shape[0] - 1
    load = pltpu.make_async_copy(delta_hbm.at[last], delta, sem.at[0])
    load.start()
    load.wait()

    @pl.when(flag_ref[0] == 1)
    def _():
        delta[...] = (came[...].astype(F32) * delta[...].astype(F32)).astype(BF16)

    for c, (turned, early) in enumerate(((turned_first, early_first), (turned_second, early_second))):
        for at in range(0, half, TILE):
            product = dot(
                turned[which * half : (which + 1) * half, last * rows :],
                delta[:, c * half + at : c * half + at + TILE],
                NN,
            )
            outs[c][:, at : at + TILE] = (early[:, at : at + TILE] + product).astype(outs[c].dtype)


def weight_call(which, flag, turned, delta, came, early):
    micros, rows, width = delta.shape
    half = (width // 2, width // 2)
    return pl.pallas_call(
        functools.partial(weight_kernel, which),
        out_shape=(jax.ShapeDtypeStruct(half, F32) if which else pltpu.HBM(half, BF16),) * 2,
        in_specs=[SMEM, VMEM, VMEM, HBM, VMEM, VMEM, VMEM],
        out_specs=(VMEM,) * 2,
        scratch_shapes=[pltpu.VMEM((rows, width), BF16), pltpu.SemaphoreType.DMA((1,))],
        compiler_params=pltpu.CompilerParams(vmem_limit_bytes=20 * MIB),
        cost_estimate=LIGHT,
        name="weight",
    )(flag, *turned, stay(delta), came, *early)


def own_half(keep, got, bit):
    mine = (lax.axis_index("dp") >> bit) & 1

    def pick(which):
        return lax.dynamic_index_in_dim(keep, which, 0, keepdims=False) + lax.dynamic_index_in_dim(
            got, which, 0, keepdims=False
        ).astype(F32)

    return pick(1 - mine).astype(BF16), pick(mine)


def finish_scatter(send, keep, bits, axes, pairs_of):
    for n, bit in enumerate(bits):
        got = lax.ppermute(send, axes, pairs_of(bit))
        if n + 1 < len(bits):
            lead = (2, keep.shape[0] // 2, keep.shape[1])
            send, keep = own_half(keep.reshape(lead), got.reshape(lead), bits[n + 1])
    return keep + got.astype(F32)


def body(activations, section_weights, cand_table, cand_index, cand_count, pooled_cotangent):
    sections = lax.axis_size("section")
    replicas = lax.axis_size("dp")
    position = lax.axis_index("section")
    replica = lax.axis_index("dp")
    last = sections - 1
    final_flag = position == last
    acts = activations[0]
    weight = section_weights[0]
    micro_count, row_count, model_width = acts.shape

    def flag(truth):
        return truth.astype(jnp.int32).reshape(1)

    number = replica.reshape(1)
    count = cand_count.reshape(1, micro_count)
    pooled = pooled_cotangent.reshape(micro_count, model_width)
    final = flag(final_flag)
    grads, shares, highs = [], [], []
    delta = acts
    for m in range(micro_count):
        grad, delta, share, high = first_call(
            m, final, count, acts, weight, cand_table, cand_index, pooled, delta
        )
        grads.append(grad)
        shares.append(share)
        highs.append(high)

    def table_pairs(bit):
        return [(last * replicas + i, last * replicas + (i ^ (1 << bit))) for i in range(replicas)]

    def pairs(bit):
        return [(i, i ^ (1 << bit)) for i in range(replicas)]

    orders = bit_orders(replicas)
    table_send, table_keep = table_call(
        final, number & 1, cand_index, pooled, cand_table, shares, highs, replicas
    )
    own_table = finish_scatter(table_send, table_keep, orders[0], ("section", "dp"), table_pairs)
    for hop in range(last):
        source = last - hop
        received = [lax.ppermute(g, "section", [(source, source - 1)]) for g in grads]
        active = flag(position == source - 1)
        for m in range(micro_count):
            if hop + 1 < last:
                after = token if hop == 0 and m == 1 else acts
                grads[m], delta = hop_call(m, active, received[m], delta, weight, after, True)
                if hop == 0 and m == 0:
                    *turned, token = turn_call(number, acts, grads[0], replicas)
            elif m + 1 < micro_count:
                after = own_table if m + 2 == micro_count else acts
                (delta,) = hop_call(m, active, received[m], delta, weight, after, False)

    width = 2 * model_width // sections
    spread = [
        lax.ppermute(own_table[:, s * width : (s + 1) * width].astype(BF16), "section", [(last, s)])
        for s in range(last)
    ]

    early = early_call(turned, delta)
    sends = weight_call(0, active, turned, delta, received[-1], early[::2])
    keeps = weight_call(1, active, turned, delta, received[-1], early[1::2])
    sums = [finish_scatter(sends[c], keeps[c], orders[c], "dp", pairs) for c in range(2)]
    late_flag, sums = lax.optimization_barrier((flag(final_flag), sums))
    table_sum = jnp.where(
        late_flag[0] == 1, own_table[:, last * width :], sum(piece.astype(F32) for piece in spread)
    )
    return jnp.concatenate(sums, axis=1)[None], table_sum


def solution(mesh):
    in_specs = (
        P("section", None, "dp", None),
        P("section", None, None),
        P(),
        P(None, "dp", None),
        P(None, "dp"),
        P(None, "dp", None),
    )
    out_specs = (P("section", "dp", None), P("dp", "section"))
    return jax.shard_map(body, mesh=mesh, in_specs=in_specs, out_specs=out_specs, check_vma=False)
```

```python
import functools
import math

import jax
import jax.numpy as jnp
from jax import lax
from jax.experimental import pallas as pl
from jax.experimental.pallas import tpu as pltpu
from jax.sharding import PartitionSpec as P

HEAD = 64
PAIR = 2 * HEAD
TILE = 256
MIB = 1024 * 1024
HBM = pl.BlockSpec(memory_space=pltpu.HBM)
VMEM = pl.BlockSpec(memory_space=pltpu.VMEM)
SMEM = pl.BlockSpec(memory_space=pltpu.SMEM)
BF16 = jnp.bfloat16
F32 = jnp.float32
LIGHT = pl.CostEstimate(flops=1024, bytes_accessed=1024, transcendentals=0)

NN = (((1,), (0,)), ((), ()))
NT = (((1,), (1,)), ((), ()))
TN = (((0,), (0,)), ((), ()))


def dot(left, right, dims):
    return lax.dot_general(left, right, dims, preferred_element_type=F32)


def gelu_parts(hidden):
    root = math.sqrt(2.0 / math.pi)
    square = hidden * hidden
    bent = jnp.tanh(root * hidden * (1.0 + 0.044715 * square))
    share = 0.5 + 0.5 * bent
    slope = share + (0.5 * root) * hidden * (1.0 - bent * bent) * (1.0 + (3 * 0.044715) * square)
    return hidden * share, slope


def high_low(values):
    high = values.astype(BF16)
    return high, (values - high.astype(F32)).astype(BF16)


def stay(array):
    return pltpu.with_memory_space_constraint(array, pltpu.HBM)


def own_heads(width):
    shift = HEAD.bit_length() - 1
    row = lax.broadcasted_iota(jnp.int32, (PAIR, width), 0) >> shift
    return row == ((lax.broadcasted_iota(jnp.int32, (PAIR, width), 1) >> shift) & 1)


def first_kernel(
    m, flag_ref, count_hbm, acts_in, weight_in, table_in, index_hbm, pooled_hbm, delta_in,
    grad_hbm, delta_hbm, share_hbm, high_hbm,
    count_ref, acts_buf, weight_buf, table_buf, index_ref, pooled_ref, grad, aux, share_ref, high_ref, sems,
):
    micros, rows, width = acts_in.shape
    table_rows = table_in.shape[0]
    pairs = width // PAIR
    tiles = width // TILE
    tile = [slice(q * TILE, (q + 1) * TILE) for q in range(tiles)]
    pair = [slice(j * PAIR, (j + 1) * PAIR) for j in range(pairs)]

    def copy(source, target, at):
        started = pltpu.make_async_copy(source, target, sems.at[at])
        started.start()
        return started

    if m == 0:
        acts_ref, weight, table = acts_buf, weight_buf, table_buf

        @pl.when(flag_ref[0] == 0)
        def _():
            load_weight = copy(weight_in, weight, 0)
            loads = [copy(acts_in.at[k], acts_ref.at[k], 1 + k) for k in range(micros)]
            load_weight.wait()
            stores = []
            for k in range(micros):
                loads[k].wait()
                for cols in tile:
                    hidden = dot(acts_ref[k], weight[:, cols], NN)
                    aux[k, :, cols] = gelu_parts(hidden)[1].astype(BF16)
                stores.append(copy(aux.at[k], delta_hbm.at[k], 1 + micros + k))
            for store in stores:
                store.wait()

    else:
        acts_ref, weight, table = acts_in, weight_in, table_in

    @pl.when(flag_ref[0] == 1)
    def _():
        loads = [copy(index_hbm, index_ref, 0), copy(pooled_hbm, pooled_ref, 1), copy(count_hbm, count_ref, 2)]
        if m == 0:
            loads.append(copy(table_in, table, 3))
            load_weight = copy(weight_in, weight, 4)
            load_acts = copy(acts_in.at[0], acts_ref.at[0], 5)
            load_acts.wait()
            load_weight.wait()
        acts = acts_ref.at[m]
        slopes, lows = [], []
        for cols in tile:
            hidden = dot(acts[...], weight[:, cols], NN)
            bent, slope = gelu_parts(hidden)
            high, low = high_low(acts[:, cols].astype(F32) + bent)
            high_ref[:, cols] = high
            slopes.append(slope)
            lows.append(low)
        store_high = copy(high_ref, high_hbm, 6)
        for load in loads:
            load.wait()
        index = index_ref[m]
        index = jnp.concatenate([index, index], axis=1)
        onehot = (lax.broadcasted_iota(jnp.int32, (table_rows, PAIR), 0) == index).astype(BF16)
        gathered = dot(onehot, table[...], TN)
        own = own_heads(width)
        keys = jnp.where(own, gathered[:, :width] * (1.0 / math.sqrt(HEAD)), 0.0).astype(BF16)
        values = jnp.where(own, gathered[:, width:], 0.0).astype(BF16)
        allowed = lax.broadcasted_iota(jnp.int32, (2, HEAD, rows), 1) < count_ref[0, m]
        given_row = pooled_ref[m : m + 1].astype(F32) * (1.0 / rows)
        given = jnp.broadcast_to(given_row, (rows, width)).astype(BF16)
        scores = []
        for j, here in enumerate(pair):
            part = slice(j * PAIR % TILE, j * PAIR % TILE + PAIR)
            scores.append(
                dot(
                    jnp.concatenate([keys[:, here], keys[:, here]], axis=1),
                    jnp.concatenate([high_ref[:, here], lows[j * PAIR // TILE][:, part]], axis=1),
                    NT,
                )
            )
        slants = []
        for j, here in enumerate(pair):
            share, slant = soften(scores[j], dot(values[:, here], given[:, here], NT), allowed)
            share_ref[here] = share
            slants.append(slant)
        store_share = copy(share_ref, share_hbm, 7)
        totals = []
        for j, here in enumerate(pair):
            part = slice(j * PAIR % TILE, j * PAIR % TILE + PAIR)
            total = given_row[:, here] + dot(slants[j], keys[:, here], TN)
            totals.append(total)
            aux[0, :, here] = (total * slopes[j * PAIR // TILE][:, part]).astype(BF16)
        store_aux = copy(aux.at[0], delta_hbm.at[m], 8)
        for q, cols in enumerate(tile):
            total = jnp.concatenate(totals[q * TILE // PAIR : (q + 1) * TILE // PAIR], axis=1)
            grad[:, cols] = (total + dot(aux[0], weight[cols, :], NT)).astype(BF16)
        store_grad = copy(grad, grad_hbm, 9)
        store_high.wait()
        store_share.wait()
        store_aux.wait()
        store_grad.wait()


def lean(share, worth):
    worth = worth.reshape(share.shape)
    centre = jnp.sum(share * worth, axis=1, keepdims=True)
    return (share * (worth - centre)).reshape(worth.shape[0] * worth.shape[1], -1).astype(BF16)


def soften(score, worth, allowed):
    score = jnp.where(allowed, score.reshape(allowed.shape), -1e30)
    raised = jnp.exp(score - jnp.max(score, axis=1, keepdims=True))
    share = raised * (1.0 / jnp.sum(raised, axis=1, keepdims=True))
    return share.reshape(worth.shape).astype(BF16), lean(share, worth)


def first_call(m, flag, count, acts, weight, table, index, pooled, delta):
    micros, rows, width = acts.shape
    turned = (width // HEAD * index.shape[2], rows)
    block = pltpu.HBM((rows, width), BF16)
    big = HBM if m == 0 else VMEM
    small = pltpu.VMEM((8, 128), BF16)
    return pl.pallas_call(
        functools.partial(first_kernel, m),
        out_shape=(block, pltpu.HBM(acts.shape, BF16), pltpu.HBM(turned, BF16), block),
        in_specs=[SMEM, HBM, big, big, big, HBM, HBM, HBM],
        out_specs=(HBM,) * 4,
        scratch_shapes=[
            pltpu.SMEM(count.shape, jnp.int32),
            pltpu.VMEM(acts.shape, BF16) if m == 0 else small,
            pltpu.VMEM(weight.shape, BF16) if m == 0 else small,
            pltpu.VMEM(table.shape, BF16) if m == 0 else small,
            pltpu.VMEM(index.shape, jnp.int32),
            pltpu.VMEM(pooled.shape, BF16),
            pltpu.VMEM((rows, width), BF16),
            pltpu.VMEM((micros if m == 0 else 1, rows, width), BF16),
            pltpu.VMEM(turned, BF16),
            pltpu.VMEM((rows, width), BF16),
            pltpu.SemaphoreType.DMA((max(10, 1 + 2 * micros),)),
        ],
        input_output_aliases={} if m == 0 else {7: 1},
        compiler_params=pltpu.CompilerParams(vmem_limit_bytes=28 * MIB),
        cost_estimate=LIGHT,
        name="first",
    )(
        flag,
        stay(count),
        *(stay(array) if m == 0 else array for array in (acts, weight, table)),
        stay(index),
        stay(pooled),
        stay(delta),
    )


def table_kernel(replicas, flag_ref, number_ref, index_ref, pooled_ref, table_hbm, after_hbm, *refs):
    table, share, high, kv, sems = refs[-5:]
    count = share.shape[0]
    sources, outs = refs[: 2 * count], refs[2 * count : -5]
    width = high.shape[2]
    rows = high.shape[1]
    table_rows = table.shape[0]
    span = 2 * width // len(outs)
    cands = index_ref.shape[2]

    @pl.when(flag_ref[0] == 1)
    def _():
        loads = []
        for m in range(count):
            for k, target in enumerate((share, high)):
                loads.append(pltpu.make_async_copy(sources[k * count + m], target.at[m], sems.at[2 * m + k]))
        loads.append(pltpu.make_async_copy(table_hbm, table, sems.at[2 * count]))
        for load in loads:
            load.start()
        bits = bit_orders(replicas)[1]
        shift = (table_rows // replicas).bit_length() - 1
        spot = lax.broadcasted_iota(jnp.int32, (table_rows, cands), 0)
        block = spot >> shift
        mine = (number_ref[0] >> bits[0]) & 1
        row = jnp.where(block < replicas // 2, 1 - mine, mine) << bits[0]
        for k, bit in enumerate(bits[1:]):
            row = row + (((block >> (len(bits) - 2 - k)) & 1) << bit)
        row = (row << shift) + (spot & ((1 << shift) - 1))
        left_half = lax.broadcasted_iota(jnp.int32, (HEAD, PAIR), 1) < HEAD
        own = own_heads(width)
        loads[-1].wait()
        onehots = []
        for m in range(count):
            onehots.append((row == index_ref[m]).astype(BF16))
            given = jnp.broadcast_to(pooled_ref[m : m + 1].astype(F32) * (1.0 / rows), (rows, width)).astype(BF16)
            index = jnp.concatenate([index_ref[m], index_ref[m]], axis=1)
            onehot = (lax.broadcasted_iota(jnp.int32, (table_rows, PAIR), 0) == index).astype(BF16)
            values = jnp.where(own, dot(onehot, table[:, width:], TN), 0.0).astype(BF16)
            for k in range(2):
                loads[2 * m + k].wait()
            for j in range(width // PAIR):
                here = slice(j * PAIR, (j + 1) * PAIR)
                slant = lean(
                    share[m, here].astype(F32).reshape(2, HEAD, rows), dot(values[:, here], given[:, here], NT)
                )
                key = dot(slant, high[m, :, here], NN) * (1.0 / math.sqrt(HEAD))
                value = dot(share[m, here], given[:, here], NN)
                lines = slice(m * cands, (m + 1) * cands)
                kv[lines, here] = jnp.where(left_half, key[:HEAD], key[HEAD:])
                kv[lines, width + j * PAIR : width + (j + 1) * PAIR] = jnp.where(
                    left_half, value[:HEAD], value[HEAD:]
                )
        onehot = jnp.concatenate(onehots, axis=1)
        for k, out in enumerate(outs):
            kv_high, kv_low = high_low(kv[:, k * span : (k + 1) * span])
            out[...] = (dot(onehot, kv_high, NN) + dot(onehot, kv_low, NN)).astype(BF16)


def table_call(flag, number, index, pooled, table, after, shares, highs, sections, replicas):
    rows, width = highs[0].shape
    count = len(highs)
    return pl.pallas_call(
        functools.partial(table_kernel, replicas),
        out_shape=(pltpu.HBM((table.shape[0], 2 * width // sections), BF16),) * sections,
        in_specs=[SMEM, SMEM, VMEM, VMEM, HBM, HBM] + [HBM] * (2 * count),
        out_specs=(VMEM,) * sections,
        scratch_shapes=[
            pltpu.VMEM(table.shape, BF16),
            pltpu.VMEM((count,) + shares[0].shape, BF16),
            pltpu.VMEM((count,) + highs[0].shape, BF16),
            pltpu.VMEM((count * index.shape[2], 2 * width), F32),
            pltpu.SemaphoreType.DMA((2 * count + 1,)),
        ],
        compiler_params=pltpu.CompilerParams(vmem_limit_bytes=28 * MIB),
        cost_estimate=LIGHT,
        name="table",
    )(flag, number, index, pooled, stay(table), stay(after), *map(stay, shares), *map(stay, highs))


def hop_kernel(m, with_grad, flag_ref, came, delta_in, weight, after_hbm, *rest):
    if with_grad:
        grad_hbm, delta_hbm, aux, grad, sems = rest
    else:
        delta_hbm, aux, sems = rest
    width = came.shape[1]

    @pl.when(flag_ref[0] == 1)
    def _():
        load = pltpu.make_async_copy(delta_in.at[m], aux, sems.at[0])
        load.start()
        load.wait()
        aux[...] = (came[...].astype(F32) * aux[...].astype(F32)).astype(BF16)
        stores = [pltpu.make_async_copy(aux, delta_hbm.at[m], sems.at[1])]
        stores[0].start()
        if with_grad:
            for n in range(width // TILE):
                part = slice(n * TILE, (n + 1) * TILE)
                grad[:, part] = (came[:, part].astype(F32) + dot(aux[...], weight[part, :], NT)).astype(BF16)
            stores.append(pltpu.make_async_copy(grad, grad_hbm, sems.at[2]))
            stores[-1].start()
        for store in stores:
            store.wait()


def hop_call(m, flag, came, delta, weight, after, with_grad):
    rows, width = came.shape
    scratch = [pltpu.VMEM((rows, width), BF16)] * (2 if with_grad else 1)
    scratch.append(pltpu.SemaphoreType.DMA((3,)))
    outs = (pltpu.HBM(delta.shape, BF16),)
    if with_grad:
        outs = (pltpu.HBM((rows, width), BF16),) + outs
    return pl.pallas_call(
        functools.partial(hop_kernel, m, with_grad),
        out_shape=outs,
        in_specs=[SMEM, VMEM, HBM, VMEM if with_grad else HBM, HBM],
        out_specs=(HBM,) * len(outs),
        scratch_shapes=scratch,
        input_output_aliases={2: len(outs) - 1},
        compiler_params=pltpu.CompilerParams(vmem_limit_bytes=12 * MIB),
        cost_estimate=LIGHT,
        name="hop" if with_grad else "end",
    )(flag, came, stay(delta), weight if with_grad else stay(weight), stay(after))


def bit_orders(replicas):
    bits = list(range(replicas.bit_length() - 1))
    return [bits, bits[1::-1] + bits[2:]]


def block_order(bits):
    rest = bits[1:]
    order = []
    for i in range(1 << len(rest)):
        order.append(sum(((i >> (len(rest) - 1 - k)) & 1) << bit for k, bit in enumerate(rest)))
    return order


def turn_kernel(replicas, number_ref, acts_hbm, after_hbm, *refs):
    outs, token_ref = refs[:2], refs[2]
    acts, turned, sems = refs[3:]
    token_ref[...] = jnp.zeros_like(token_ref)
    count, rows, width = acts.shape
    size = width // replicas
    loads = [pltpu.make_async_copy(acts_hbm.at[m], acts.at[m], sems.at[m]) for m in range(count)]
    for load in loads:
        load.start()
    for m in range(count):
        loads[m].wait()
        turned[...] = acts[m].T
        for out, bits in zip(outs, bit_orders(replicas)):
            order = block_order(bits)
            mine = (number_ref[0] >> bits[0]) & 1
            for i, block in enumerate(order + order):
                bit = 1 - mine if i < len(order) else mine
                source = pl.ds(pl.multiple_of((block + (bit << bits[0])) * size, size), size)
                out[i * size : (i + 1) * size, m * rows : (m + 1) * rows] = turned[source]


def turn_call(number, acts, after, replicas):
    count, rows, width = acts.shape
    return pl.pallas_call(
        functools.partial(turn_kernel, replicas),
        out_shape=(pltpu.HBM((width, count * rows), BF16),) * 2 + (pltpu.HBM((16, 128), BF16),),
        in_specs=[SMEM, HBM, HBM],
        out_specs=(VMEM,) * 3,
        scratch_shapes=[
            pltpu.VMEM(acts.shape, BF16),
            pltpu.VMEM((width, rows), BF16),
            pltpu.SemaphoreType.DMA((count,)),
        ],
        compiler_params=pltpu.CompilerParams(vmem_limit_bytes=24 * MIB),
        cost_estimate=LIGHT,
        name="turn",
    )(number, stay(acts), after)


def early_kernel(turned_first, turned_second, delta_hbm, *refs):
    outs, (delta, sems) = refs[:4], refs[4:]
    micros, rows, width = delta.shape
    half = width // 2
    loads = [pltpu.make_async_copy(delta_hbm.at[m], delta.at[m], sems.at[m]) for m in range(micros)]
    for load in loads:
        load.start()
    for load in loads:
        load.wait()
    flat = delta.reshape(micros * rows, width)
    for c, turned in enumerate((turned_first, turned_second)):
        for which in range(2):
            for at in range(0, half, TILE):
                outs[2 * c + which][:, at : at + TILE] = dot(
                    turned[which * half : (which + 1) * half, : micros * rows],
                    flat[:, c * half + at : c * half + at + TILE],
                    NN,
                )


def early_call(turned, delta):
    micros, rows, width = delta.shape
    half = jax.ShapeDtypeStruct((width // 2, width // 2), F32)
    return pl.pallas_call(
        early_kernel,
        out_shape=(half,) * 4,
        in_specs=[VMEM, VMEM, HBM],
        out_specs=(VMEM,) * 4,
        scratch_shapes=[
            pltpu.VMEM((micros - 1, rows, width), BF16),
            pltpu.SemaphoreType.DMA((micros - 1,)),
        ],
        compiler_params=pltpu.CompilerParams(vmem_limit_bytes=28 * MIB),
        cost_estimate=LIGHT,
        name="early",
    )(*turned, stay(delta))


def weight_kernel(
    replicas, which, flag_ref, turned_first, turned_second, delta_hbm, came, early_first, early_second, table_ref, *refs
):
    outs, (delta, sem) = refs[:2], refs[2:]
    rows, width = delta.shape
    half = width // 2
    size = width // replicas
    lines = table_ref.shape[0] // replicas
    pitch = outs[1].shape[0] // (replicas // 2)
    last = delta_hbm.shape[0] - 1
    load = pltpu.make_async_copy(delta_hbm.at[last], delta, sem.at[0])
    load.start()
    table = table_ref[which * table_ref.shape[0] // 2 : (which + 1) * table_ref.shape[0] // 2].astype(F32)
    for i in range(replicas // 2):
        extra = table[i * lines : (i + 1) * lines]
        if extra.shape != (pitch - size, half):
            extra = jnp.pad(extra, ((0, pitch - size - lines), (0, half - extra.shape[1])))
        outs[1][i * pitch + size : (i + 1) * pitch] = extra.astype(outs[1].dtype)
    load.wait()

    @pl.when(flag_ref[0] == 1)
    def _():
        delta[...] = (came[...].astype(F32) * delta[...].astype(F32)).astype(BF16)

    for c, (turned, early) in enumerate(((turned_first, early_first), (turned_second, early_second))):
        for at in range(0, half, TILE):
            cols = slice(at, at + TILE)
            product = early[:, cols] + dot(
                turned[which * half : (which + 1) * half, last * rows :],
                delta[:, c * half + at : c * half + at + TILE],
                NN,
            )
            product = product.astype(outs[c].dtype)
            if c == 0:
                outs[c][:, cols] = product
            else:
                for i in range(replicas // 2):
                    outs[c][i * pitch : i * pitch + size, cols] = product[i * size : (i + 1) * size]


def weight_call(which, flag, turned, delta, came, early, table, replicas):
    micros, rows, width = delta.shape
    half = width // 2
    extra = max(16, table.shape[0] // replicas) * (replicas // 2)
    array = functools.partial(jax.ShapeDtypeStruct, dtype=F32) if which else functools.partial(pltpu.HBM, dtype=BF16)
    return pl.pallas_call(
        functools.partial(weight_kernel, replicas, which),
        out_shape=(array((half, half)), array((half + extra, half))),
        in_specs=[SMEM, VMEM, VMEM, HBM] + [VMEM] * 4,
        out_specs=(VMEM,) * 2,
        scratch_shapes=[pltpu.VMEM((rows, width), BF16), pltpu.SemaphoreType.DMA((1,))],
        compiler_params=pltpu.CompilerParams(vmem_limit_bytes=20 * MIB),
        cost_estimate=LIGHT,
        name="weight",
    )(flag, *turned, stay(delta), came, *early, table)


def own_half(keep, got, bit):
    mine = (lax.axis_index("dp") >> bit) & 1

    def pick(which):
        return lax.dynamic_index_in_dim(keep, which, 0, keepdims=False) + lax.dynamic_index_in_dim(
            got, which, 0, keepdims=False
        ).astype(F32)

    return pick(1 - mine).astype(BF16), pick(mine)


def finish_scatter(send, keep, bits, axes, pairs_of):
    for n, bit in enumerate(bits):
        got = lax.ppermute(send, axes, pairs_of(bit))
        if n + 1 < len(bits):
            lead = (2, keep.shape[0] // 2, keep.shape[1])
            send, keep = own_half(keep.reshape(lead), got.reshape(lead), bits[n + 1])
    return keep + got.astype(F32)


def body(activations, section_weights, cand_table, cand_index, cand_count, pooled_cotangent):
    sections = lax.axis_size("section")
    replicas = lax.axis_size("dp")
    position = lax.axis_index("section")
    replica = lax.axis_index("dp")
    last = sections - 1
    final_flag = position == last
    acts = activations[0]
    weight = section_weights[0]
    micro_count, row_count, model_width = acts.shape

    def flag(truth):
        return truth.astype(jnp.int32).reshape(1)

    number = replica.reshape(1)
    count = cand_count.reshape(1, micro_count)
    pooled = pooled_cotangent.reshape(micro_count, model_width)
    final = flag(final_flag)
    grads, shares, highs = [], [], []
    delta = acts
    for m in range(micro_count):
        grad, delta, share, high = first_call(
            m, final, count, acts, weight, cand_table, cand_index, pooled, delta
        )
        grads.append(grad)
        shares.append(share)
        highs.append(high)

    def pairs(bit):
        return [(i, i ^ (1 << bit)) for i in range(replicas)]

    for hop in range(last):
        source = last - hop
        received = [lax.ppermute(g, "section", [(source, source - 1)]) for g in grads]
        active = flag(position == source - 1)
        for m in range(micro_count):
            if hop + 1 < last:
                after = token if hop == 1 and m == 0 else acts
                grads[m], delta = hop_call(m, active, received[m], delta, weight, after, True)
            elif m + 1 < micro_count:
                (delta,) = hop_call(m, active, received[m], delta, weight, acts, False)
        if hop == 0:
            parts = table_call(
                final, number, cand_index, pooled, cand_table, grads[-1], shares, highs, sections, replicas
            )
            *turned, token = turn_call(number, acts, grads[-1], replicas)

    spread = [lax.ppermute(parts[s], "section", [(last, s)]) for s in range(last)]
    table_part = jnp.where(final_flag, parts[last], sum(spread))

    orders = bit_orders(replicas)
    early = early_call(turned, delta)
    sends = weight_call(0, active, turned, delta, received[-1], early[::2], table_part, replicas)
    keeps = weight_call(1, active, turned, delta, received[-1], early[1::2], table_part, replicas)
    sums = [finish_scatter(sends[c], keeps[c], orders[c], "dp", pairs) for c in range(2)]
    size = model_width // replicas
    lines = cand_table.shape[0] // replicas
    table_sum = sums[1][size : size + lines, : 2 * model_width // sections]
    return jnp.concatenate([sums[0], sums[1][:size]], axis=1)[None], table_sum


def solution(mesh):
    in_specs = (
        P("section", None, "dp", None),
        P("section", None, None),
        P(),
        P(None, "dp", None),
        P(None, "dp"),
        P(None, "dp", None),
    )
    out_specs = (P("section", "dp", None), P("dp", "section"))
    return jax.shard_map(body, mesh=mesh, in_specs=in_specs, out_specs=out_specs, check_vma=False)
```

```python
import functools
import math

import jax
import jax.numpy as jnp
from jax import lax
from jax.experimental import pallas as pl
from jax.experimental.pallas import tpu as pltpu
from jax.sharding import PartitionSpec as P

HEAD = 64
PAIR = 2 * HEAD
TILE = 256
MIB = 1024 * 1024
HBM = pl.BlockSpec(memory_space=pltpu.HBM)
VMEM = pl.BlockSpec(memory_space=pltpu.VMEM)
SMEM = pl.BlockSpec(memory_space=pltpu.SMEM)
BF16 = jnp.bfloat16
F32 = jnp.float32
LIGHT = pl.CostEstimate(flops=1024, bytes_accessed=1024, transcendentals=0)

NN = (((1,), (0,)), ((), ()))
NT = (((1,), (1,)), ((), ()))
TN = (((0,), (0,)), ((), ()))


def dot(left, right, dims):
    return lax.dot_general(left, right, dims, preferred_element_type=F32)


def gelu_parts(hidden):
    root = math.sqrt(2.0 / math.pi)
    square = hidden * hidden
    bent = jnp.tanh(root * hidden * (1.0 + 0.044715 * square))
    share = 0.5 + 0.5 * bent
    slope = share + (0.5 * root) * hidden * (1.0 - bent * bent) * (1.0 + (3 * 0.044715) * square)
    return hidden * share, slope


def high_low(values):
    high = values.astype(BF16)
    return high, (values - high.astype(F32)).astype(BF16)


def stay(array):
    return pltpu.with_memory_space_constraint(array, pltpu.HBM)


def near(array):
    return pltpu.with_memory_space_constraint(array, pltpu.VMEM)


def own_heads(width):
    shift = HEAD.bit_length() - 1
    row = lax.broadcasted_iota(jnp.int32, (PAIR, width), 0) >> shift
    return row == ((lax.broadcasted_iota(jnp.int32, (PAIR, width), 1) >> shift) & 1)


def first_kernel(
    m, flag_ref, count_hbm, acts_in, weight_in, table_in, index_hbm, pooled_hbm, delta_in,
    grad_hbm, delta_hbm, share_hbm, slant_hbm, high_hbm,
    count_ref, acts_buf, weight_buf, table_buf, index_ref, pooled_ref, grad, aux, share_ref, slant_ref, high_ref, sems,
):
    micros, rows, width = acts_in.shape
    table_rows = table_in.shape[0]
    pairs = width // PAIR
    tiles = width // TILE
    tile = [slice(q * TILE, (q + 1) * TILE) for q in range(tiles)]
    pair = [slice(j * PAIR, (j + 1) * PAIR) for j in range(pairs)]

    def copy(source, target, at):
        started = pltpu.make_async_copy(source, target, sems.at[at])
        started.start()
        return started

    if m == 0:
        acts_ref, weight, table = acts_buf, weight_buf, table_buf

        @pl.when(flag_ref[0] == 0)
        def _():
            load_weight = copy(weight_in, weight, 0)
            loads = [copy(acts_in.at[k], acts_ref.at[k], 1 + k) for k in range(micros)]
            load_weight.wait()
            stores = []
            for k in range(micros):
                loads[k].wait()
                for cols in tile:
                    hidden = dot(acts_ref[k], weight[:, cols], NN)
                    aux[k, :, cols] = gelu_parts(hidden)[1].astype(BF16)
                stores.append(copy(aux.at[k], delta_hbm.at[k], 1 + micros + k))
            for store in stores:
                store.wait()

    else:
        acts_ref, weight, table = acts_in, weight_in, table_in

    @pl.when(flag_ref[0] == 1)
    def _():
        loads = [copy(index_hbm, index_ref, 0), copy(pooled_hbm, pooled_ref, 1), copy(count_hbm, count_ref, 2)]
        if m == 0:
            loads.append(copy(table_in, table, 3))
            load_weight = copy(weight_in, weight, 4)
            load_acts = copy(acts_in.at[0], acts_ref.at[0], 5)
            load_acts.wait()
            load_weight.wait()
        acts = acts_ref.at[m]
        slopes, lows = [], []
        for cols in tile:
            hidden = dot(acts[...], weight[:, cols], NN)
            bent, slope = gelu_parts(hidden)
            high, low = high_low(acts[:, cols].astype(F32) + bent)
            high_ref[:, cols] = high
            slopes.append(slope)
            lows.append(low)
        store_high = copy(high_ref, high_hbm, 6)
        for load in loads:
            load.wait()
        index = index_ref[m]
        index = jnp.concatenate([index, index], axis=1)
        onehot = (lax.broadcasted_iota(jnp.int32, (table_rows, PAIR), 0) == index).astype(BF16)
        gathered = dot(onehot, table[...], TN)
        own = own_heads(width)
        keys = jnp.where(own, gathered[:, :width] * (1.0 / math.sqrt(HEAD)), 0.0).astype(BF16)
        values = jnp.where(own, gathered[:, width:], 0.0).astype(BF16)
        allowed = lax.broadcasted_iota(jnp.int32, (2, HEAD, rows), 1) < count_ref[0, m]
        given_row = pooled_ref[m : m + 1].astype(F32) * (1.0 / rows)
        given = jnp.broadcast_to(given_row, (rows, width)).astype(BF16)
        scores = []
        for j, here in enumerate(pair):
            part = slice(j * PAIR % TILE, j * PAIR % TILE + PAIR)
            scores.append(
                dot(
                    jnp.concatenate([keys[:, here], keys[:, here]], axis=1),
                    jnp.concatenate([high_ref[:, here], lows[j * PAIR // TILE][:, part]], axis=1),
                    NT,
                )
            )
        slants = []
        for j, here in enumerate(pair):
            share, slant = soften(scores[j], dot(values[:, here], given[:, here], NT), allowed)
            share_ref[here] = share
            slant_ref[here] = slant
            slants.append(slant)
        store_share = copy(share_ref, share_hbm, 7)
        store_slant = copy(slant_ref, slant_hbm, 10)
        totals = []
        for j, here in enumerate(pair):
            part = slice(j * PAIR % TILE, j * PAIR % TILE + PAIR)
            total = given_row[:, here] + dot(slants[j], keys[:, here], TN)
            totals.append(total)
            aux[0, :, here] = (total * slopes[j * PAIR // TILE][:, part]).astype(BF16)
        store_aux = copy(aux.at[0], delta_hbm.at[m], 8)
        for q, cols in enumerate(tile):
            total = jnp.concatenate(totals[q * TILE // PAIR : (q + 1) * TILE // PAIR], axis=1)
            grad[:, cols] = (total + dot(aux[0], weight[cols, :], NT)).astype(BF16)
        store_grad = copy(grad, grad_hbm, 9)
        store_high.wait()
        store_share.wait()
        store_slant.wait()
        store_aux.wait()
        store_grad.wait()


def lean(share, worth):
    worth = worth.reshape(share.shape)
    centre = jnp.sum(share * worth, axis=1, keepdims=True)
    return (share * (worth - centre)).reshape(worth.shape[0] * worth.shape[1], -1).astype(BF16)


def soften(score, worth, allowed):
    score = jnp.where(allowed, score.reshape(allowed.shape), -1e30)
    raised = jnp.exp(score - jnp.max(score, axis=1, keepdims=True))
    share = raised * (1.0 / jnp.sum(raised, axis=1, keepdims=True))
    return share.reshape(worth.shape).astype(BF16), lean(share, worth)


def first_call(m, flag, count, acts, weight, table, index, pooled, delta):
    micros, rows, width = acts.shape
    turned = (width // HEAD * index.shape[2], rows)
    block = pltpu.HBM((rows, width), BF16)
    big = HBM if m == 0 else VMEM
    small = pltpu.VMEM((8, 128), BF16)
    return pl.pallas_call(
        functools.partial(first_kernel, m),
        out_shape=(block, pltpu.HBM(acts.shape, BF16), pltpu.HBM(turned, BF16), pltpu.HBM(turned, BF16), block),
        in_specs=[SMEM, HBM, big, big, big, HBM, HBM, HBM],
        out_specs=(HBM,) * 5,
        scratch_shapes=[
            pltpu.SMEM(count.shape, jnp.int32),
            pltpu.VMEM(acts.shape, BF16) if m == 0 else small,
            pltpu.VMEM(weight.shape, BF16) if m == 0 else small,
            pltpu.VMEM(table.shape, BF16) if m == 0 else small,
            pltpu.VMEM(index.shape, jnp.int32),
            pltpu.VMEM(pooled.shape, BF16),
            pltpu.VMEM((rows, width), BF16),
            pltpu.VMEM((micros if m == 0 else 1, rows, width), BF16),
            pltpu.VMEM(turned, BF16),
            pltpu.VMEM(turned, BF16),
            pltpu.VMEM((rows, width), BF16),
            pltpu.SemaphoreType.DMA((max(11, 1 + 2 * micros),)),
        ],
        input_output_aliases={} if m == 0 else {7: 1},
        compiler_params=pltpu.CompilerParams(vmem_limit_bytes=28 * MIB),
        cost_estimate=LIGHT,
        name="first",
    )(
        flag,
        stay(count),
        *(stay(array) if m == 0 else array for array in (acts, weight, table)),
        stay(index),
        stay(pooled),
        stay(delta),
    )


def table_kernel(replicas, flag_ref, number_ref, index_ref, pooled_ref, after_hbm, *refs):
    share, slant, high, kv, sems = refs[-5:]
    count, rows, width = high.shape
    sources, outs = refs[: 3 * count], refs[3 * count : -5]
    span, table_rows = outs[0].shape[1], outs[0].shape[0]
    cands = index_ref.shape[2]

    @pl.when(flag_ref[0] == 1)
    def _():
        loads = []
        for m in range(count):
            for k, target in enumerate((share, slant, high)):
                loads.append(pltpu.make_async_copy(sources[k * count + m], target.at[m], sems.at[3 * m + k]))
        for load in loads:
            load.start()
        bits = bit_orders(replicas)[1]
        shift = (table_rows // replicas).bit_length() - 1
        spot = lax.broadcasted_iota(jnp.int32, (table_rows, cands), 0)
        block = spot >> shift
        mine = (number_ref[0] >> bits[0]) & 1
        row = jnp.where(block < replicas // 2, 1 - mine, mine) << bits[0]
        for k, bit in enumerate(bits[1:]):
            row = row + (((block >> (len(bits) - 2 - k)) & 1) << bit)
        row = (row << shift) + (spot & ((1 << shift) - 1))
        head = lax.broadcasted_iota(jnp.int32, (cands, TILE), 1) >> (HEAD.bit_length() - 1)
        ones = jnp.ones((rows, PAIR), BF16)
        onehot = jnp.concatenate([(row == index_ref[m]).astype(BF16) for m in range(count)], axis=1)

        def by_head(blocks):
            chosen = blocks[0]
            for k in range(1, len(blocks)):
                chosen = jnp.where(head == k, blocks[k], chosen)
            return chosen

        for m in range(count):
            given = pooled_ref[m : m + 1].astype(F32) * (1.0 / rows)
            lines = slice(m * cands, (m + 1) * cands)
            for k in range(3):
                loads[3 * m + k].wait()
            column = dot(share[m], ones, NN)
            column = jnp.concatenate([column, column], axis=1)
            for q in range(width // TILE):
                cols = slice(q * TILE, (q + 1) * TILE)
                key = dot(slant[m, cols], high[m, :, cols], NN) * (1.0 / math.sqrt(HEAD))
                starts = range(0, TILE, cands)
                kv[lines, cols] = by_head([key[at : at + cands] for at in starts])
                value = by_head([column[q * TILE + at : q * TILE + at + cands] for at in starts])
                kv[lines, width + q * TILE : width + (q + 1) * TILE] = value * given[:, cols]
        for k, out in enumerate(outs):
            kv_high, kv_low = high_low(kv[:, k * span : (k + 1) * span])
            out[...] = (dot(onehot, kv_high, NN) + dot(onehot, kv_low, NN)).astype(BF16)


def table_call(flag, number, index, pooled, table_rows, after, shares, slants, highs, sections, replicas):
    rows, width = highs[0].shape
    count = len(highs)
    return pl.pallas_call(
        functools.partial(table_kernel, replicas),
        out_shape=(pltpu.HBM((table_rows, 2 * width // sections), BF16),) * sections,
        in_specs=[SMEM, SMEM, VMEM, VMEM, HBM] + [HBM] * (3 * count),
        out_specs=(VMEM,) * sections,
        scratch_shapes=[
            pltpu.VMEM((count,) + shares[0].shape, BF16),
            pltpu.VMEM((count,) + slants[0].shape, BF16),
            pltpu.VMEM((count,) + highs[0].shape, BF16),
            pltpu.VMEM((count * index.shape[2], 2 * width), F32),
            pltpu.SemaphoreType.DMA((3 * count,)),
        ],
        compiler_params=pltpu.CompilerParams(vmem_limit_bytes=28 * MIB),
        cost_estimate=LIGHT,
        name="table",
    )(flag, number, index, pooled, stay(after), *map(stay, shares), *map(stay, slants), *map(stay, highs))


def hop_kernel(m, with_grad, flag_ref, came, delta_in, weight, after_hbm, *rest):
    if with_grad:
        grad_hbm, delta_hbm, aux, grad, sems = rest
    else:
        delta_hbm, aux, sems = rest
    width = came.shape[1]

    @pl.when(flag_ref[0] == 1)
    def _():
        load = pltpu.make_async_copy(delta_in.at[m], aux, sems.at[0])
        load.start()
        load.wait()
        aux[...] = (came[...].astype(F32) * aux[...].astype(F32)).astype(BF16)
        stores = [pltpu.make_async_copy(aux, delta_hbm.at[m], sems.at[1])]
        stores[0].start()
        if with_grad:
            for n in range(width // TILE):
                part = slice(n * TILE, (n + 1) * TILE)
                grad[:, part] = (came[:, part].astype(F32) + dot(aux[...], weight[part, :], NT)).astype(BF16)
            stores.append(pltpu.make_async_copy(grad, grad_hbm, sems.at[2]))
            stores[-1].start()
        for store in stores:
            store.wait()


def hop_call(m, flag, came, delta, weight, after, with_grad):
    rows, width = came.shape
    scratch = [pltpu.VMEM((rows, width), BF16)] * (2 if with_grad else 1)
    scratch.append(pltpu.SemaphoreType.DMA((3,)))
    outs = (pltpu.HBM(delta.shape, BF16),)
    if with_grad:
        outs = (pltpu.HBM((rows, width), BF16),) + outs
    return pl.pallas_call(
        functools.partial(hop_kernel, m, with_grad),
        out_shape=outs,
        in_specs=[SMEM, VMEM, HBM, VMEM if with_grad else HBM, HBM],
        out_specs=(HBM,) * len(outs),
        scratch_shapes=scratch,
        input_output_aliases={2: len(outs) - 1},
        compiler_params=pltpu.CompilerParams(vmem_limit_bytes=12 * MIB),
        cost_estimate=LIGHT,
        name="hop" if with_grad else "end",
    )(flag, near(came), stay(delta), weight if with_grad else stay(weight), stay(after))


def bit_orders(replicas):
    bits = list(range(replicas.bit_length() - 1))
    return [bits, bits[1::-1] + bits[2:]]


def block_order(bits):
    rest = bits[1:]
    order = []
    for i in range(1 << len(rest)):
        order.append(sum(((i >> (len(rest) - 1 - k)) & 1) << bit for k, bit in enumerate(rest)))
    return order


def turn_kernel(acts_hbm, after_hbm, out, token_ref, acts, sems):
    count, rows, width = acts.shape
    token_ref[...] = jnp.zeros_like(token_ref)
    loads = [pltpu.make_async_copy(acts_hbm.at[m], acts.at[m], sems.at[m]) for m in range(count)]
    for load in loads:
        load.start()
    for m in range(count):
        loads[m].wait()
        out[:, m * rows : (m + 1) * rows] = acts[m].T


def turn_call(acts, after):
    count, rows, width = acts.shape
    return pl.pallas_call(
        turn_kernel,
        out_shape=(jax.ShapeDtypeStruct((width, count * rows), BF16), pltpu.HBM((16, 128), BF16)),
        in_specs=[HBM, HBM],
        out_specs=(VMEM,) * 2,
        scratch_shapes=[pltpu.VMEM(acts.shape, BF16), pltpu.SemaphoreType.DMA((count,))],
        compiler_params=pltpu.CompilerParams(vmem_limit_bytes=20 * MIB),
        cost_estimate=LIGHT,
        name="turn",
    )(stay(acts), stay(after))


def picked_rows(turned, number, bits, which, size, columns):
    mine = (number >> bits[0]) & 1
    base = (mine if which else 1 - mine) << bits[0]
    return jnp.concatenate(
        [turned[pl.ds(pl.multiple_of((base + block) * size, size), size), columns] for block in block_order(bits)],
        axis=0,
    )


def early_kernel(replicas, number_ref, turned, delta_hbm, *refs):
    outs, (delta, sems) = refs[:4], refs[4:]
    micros, rows, width = delta.shape
    half = width // 2
    loads = [pltpu.make_async_copy(delta_hbm.at[m], delta.at[m], sems.at[m]) for m in range(micros)]
    for load in loads:
        load.start()
    for load in loads:
        load.wait()
    flat = delta.reshape(micros * rows, width)
    for c, bits in enumerate(bit_orders(replicas)):
        for which in range(2):
            left = picked_rows(turned, number_ref[0], bits, which, width // replicas, slice(0, micros * rows))
            for at in range(0, half, TILE):
                outs[2 * c + which][:, at : at + TILE] = dot(
                    left, flat[:, c * half + at : c * half + at + TILE], NN
                )


def early_call(number, turned, delta, replicas):
    micros, rows, width = delta.shape
    half = jax.ShapeDtypeStruct((width // 2, width // 2), F32)
    return pl.pallas_call(
        functools.partial(early_kernel, replicas),
        out_shape=(half,) * 4,
        in_specs=[SMEM, VMEM, HBM],
        out_specs=(VMEM,) * 4,
        scratch_shapes=[
            pltpu.VMEM((micros - 1, rows, width), BF16),
            pltpu.SemaphoreType.DMA((micros - 1,)),
        ],
        compiler_params=pltpu.CompilerParams(vmem_limit_bytes=28 * MIB),
        cost_estimate=LIGHT,
        name="early",
    )(number, turned, stay(delta))


def weight_kernel(
    replicas, which, flag_ref, number_ref, turned, delta_hbm, came, early_first, early_second, table_ref, *refs
):
    outs, (delta, sem) = refs[:2], refs[2:]
    rows, width = delta.shape
    half = width // 2
    size = width // replicas
    lines = table_ref.shape[0] // replicas
    pitch = outs[1].shape[0] // (replicas // 2)
    last = delta_hbm.shape[0] - 1
    load = pltpu.make_async_copy(delta_hbm.at[last], delta, sem.at[0])
    load.start()
    table = table_ref[which * table_ref.shape[0] // 2 : (which + 1) * table_ref.shape[0] // 2].astype(F32)
    for i in range(replicas // 2):
        extra = table[i * lines : (i + 1) * lines]
        if extra.shape != (pitch - size, half):
            extra = jnp.pad(extra, ((0, pitch - size - lines), (0, half - extra.shape[1])))
        outs[1][i * pitch + size : (i + 1) * pitch] = extra.astype(outs[1].dtype)
    load.wait()

    @pl.when(flag_ref[0] == 1)
    def _():
        delta[...] = (came[...].astype(F32) * delta[...].astype(F32)).astype(BF16)

    for c, (bits, early) in enumerate(zip(bit_orders(replicas), (early_first, early_second))):
        left = picked_rows(turned, number_ref[0], bits, which, size, slice(last * rows, (last + 1) * rows))
        for at in range(0, half, TILE):
            cols = slice(at, at + TILE)
            product = early[:, cols] + dot(
                left,
                delta[:, c * half + at : c * half + at + TILE],
                NN,
            )
            product = product.astype(outs[c].dtype)
            if c == 0:
                outs[c][:, cols] = product
            else:
                for i in range(replicas // 2):
                    outs[c][i * pitch : i * pitch + size, cols] = product[i * size : (i + 1) * size]


def weight_call(which, flag, number, turned, delta, came, early, table, replicas):
    micros, rows, width = delta.shape
    half = width // 2
    extra = max(16, table.shape[0] // replicas) * (replicas // 2)
    array = functools.partial(jax.ShapeDtypeStruct, dtype=F32) if which else functools.partial(pltpu.HBM, dtype=BF16)
    return pl.pallas_call(
        functools.partial(weight_kernel, replicas, which),
        out_shape=(array((half, half)), array((half + extra, half))),
        in_specs=[SMEM, SMEM, VMEM, HBM] + [VMEM] * 4,
        out_specs=(VMEM,) * 2,
        scratch_shapes=[pltpu.VMEM((rows, width), BF16), pltpu.SemaphoreType.DMA((1,))],
        compiler_params=pltpu.CompilerParams(vmem_limit_bytes=20 * MIB),
        cost_estimate=LIGHT,
        name="weight",
    )(flag, number, turned, stay(delta), near(came), *early, table)


def own_half(keep, got, bit):
    mine = (lax.axis_index("dp") >> bit) & 1

    def pick(which):
        return lax.dynamic_index_in_dim(keep, which, 0, keepdims=False) + lax.dynamic_index_in_dim(
            got, which, 0, keepdims=False
        ).astype(F32)

    return pick(1 - mine).astype(BF16), pick(mine)


def finish_scatter(send, keep, bits, axes, pairs_of):
    for n, bit in enumerate(bits):
        got = lax.ppermute(send, axes, pairs_of(bit))
        if n + 1 < len(bits):
            lead = (2, keep.shape[0] // 2, keep.shape[1])
            send, keep = own_half(keep.reshape(lead), got.reshape(lead), bits[n + 1])
    return keep + got.astype(F32)


def body(activations, section_weights, cand_table, cand_index, cand_count, pooled_cotangent):
    sections = lax.axis_size("section")
    replicas = lax.axis_size("dp")
    position = lax.axis_index("section")
    replica = lax.axis_index("dp")
    last = sections - 1
    final_flag = position == last
    acts = activations[0]
    weight = section_weights[0]
    micro_count, row_count, model_width = acts.shape

    def flag(truth):
        return truth.astype(jnp.int32).reshape(1)

    number = replica.reshape(1)
    count = cand_count.reshape(1, micro_count)
    pooled = pooled_cotangent.reshape(micro_count, model_width)
    final = flag(final_flag)
    grads, shares, slants, highs = [], [], [], []
    delta = acts
    for m in range(micro_count):
        grad, delta, share, slant, high = first_call(
            m, final, count, acts, weight, cand_table, cand_index, pooled, delta
        )
        grads.append(grad)
        shares.append(share)
        slants.append(slant)
        highs.append(high)

    def pairs(bit):
        return [(i, i ^ (1 << bit)) for i in range(replicas)]

    for hop in range(last):
        source = last - hop
        received = [lax.ppermute(g, "section", [(source, source - 1)]) for g in grads]
        active = flag(position == source - 1)
        for m in range(micro_count):
            if hop + 1 < last:
                after = token if hop == 1 and m == 0 else acts
                grads[m], delta = hop_call(m, active, received[m], delta, weight, after, True)
            elif m + 1 < micro_count:
                (delta,) = hop_call(m, active, received[m], delta, weight, acts, False)
        if hop == 0:
            parts = table_call(
                final, number, cand_index, pooled, cand_table.shape[0], grads[-1], shares, slants, highs, sections,
                replicas,
            )
            turned, token = turn_call(acts, grads[-1])

    spread = [lax.ppermute(parts[s], "section", [(last, s)]) for s in range(last)]
    table_part = jnp.where(final_flag, parts[last], sum(spread))

    orders = bit_orders(replicas)
    early = early_call(number, turned, delta, replicas)
    sends = weight_call(0, active, number, turned, delta, received[-1], early[::2], table_part, replicas)
    keeps = weight_call(1, active, number, turned, delta, received[-1], early[1::2], table_part, replicas)
    sums = [finish_scatter(sends[c], keeps[c], orders[c], "dp", pairs) for c in range(2)]
    size = model_width // replicas
    lines = cand_table.shape[0] // replicas
    table_sum = sums[1][size : size + lines, : 2 * model_width // sections]
    return jnp.concatenate([sums[0], sums[1][:size]], axis=1)[None], table_sum


def solution(mesh):
    in_specs = (
        P("section", None, "dp", None),
        P("section", None, None),
        P(),
        P(None, "dp", None),
        P(None, "dp"),
        P(None, "dp", None),
    )
    out_specs = (P("section", "dp", None), P("dp", "section"))
    return jax.shard_map(body, mesh=mesh, in_specs=in_specs, out_specs=out_specs, check_vma=False)
```

```python
import functools
import math

import jax
import jax.numpy as jnp
from jax import lax
from jax.experimental import pallas as pl
from jax.experimental.pallas import tpu as pltpu
from jax.sharding import PartitionSpec as P

HEAD = 64
PAIR = 2 * HEAD
TILE = 256
MIB = 1024 * 1024
HBM = pl.BlockSpec(memory_space=pltpu.HBM)
VMEM = pl.BlockSpec(memory_space=pltpu.VMEM)
SMEM = pl.BlockSpec(memory_space=pltpu.SMEM)
BF16 = jnp.bfloat16
F32 = jnp.float32
LIGHT = pl.CostEstimate(flops=1024, bytes_accessed=1024, transcendentals=0)

NN = (((1,), (0,)), ((), ()))
NT = (((1,), (1,)), ((), ()))
TN = (((0,), (0,)), ((), ()))


def dot(left, right, dims):
    return lax.dot_general(left, right, dims, preferred_element_type=F32)


def gelu_parts(hidden):
    root = math.sqrt(2.0 / math.pi)
    square = hidden * hidden
    bent = jnp.tanh(root * hidden * (1.0 + 0.044715 * square))
    share = 0.5 + 0.5 * bent
    slope = share + (0.5 * root) * hidden * (1.0 - bent * bent) * (1.0 + (3 * 0.044715) * square)
    return hidden * share, slope


def high_low(values):
    high = values.astype(BF16)
    return high, (values - high.astype(F32)).astype(BF16)


def stay(array):
    return pltpu.with_memory_space_constraint(array, pltpu.HBM)


def own_heads(width):
    shift = HEAD.bit_length() - 1
    row = lax.broadcasted_iota(jnp.int32, (PAIR, width), 0) >> shift
    return row == ((lax.broadcasted_iota(jnp.int32, (PAIR, width), 1) >> shift) & 1)


def first_kernel(
    m, flag_ref, count_hbm, acts_in, weight_in, table_in, index_hbm, pooled_hbm, delta_in,
    grad_hbm, delta_hbm, share_hbm, slant_hbm, high_hbm,
    count_ref, acts_buf, weight_buf, table_buf, index_ref, pooled_ref, grad, aux, share_ref, slant_ref, high_ref, sems,
):
    micros, rows, width = acts_in.shape
    table_rows = table_in.shape[0]
    pairs = width // PAIR
    tiles = width // TILE
    tile = [slice(q * TILE, (q + 1) * TILE) for q in range(tiles)]
    pair = [slice(j * PAIR, (j + 1) * PAIR) for j in range(pairs)]

    def copy(source, target, at):
        started = pltpu.make_async_copy(source, target, sems.at[at])
        started.start()
        return started

    if m == 0:
        acts_ref, weight, table = acts_buf, weight_buf, table_buf

        @pl.when(flag_ref[0] == 0)
        def _():
            load_weight = copy(weight_in, weight, 0)
            loads = [copy(acts_in.at[k], acts_ref.at[k], 1 + k) for k in range(micros)]
            load_weight.wait()
            stores = []
            for k in range(micros):
                loads[k].wait()
                for cols in tile:
                    hidden = dot(acts_ref[k], weight[:, cols], NN)
                    aux[k, :, cols] = gelu_parts(hidden)[1].astype(BF16)
                stores.append(copy(aux.at[k], delta_hbm.at[k], 1 + micros + k))
            for store in stores:
                store.wait()

    else:
        acts_ref, weight, table = acts_in, weight_in, table_in

    @pl.when(flag_ref[0] == 1)
    def _():
        loads = [copy(index_hbm, index_ref, 0), copy(pooled_hbm, pooled_ref, 1), copy(count_hbm, count_ref, 2)]
        if m == 0:
            loads.append(copy(table_in, table, 3))
            load_weight = copy(weight_in, weight, 4)
            load_acts = copy(acts_in.at[0], acts_ref.at[0], 5)
            load_acts.wait()
            load_weight.wait()
        acts = acts_ref.at[m]
        slopes, lows = [], []
        for cols in tile:
            hidden = dot(acts[...], weight[:, cols], NN)
            bent, slope = gelu_parts(hidden)
            high, low = high_low(acts[:, cols].astype(F32) + bent)
            high_ref[:, cols] = high
            slopes.append(slope)
            lows.append(low)
        store_high = copy(high_ref, high_hbm, 6)
        for load in loads:
            load.wait()
        index = index_ref[m]
        index = jnp.concatenate([index, index], axis=1)
        onehot = (lax.broadcasted_iota(jnp.int32, (table_rows, PAIR), 0) == index).astype(BF16)
        gathered = dot(onehot, table[...], TN)
        own = own_heads(width)
        keys = jnp.where(own, gathered[:, :width] * (1.0 / math.sqrt(HEAD)), 0.0).astype(BF16)
        values = jnp.where(own, gathered[:, width:], 0.0).astype(BF16)
        allowed = lax.broadcasted_iota(jnp.int32, (2, HEAD, rows), 1) < count_ref[0, m]
        given_row = pooled_ref[m : m + 1].astype(F32) * (1.0 / rows)
        given = jnp.broadcast_to(given_row, (rows, width)).astype(BF16)
        scores = []
        for j, here in enumerate(pair):
            part = slice(j * PAIR % TILE, j * PAIR % TILE + PAIR)
            scores.append(
                dot(
                    jnp.concatenate([keys[:, here], keys[:, here]], axis=1),
                    jnp.concatenate([high_ref[:, here], lows[j * PAIR // TILE][:, part]], axis=1),
                    NT,
                )
            )
        slants = []
        for j, here in enumerate(pair):
            share, slant = soften(scores[j], dot(values[:, here], given[:, here], NT), allowed)
            share_ref[here] = share
            slant_ref[here] = slant
            slants.append(slant)
        store_share = copy(share_ref, share_hbm, 7)
        store_slant = copy(slant_ref, slant_hbm, 10)
        totals = []
        for j, here in enumerate(pair):
            part = slice(j * PAIR % TILE, j * PAIR % TILE + PAIR)
            total = given_row[:, here] + dot(slants[j], keys[:, here], TN)
            totals.append(total)
            aux[0, :, here] = (total * slopes[j * PAIR // TILE][:, part]).astype(BF16)
        store_aux = copy(aux.at[0], delta_hbm.at[m], 8)
        for q, cols in enumerate(tile):
            total = jnp.concatenate(totals[q * TILE // PAIR : (q + 1) * TILE // PAIR], axis=1)
            grad[:, cols] = (total + dot(aux[0], weight[cols, :], NT)).astype(BF16)
        store_grad = copy(grad, grad_hbm, 9)
        store_high.wait()
        store_share.wait()
        store_slant.wait()
        store_aux.wait()
        store_grad.wait()


def lean(share, worth):
    worth = worth.reshape(share.shape)
    centre = jnp.sum(share * worth, axis=1, keepdims=True)
    return (share * (worth - centre)).reshape(worth.shape[0] * worth.shape[1], -1).astype(BF16)


def soften(score, worth, allowed):
    score = jnp.where(allowed, score.reshape(allowed.shape), -1e30)
    raised = jnp.exp(score - jnp.max(score, axis=1, keepdims=True))
    share = raised * (1.0 / jnp.sum(raised, axis=1, keepdims=True))
    return share.reshape(worth.shape).astype(BF16), lean(share, worth)


def first_call(m, flag, count, acts, weight, table, index, pooled, delta):
    micros, rows, width = acts.shape
    turned = (width // HEAD * index.shape[2], rows)
    block = pltpu.HBM((rows, width), BF16)
    big = HBM if m == 0 else VMEM
    small = pltpu.VMEM((8, 128), BF16)
    return pl.pallas_call(
        functools.partial(first_kernel, m),
        out_shape=(block, pltpu.HBM(acts.shape, BF16), pltpu.HBM(turned, BF16), pltpu.HBM(turned, BF16), block),
        in_specs=[SMEM, HBM, big, big, big, HBM, HBM, HBM],
        out_specs=(HBM,) * 5,
        scratch_shapes=[
            pltpu.SMEM(count.shape, jnp.int32),
            pltpu.VMEM(acts.shape, BF16) if m == 0 else small,
            pltpu.VMEM(weight.shape, BF16) if m == 0 else small,
            pltpu.VMEM(table.shape, BF16) if m == 0 else small,
            pltpu.VMEM(index.shape, jnp.int32),
            pltpu.VMEM(pooled.shape, BF16),
            pltpu.VMEM((rows, width), BF16),
            pltpu.VMEM((micros if m == 0 else 1, rows, width), BF16),
            pltpu.VMEM(turned, BF16),
            pltpu.VMEM(turned, BF16),
            pltpu.VMEM((rows, width), BF16),
            pltpu.SemaphoreType.DMA((max(11, 1 + 2 * micros),)),
        ],
        input_output_aliases={} if m == 0 else {7: 1},
        compiler_params=pltpu.CompilerParams(vmem_limit_bytes=18 * MIB),
        cost_estimate=LIGHT,
        name="first",
    )(
        flag,
        stay(count),
        *(stay(array) if m == 0 else array for array in (acts, weight, table)),
        stay(index),
        stay(pooled),
        stay(delta),
    )


def table_kernel(flag_ref, index_ref, pooled_ref, after_hbm, *refs):
    share, slant, high, kv, sems = refs[-5:]
    count, rows, width = high.shape
    sections = (len(refs) - 5 - 3 * count) // 2
    sources, outs, parts = refs[: 3 * count], refs[3 * count : -5 - sections], refs[-5 - sections : -5]
    table_rows, span = parts[0].shape
    cands = index_ref.shape[2]

    @pl.when(flag_ref[0] == 1)
    def _():
        loads = []
        for m in range(count):
            for k, target in enumerate((share, slant, high)):
                loads.append(pltpu.make_async_copy(sources[k * count + m], target.at[m], sems.at[3 * m + k]))
        for load in loads:
            load.start()
        row = lax.broadcasted_iota(jnp.int32, (table_rows, cands), 0)
        head = lax.broadcasted_iota(jnp.int32, (cands, TILE), 1) >> (HEAD.bit_length() - 1)
        ones = jnp.ones((rows, PAIR), BF16)
        onehot = jnp.concatenate([(row == index_ref[m]).astype(BF16) for m in range(count)], axis=1)

        def by_head(blocks):
            chosen = blocks[0]
            for k in range(1, len(blocks)):
                chosen = jnp.where(head == k, blocks[k], chosen)
            return chosen

        for m in range(count):
            given = pooled_ref[m : m + 1].astype(F32) * (1.0 / rows)
            lines = slice(m * cands, (m + 1) * cands)
            for k in range(3):
                loads[3 * m + k].wait()
            column = dot(share[m], ones, NN)
            column = jnp.concatenate([column, column], axis=1)
            for q in range(width // TILE):
                cols = slice(q * TILE, (q + 1) * TILE)
                key = dot(slant[m, cols], high[m, :, cols], NN) * (1.0 / math.sqrt(HEAD))
                starts = range(0, TILE, cands)
                kv[lines, cols] = by_head([key[at : at + cands] for at in starts])
                value = by_head([column[q * TILE + at : q * TILE + at + cands] for at in starts])
                kv[lines, width + q * TILE : width + (q + 1) * TILE] = value * given[:, cols]
        stores = []
        for k, part in enumerate(parts):
            kv_high, kv_low = high_low(kv[:, k * span : (k + 1) * span])
            part[...] = (dot(onehot, kv_high, NN) + dot(onehot, kv_low, NN)).astype(BF16)
            stores.append(pltpu.make_async_copy(part, outs[k], sems.at[3 * count + k]))
            stores[k].start()
        for store in stores:
            store.wait()


def table_call(flag, index, pooled, table_rows, after, shares, slants, highs, sections):
    rows, width = highs[0].shape
    count = len(highs)
    part = (table_rows, 2 * width // sections)
    return pl.pallas_call(
        table_kernel,
        out_shape=(pltpu.HBM(part, BF16),) * sections,
        in_specs=[SMEM, VMEM, VMEM, HBM] + [HBM] * (3 * count),
        out_specs=(HBM,) * sections,
        scratch_shapes=[pltpu.VMEM(part, BF16)] * sections
        + [
            pltpu.VMEM((count,) + shares[0].shape, BF16),
            pltpu.VMEM((count,) + slants[0].shape, BF16),
            pltpu.VMEM((count,) + highs[0].shape, BF16),
            pltpu.VMEM((count * index.shape[2], 2 * width), F32),
            pltpu.SemaphoreType.DMA((3 * count + sections,)),
        ],
        compiler_params=pltpu.CompilerParams(vmem_limit_bytes=18 * MIB),
        cost_estimate=LIGHT,
        name="table",
    )(flag, index, pooled, stay(after), *map(stay, shares), *map(stay, slants), *map(stay, highs))


def hop_kernel(m, with_grad, flag_ref, came_hbm, delta_in, weight, after_hbm, *rest):
    if with_grad:
        grad_hbm, delta_hbm, came, aux, grad, sems = rest
    else:
        delta_hbm, came, aux, sems = rest
    width = came.shape[1]

    @pl.when(flag_ref[0] == 1)
    def _():
        first = pltpu.make_async_copy(came_hbm, came, sems.at[0])
        second = pltpu.make_async_copy(delta_in.at[m], aux, sems.at[1])
        first.start()
        second.start()
        first.wait()
        second.wait()
        aux[...] = (came[...].astype(F32) * aux[...].astype(F32)).astype(BF16)
        stores = [pltpu.make_async_copy(aux, delta_hbm.at[m], sems.at[2])]
        stores[0].start()
        if with_grad:
            for n in range(width // TILE):
                part = slice(n * TILE, (n + 1) * TILE)
                grad[:, part] = (came[:, part].astype(F32) + dot(aux[...], weight[part, :], NT)).astype(BF16)
            stores.append(pltpu.make_async_copy(grad, grad_hbm, sems.at[3]))
            stores[-1].start()
        for store in stores:
            store.wait()


def hop_call(m, flag, came, delta, weight, after, with_grad):
    rows, width = came.shape
    scratch = [pltpu.VMEM((rows, width), BF16)] * (3 if with_grad else 2)
    scratch.append(pltpu.SemaphoreType.DMA((4,)))
    outs = (pltpu.HBM(delta.shape, BF16),)
    if with_grad:
        outs = (pltpu.HBM((rows, width), BF16),) + outs
    return pl.pallas_call(
        functools.partial(hop_kernel, m, with_grad),
        out_shape=outs,
        in_specs=[SMEM, HBM, HBM, VMEM if with_grad else HBM, HBM],
        out_specs=(HBM,) * len(outs),
        scratch_shapes=scratch,
        input_output_aliases={2: len(outs) - 1},
        compiler_params=pltpu.CompilerParams(vmem_limit_bytes=12 * MIB),
        cost_estimate=LIGHT,
        name="hop" if with_grad else "end",
    )(flag, came, stay(delta), weight if with_grad else stay(weight), stay(after))


def bit_orders(replicas):
    bits = list(range(replicas.bit_length() - 1))
    return [bits, bits[1::-1] + bits[2:]]


def block_order(bits):
    rest = bits[1:]
    order = []
    for i in range(1 << len(rest)):
        order.append(sum(((i >> (len(rest) - 1 - k)) & 1) << bit for k, bit in enumerate(rest)))
    return order


def turn_kernel(acts_hbm, after_hbm, out, token_ref, acts, sems):
    count, rows, width = acts.shape
    token_ref[...] = jnp.zeros_like(token_ref)
    loads = [pltpu.make_async_copy(acts_hbm.at[m], acts.at[m], sems.at[m]) for m in range(count)]
    for load in loads:
        load.start()
    for m in range(count):
        loads[m].wait()
        out[:, m * rows : (m + 1) * rows] = acts[m].T


def turn_call(acts, after):
    count, rows, width = acts.shape
    return pl.pallas_call(
        turn_kernel,
        out_shape=(jax.ShapeDtypeStruct((width, count * rows), BF16), pltpu.HBM((16, 128), BF16)),
        in_specs=[HBM, HBM],
        out_specs=(VMEM,) * 2,
        scratch_shapes=[pltpu.VMEM(acts.shape, BF16), pltpu.SemaphoreType.DMA((count,))],
        compiler_params=pltpu.CompilerParams(vmem_limit_bytes=14 * MIB),
        cost_estimate=LIGHT,
        name="turn",
    )(stay(acts), stay(after))


def picked_rows(turned, number, bits, which, size, columns):
    mine = (number >> bits[0]) & 1
    base = (mine if which else 1 - mine) << bits[0]
    return jnp.concatenate(
        [turned[pl.ds(pl.multiple_of((base + block) * size, size), size), columns] for block in block_order(bits)],
        axis=0,
    )


def early_kernel(replicas, number_ref, turned, delta_hbm, *refs):
    outs, (delta, sems) = refs[:4], refs[4:]
    micros, rows, width = delta.shape
    half = width // 2
    loads = [pltpu.make_async_copy(delta_hbm.at[m], delta.at[m], sems.at[m]) for m in range(micros)]
    for load in loads:
        load.start()
    for load in loads:
        load.wait()
    flat = delta.reshape(micros * rows, width)
    for c, bits in enumerate(bit_orders(replicas)):
        for which in range(2):
            left = picked_rows(turned, number_ref[0], bits, which, width // replicas, slice(0, micros * rows))
            for at in range(0, half, TILE):
                outs[2 * c + which][:, at : at + TILE] = dot(
                    left, flat[:, c * half + at : c * half + at + TILE], NN
                )


def early_call(number, turned, delta, replicas):
    micros, rows, width = delta.shape
    half = jax.ShapeDtypeStruct((width // 2, width // 2), F32)
    return pl.pallas_call(
        functools.partial(early_kernel, replicas),
        out_shape=(half,) * 4,
        in_specs=[SMEM, VMEM, HBM],
        out_specs=(VMEM,) * 4,
        scratch_shapes=[
            pltpu.VMEM((micros - 1, rows, width), BF16),
            pltpu.SemaphoreType.DMA((micros - 1,)),
        ],
        compiler_params=pltpu.CompilerParams(vmem_limit_bytes=18 * MIB),
        cost_estimate=LIGHT,
        name="early",
    )(number, turned, stay(delta))


def weight_kernel(
    replicas, which, flag_ref, number_ref, turned, delta_hbm, came, early_first, early_second, *refs
):
    outs, (delta, sem) = refs[:2], refs[2:]
    rows, width = delta.shape
    half = width // 2
    last = delta_hbm.shape[0] - 1
    load = pltpu.make_async_copy(delta_hbm.at[last], delta, sem.at[0])
    load.start()
    load.wait()

    @pl.when(flag_ref[0] == 1)
    def _():
        delta[...] = (came[...].astype(F32) * delta[...].astype(F32)).astype(BF16)

    for c, (bits, early) in enumerate(zip(bit_orders(replicas), (early_first, early_second))):
        columns = slice(last * rows, (last + 1) * rows)
        left = picked_rows(turned, number_ref[0], bits, which, width // replicas, columns)
        for at in range(0, half, TILE):
            product = dot(left, delta[:, c * half + at : c * half + at + TILE], NN)
            outs[c][:, at : at + TILE] = (early[:, at : at + TILE] + product).astype(outs[c].dtype)


def weight_call(which, flag, number, turned, delta, came, early, replicas):
    micros, rows, width = delta.shape
    half = (width // 2, width // 2)
    return pl.pallas_call(
        functools.partial(weight_kernel, replicas, which),
        out_shape=(jax.ShapeDtypeStruct(half, F32) if which else pltpu.HBM(half, BF16),) * 2,
        in_specs=[SMEM, SMEM, VMEM, HBM, VMEM, VMEM, VMEM],
        out_specs=(VMEM,) * 2,
        scratch_shapes=[pltpu.VMEM((rows, width), BF16), pltpu.SemaphoreType.DMA((1,))],
        compiler_params=pltpu.CompilerParams(vmem_limit_bytes=14 * MIB),
        cost_estimate=LIGHT,
        name="weight",
    )(flag, number, turned, stay(delta), came, *early)


def own_half(keep, got, bit):
    mine = (lax.axis_index("dp") >> bit) & 1

    def pick(which):
        return lax.dynamic_index_in_dim(keep, which, 0, keepdims=False) + lax.dynamic_index_in_dim(
            got, which, 0, keepdims=False
        ).astype(F32)

    return pick(1 - mine).astype(BF16), pick(mine)


def finish_scatter(send, keep, bits, axes, pairs_of):
    for n, bit in enumerate(bits):
        got = lax.ppermute(send, axes, pairs_of(bit))
        if n + 1 < len(bits):
            lead = (2, keep.shape[0] // 2, keep.shape[1])
            send, keep = own_half(keep.reshape(lead), got.reshape(lead), bits[n + 1])
    return keep + got.astype(F32)


def body(activations, section_weights, cand_table, cand_index, cand_count, pooled_cotangent):
    sections = lax.axis_size("section")
    replicas = lax.axis_size("dp")
    position = lax.axis_index("section")
    replica = lax.axis_index("dp")
    last = sections - 1
    final_flag = position == last
    acts = activations[0]
    weight = section_weights[0]
    micro_count, row_count, model_width = acts.shape

    def flag(truth):
        return truth.astype(jnp.int32).reshape(1)

    number = replica.reshape(1)
    count = cand_count.reshape(1, micro_count)
    pooled = pooled_cotangent.reshape(micro_count, model_width)
    final = flag(final_flag)
    grads, shares, slants, highs = [], [], [], []
    delta = acts
    for m in range(micro_count):
        grad, delta, share, slant, high = first_call(
            m, final, count, acts, weight, cand_table, cand_index, pooled, delta
        )
        grads.append(grad)
        shares.append(share)
        slants.append(slant)
        highs.append(high)

    def pairs(bit):
        return [(i, i ^ (1 << bit)) for i in range(replicas)]

    for hop in range(last):
        source = last - hop
        received = [lax.ppermute(g, "section", [(source, source - 1)]) for g in grads]
        active = flag(position == source - 1)
        for m in range(micro_count):
            if hop + 1 < last:
                after = token if hop == 1 and m == 0 else acts
                grads[m], delta = hop_call(m, active, received[m], delta, weight, after, True)
            elif m + 1 < micro_count:
                (delta,) = hop_call(m, active, received[m], delta, weight, acts, False)
        if hop == 0:
            parts = table_call(
                final, cand_index, pooled, cand_table.shape[0], grads[-1], shares, slants, highs, sections
            )
            turned, token = turn_call(acts, grads[-1])

    spread = [lax.ppermute(parts[s], "section", [(last, s)]) for s in range(last)]
    table_part = jnp.where(final_flag, parts[last], sum(spread))
    table_sum = lax.psum_scatter(table_part, "dp", scatter_dimension=0, tiled=True).astype(F32)

    orders = bit_orders(replicas)
    early = early_call(number, turned, delta, replicas)
    sends = weight_call(0, active, number, turned, delta, received[-1], early[::2], replicas)
    keeps = weight_call(1, active, number, turned, delta, received[-1], early[1::2], replicas)
    sums = [finish_scatter(sends[c], keeps[c], orders[c], "dp", pairs) for c in range(2)]
    return jnp.concatenate(sums, axis=1)[None], table_sum


def solution(mesh):
    in_specs = (
        P("section", None, "dp", None),
        P("section", None, None),
        P(),
        P(None, "dp", None),
        P(None, "dp"),
        P(None, "dp", None),
    )
    out_specs = (P("section", "dp", None), P("dp", "section"))
    return jax.shard_map(body, mesh=mesh, in_specs=in_specs, out_specs=out_specs, check_vma=False)
```

```python
import functools
import math

import jax
import jax.numpy as jnp
from jax import lax
from jax.experimental import pallas as pl
from jax.experimental.pallas import tpu as pltpu
from jax.sharding import PartitionSpec as P

HEAD = 64
PAIR = 2 * HEAD
TILE = 256
MIB = 1024 * 1024
HBM = pl.BlockSpec(memory_space=pltpu.HBM)
VMEM = pl.BlockSpec(memory_space=pltpu.VMEM)
SMEM = pl.BlockSpec(memory_space=pltpu.SMEM)
BF16 = jnp.bfloat16
F32 = jnp.float32
LIGHT = pl.CostEstimate(flops=1024, bytes_accessed=1024, transcendentals=0)

NN = (((1,), (0,)), ((), ()))
NT = (((1,), (1,)), ((), ()))
TN = (((0,), (0,)), ((), ()))


def dot(left, right, dims):
    return lax.dot_general(left, right, dims, preferred_element_type=F32)


def gelu_parts(hidden):
    root = math.sqrt(2.0 / math.pi)
    square = hidden * hidden
    bent = jnp.tanh(root * hidden * (1.0 + 0.044715 * square))
    share = 0.5 + 0.5 * bent
    slope = share + (0.5 * root) * hidden * (1.0 - bent * bent) * (1.0 + (3 * 0.044715) * square)
    return hidden * share, slope


def high_low(values):
    high = values.astype(BF16)
    return high, (values - high.astype(F32)).astype(BF16)


def stay(array):
    return pltpu.with_memory_space_constraint(array, pltpu.HBM)


def own_heads(width):
    shift = HEAD.bit_length() - 1
    row = lax.broadcasted_iota(jnp.int32, (PAIR, width), 0) >> shift
    return row == ((lax.broadcasted_iota(jnp.int32, (PAIR, width), 1) >> shift) & 1)


def first_kernel(
    m, flag_ref, count_hbm, acts_in, weight_in, table_in, index_hbm, pooled_hbm, delta_in,
    grad_hbm, delta_hbm, share_hbm, slant_hbm, high_hbm,
    count_ref, acts_buf, weight_buf, table_buf, index_ref, pooled_ref, grad, aux, share_ref, slant_ref, high_ref, sems,
):
    micros, rows, width = acts_in.shape
    table_rows = table_in.shape[0]
    pairs = width // PAIR
    tiles = width // TILE
    tile = [slice(q * TILE, (q + 1) * TILE) for q in range(tiles)]
    pair = [slice(j * PAIR, (j + 1) * PAIR) for j in range(pairs)]

    def copy(source, target, at):
        started = pltpu.make_async_copy(source, target, sems.at[at])
        started.start()
        return started

    if m == 0:
        acts_ref, weight, table = acts_buf, weight_buf, table_buf

        @pl.when(flag_ref[0] == 0)
        def _():
            load_weight = copy(weight_in, weight, 0)
            loads = [copy(acts_in.at[k], acts_ref.at[k], 1 + k) for k in range(micros)]
            load_weight.wait()
            stores = []
            for k in range(micros):
                loads[k].wait()
                for cols in tile:
                    hidden = dot(acts_ref[k], weight[:, cols], NN)
                    aux[k, :, cols] = gelu_parts(hidden)[1].astype(BF16)
                stores.append(copy(aux.at[k], delta_hbm.at[k], 1 + micros + k))
            for store in stores:
                store.wait()

    else:
        acts_ref, weight, table = acts_in, weight_in, table_in

    @pl.when(flag_ref[0] == 1)
    def _():
        loads = [copy(index_hbm, index_ref, 0), copy(pooled_hbm, pooled_ref, 1), copy(count_hbm, count_ref, 2)]
        if m == 0:
            loads.append(copy(table_in, table, 3))
            load_weight = copy(weight_in, weight, 4)
            load_acts = copy(acts_in.at[0], acts_ref.at[0], 5)
            load_acts.wait()
            load_weight.wait()
        acts = acts_ref.at[m]
        slopes, lows = [], []
        for cols in tile:
            hidden = dot(acts[...], weight[:, cols], NN)
            bent, slope = gelu_parts(hidden)
            high, low = high_low(acts[:, cols].astype(F32) + bent)
            high_ref[:, cols] = high
            slopes.append(slope)
            lows.append(low)
        store_high = copy(high_ref, high_hbm, 6)
        for load in loads:
            load.wait()
        index = index_ref[m]
        index = jnp.concatenate([index, index], axis=1)
        onehot = (lax.broadcasted_iota(jnp.int32, (table_rows, PAIR), 0) == index).astype(BF16)
        gathered = dot(onehot, table[...], TN)
        own = own_heads(width)
        keys = jnp.where(own, gathered[:, :width] * (1.0 / math.sqrt(HEAD)), 0.0).astype(BF16)
        values = jnp.where(own, gathered[:, width:], 0.0).astype(BF16)
        allowed = lax.broadcasted_iota(jnp.int32, (2, HEAD, rows), 1) < count_ref[0, m]
        given_row = pooled_ref[m : m + 1].astype(F32) * (1.0 / rows)
        given = jnp.broadcast_to(given_row, (rows, width)).astype(BF16)
        scores = []
        for j, here in enumerate(pair):
            part = slice(j * PAIR % TILE, j * PAIR % TILE + PAIR)
            scores.append(
                dot(
                    jnp.concatenate([keys[:, here], keys[:, here]], axis=1),
                    jnp.concatenate([high_ref[:, here], lows[j * PAIR // TILE][:, part]], axis=1),
                    NT,
                )
            )
        slants = []
        for j, here in enumerate(pair):
            share, slant = soften(scores[j], dot(values[:, here], given[:, here], NT), allowed)
            share_ref[here] = share
            slant_ref[here] = slant
            slants.append(slant)
        store_share = copy(share_ref, share_hbm, 7)
        store_slant = copy(slant_ref, slant_hbm, 10)
        totals = []
        for j, here in enumerate(pair):
            part = slice(j * PAIR % TILE, j * PAIR % TILE + PAIR)
            total = given_row[:, here] + dot(slants[j], keys[:, here], TN)
            totals.append(total)
            aux[0, :, here] = (total * slopes[j * PAIR // TILE][:, part]).astype(BF16)
        store_aux = copy(aux.at[0], delta_hbm.at[m], 8)
        for q, cols in enumerate(tile):
            total = jnp.concatenate(totals[q * TILE // PAIR : (q + 1) * TILE // PAIR], axis=1)
            grad[:, cols] = (total + dot(aux[0], weight[cols, :], NT)).astype(BF16)
        store_grad = copy(grad, grad_hbm, 9)
        store_high.wait()
        store_share.wait()
        store_slant.wait()
        store_aux.wait()
        store_grad.wait()


def lean(share, worth):
    worth = worth.reshape(share.shape)
    centre = jnp.sum(share * worth, axis=1, keepdims=True)
    return (share * (worth - centre)).reshape(worth.shape[0] * worth.shape[1], -1).astype(BF16)


def soften(score, worth, allowed):
    score = jnp.where(allowed, score.reshape(allowed.shape), -1e30)
    raised = jnp.exp(score - jnp.max(score, axis=1, keepdims=True))
    share = raised * (1.0 / jnp.sum(raised, axis=1, keepdims=True))
    return share.reshape(worth.shape).astype(BF16), lean(share, worth)


def first_call(m, flag, count, acts, weight, table, index, pooled, delta):
    micros, rows, width = acts.shape
    turned = (width // HEAD * index.shape[2], rows)
    block = pltpu.HBM((rows, width), BF16)
    big = HBM if m == 0 else VMEM
    small = pltpu.VMEM((8, 128), BF16)
    return pl.pallas_call(
        functools.partial(first_kernel, m),
        out_shape=(block, pltpu.HBM(acts.shape, BF16), pltpu.HBM(turned, BF16), pltpu.HBM(turned, BF16), block),
        in_specs=[SMEM, HBM, big, big, big, HBM, HBM, HBM],
        out_specs=(HBM,) * 5,
        scratch_shapes=[
            pltpu.SMEM(count.shape, jnp.int32),
            pltpu.VMEM(acts.shape, BF16) if m == 0 else small,
            pltpu.VMEM(weight.shape, BF16) if m == 0 else small,
            pltpu.VMEM(table.shape, BF16) if m == 0 else small,
            pltpu.VMEM(index.shape, jnp.int32),
            pltpu.VMEM(pooled.shape, BF16),
            pltpu.VMEM((rows, width), BF16),
            pltpu.VMEM((micros if m == 0 else 1, rows, width), BF16),
            pltpu.VMEM(turned, BF16),
            pltpu.VMEM(turned, BF16),
            pltpu.VMEM((rows, width), BF16),
            pltpu.SemaphoreType.DMA((max(11, 1 + 2 * micros),)),
        ],
        input_output_aliases={} if m == 0 else {7: 1},
        compiler_params=pltpu.CompilerParams(vmem_limit_bytes=18 * MIB),
        cost_estimate=LIGHT,
        name="first",
    )(
        flag,
        stay(count),
        *(stay(array) if m == 0 else array for array in (acts, weight, table)),
        stay(index),
        stay(pooled),
        stay(delta),
    )


def table_kernel(flag_ref, index_ref, pooled_ref, after_hbm, *refs):
    share, slant, high, kv, sems = refs[-5:]
    count, rows, width = high.shape
    sections = (len(refs) - 5 - 3 * count) // 2
    sources, outs, parts = refs[: 3 * count], refs[3 * count : -5 - sections], refs[-5 - sections : -5]
    table_rows, span = parts[0].shape
    cands = index_ref.shape[2]

    @pl.when(flag_ref[0] == 1)
    def _():
        loads = []
        for m in range(count):
            for k, target in enumerate((share, slant, high)):
                loads.append(pltpu.make_async_copy(sources[k * count + m], target.at[m], sems.at[3 * m + k]))
        for load in loads:
            load.start()
        row = lax.broadcasted_iota(jnp.int32, (table_rows, cands), 0)
        head = lax.broadcasted_iota(jnp.int32, (cands, TILE), 1) >> (HEAD.bit_length() - 1)
        ones = jnp.ones((rows, PAIR), BF16)
        onehot = jnp.concatenate([(row == index_ref[m]).astype(BF16) for m in range(count)], axis=1)

        def by_head(blocks):
            chosen = blocks[0]
            for k in range(1, len(blocks)):
                chosen = jnp.where(head == k, blocks[k], chosen)
            return chosen

        for m in range(count):
            given = pooled_ref[m : m + 1].astype(F32) * (1.0 / rows)
            lines = slice(m * cands, (m + 1) * cands)
            for k in range(3):
                loads[3 * m + k].wait()
            column = dot(share[m], ones, NN)
            column = jnp.concatenate([column, column], axis=1)
            for q in range(width // TILE):
                cols = slice(q * TILE, (q + 1) * TILE)
                key = dot(slant[m, cols], high[m, :, cols], NN) * (1.0 / math.sqrt(HEAD))
                starts = range(0, TILE, cands)
                kv[lines, cols] = by_head([key[at : at + cands] for at in starts])
                value = by_head([column[q * TILE + at : q * TILE + at + cands] for at in starts])
                kv[lines, width + q * TILE : width + (q + 1) * TILE] = value * given[:, cols]
        stores = []
        for k, part in enumerate(parts):
            kv_high, kv_low = high_low(kv[:, k * span : (k + 1) * span])
            part[...] = (dot(onehot, kv_high, NN) + dot(onehot, kv_low, NN)).astype(BF16)
            stores.append(pltpu.make_async_copy(part, outs[k], sems.at[3 * count + k]))
            stores[k].start()
        for store in stores:
            store.wait()


def table_call(flag, index, pooled, table_rows, after, shares, slants, highs, sections):
    rows, width = highs[0].shape
    count = len(highs)
    part = (table_rows, 2 * width // sections)
    return pl.pallas_call(
        table_kernel,
        out_shape=(pltpu.HBM(part, BF16),) * sections,
        in_specs=[SMEM, VMEM, VMEM, HBM] + [HBM] * (3 * count),
        out_specs=(HBM,) * sections,
        scratch_shapes=[pltpu.VMEM(part, BF16)] * sections
        + [
            pltpu.VMEM((count,) + shares[0].shape, BF16),
            pltpu.VMEM((count,) + slants[0].shape, BF16),
            pltpu.VMEM((count,) + highs[0].shape, BF16),
            pltpu.VMEM((count * index.shape[2], 2 * width), F32),
            pltpu.SemaphoreType.DMA((3 * count + sections,)),
        ],
        compiler_params=pltpu.CompilerParams(vmem_limit_bytes=18 * MIB),
        cost_estimate=LIGHT,
        name="table",
    )(flag, index, pooled, stay(after), *map(stay, shares), *map(stay, slants), *map(stay, highs))


def hop_kernel(m, with_grad, flag_ref, came_hbm, delta_in, weight, after_hbm, *rest):
    if with_grad:
        grad_hbm, delta_hbm, came, aux, grad, sems = rest
    else:
        delta_hbm, came, aux, sems = rest
    width = came.shape[1]

    @pl.when(flag_ref[0] == 1)
    def _():
        first = pltpu.make_async_copy(came_hbm, came, sems.at[0])
        second = pltpu.make_async_copy(delta_in.at[m], aux, sems.at[1])
        first.start()
        second.start()
        first.wait()
        second.wait()
        aux[...] = (came[...].astype(F32) * aux[...].astype(F32)).astype(BF16)
        stores = [pltpu.make_async_copy(aux, delta_hbm.at[m], sems.at[2])]
        stores[0].start()
        if with_grad:
            for n in range(width // TILE):
                part = slice(n * TILE, (n + 1) * TILE)
                grad[:, part] = (came[:, part].astype(F32) + dot(aux[...], weight[part, :], NT)).astype(BF16)
            stores.append(pltpu.make_async_copy(grad, grad_hbm, sems.at[3]))
            stores[-1].start()
        for store in stores:
            store.wait()


def hop_call(m, flag, came, delta, weight, after, with_grad):
    rows, width = came.shape
    scratch = [pltpu.VMEM((rows, width), BF16)] * (3 if with_grad else 2)
    scratch.append(pltpu.SemaphoreType.DMA((4,)))
    outs = (pltpu.HBM(delta.shape, BF16),)
    if with_grad:
        outs = (pltpu.HBM((rows, width), BF16),) + outs
    return pl.pallas_call(
        functools.partial(hop_kernel, m, with_grad),
        out_shape=outs,
        in_specs=[SMEM, HBM, HBM, VMEM if with_grad else HBM, HBM],
        out_specs=(HBM,) * len(outs),
        scratch_shapes=scratch,
        input_output_aliases={2: len(outs) - 1},
        compiler_params=pltpu.CompilerParams(vmem_limit_bytes=12 * MIB),
        cost_estimate=LIGHT,
        name="hop" if with_grad else "end",
    )(flag, came, stay(delta), weight if with_grad else stay(weight), stay(after))


def bit_orders(replicas):
    bits = list(range(replicas.bit_length() - 1))
    return [bits, bits[1::-1] + bits[2:]]


def block_order(bits):
    rest = bits[1:]
    order = []
    for i in range(1 << len(rest)):
        order.append(sum(((i >> (len(rest) - 1 - k)) & 1) << bit for k, bit in enumerate(rest)))
    return order


def turn_kernel(acts_hbm, after_hbm, out, token_ref, acts, sems):
    count, rows, width = acts.shape
    token_ref[...] = jnp.zeros_like(token_ref)
    loads = [pltpu.make_async_copy(acts_hbm.at[m], acts.at[m], sems.at[m]) for m in range(count)]
    for load in loads:
        load.start()
    for m in range(count):
        loads[m].wait()
        out[:, m * rows : (m + 1) * rows] = acts[m].T


def turn_call(acts, after):
    count, rows, width = acts.shape
    return pl.pallas_call(
        turn_kernel,
        out_shape=(jax.ShapeDtypeStruct((width, count * rows), BF16), pltpu.HBM((16, 128), BF16)),
        in_specs=[HBM, HBM],
        out_specs=(VMEM,) * 2,
        scratch_shapes=[pltpu.VMEM(acts.shape, BF16), pltpu.SemaphoreType.DMA((count,))],
        compiler_params=pltpu.CompilerParams(vmem_limit_bytes=14 * MIB),
        cost_estimate=LIGHT,
        name="turn",
    )(stay(acts), stay(after))


def picked_rows(turned, number, bits, which, size, columns):
    mine = (number >> bits[0]) & 1
    base = (mine if which else 1 - mine) << bits[0]
    return jnp.concatenate(
        [turned[pl.ds(pl.multiple_of((base + block) * size, size), size), columns] for block in block_order(bits)],
        axis=0,
    )


def early_kernel(replicas, number_ref, turned, delta_hbm, *refs):
    outs, (delta, sems) = refs[:4], refs[4:]
    micros, rows, width = delta.shape
    half = width // 2
    loads = [pltpu.make_async_copy(delta_hbm.at[m], delta.at[m], sems.at[m]) for m in range(micros)]
    for load in loads:
        load.start()
    for load in loads:
        load.wait()
    flat = delta.reshape(micros * rows, width)
    for c, bits in enumerate(bit_orders(replicas)):
        for which in range(2):
            left = picked_rows(turned, number_ref[0], bits, which, width // replicas, slice(0, micros * rows))
            for at in range(0, half, TILE):
                outs[2 * c + which][:, at : at + TILE] = dot(
                    left, flat[:, c * half + at : c * half + at + TILE], NN
                )


def early_call(number, turned, delta, replicas):
    micros, rows, width = delta.shape
    half = jax.ShapeDtypeStruct((width // 2, width // 2), F32)
    return pl.pallas_call(
        functools.partial(early_kernel, replicas),
        out_shape=(half,) * 4,
        in_specs=[SMEM, VMEM, HBM],
        out_specs=(VMEM,) * 4,
        scratch_shapes=[
            pltpu.VMEM((micros - 1, rows, width), BF16),
            pltpu.SemaphoreType.DMA((micros - 1,)),
        ],
        compiler_params=pltpu.CompilerParams(vmem_limit_bytes=18 * MIB),
        cost_estimate=LIGHT,
        name="early",
    )(number, turned, stay(delta))


def weight_kernel(
    replicas, which, flag_ref, number_ref, turned, delta_hbm, came, early_first, early_second, *refs
):
    outs, (delta, sem) = refs[:2], refs[2:]
    rows, width = delta.shape
    half = width // 2
    last = delta_hbm.shape[0] - 1
    load = pltpu.make_async_copy(delta_hbm.at[last], delta, sem.at[0])
    load.start()
    load.wait()

    @pl.when(flag_ref[0] == 1)
    def _():
        delta[...] = (came[...].astype(F32) * delta[...].astype(F32)).astype(BF16)

    for c, (bits, early) in enumerate(zip(bit_orders(replicas), (early_first, early_second))):
        columns = slice(last * rows, (last + 1) * rows)
        left = picked_rows(turned, number_ref[0], bits, which, width // replicas, columns)
        for at in range(0, half, TILE):
            product = dot(left, delta[:, c * half + at : c * half + at + TILE], NN)
            outs[c][:, at : at + TILE] = (early[:, at : at + TILE] + product).astype(outs[c].dtype)


def weight_call(which, flag, number, turned, delta, came, early, replicas):
    micros, rows, width = delta.shape
    half = (width // 2, width // 2)
    return pl.pallas_call(
        functools.partial(weight_kernel, replicas, which),
        out_shape=(jax.ShapeDtypeStruct(half, F32) if which else pltpu.HBM(half, BF16),) * 2,
        in_specs=[SMEM, SMEM, VMEM, HBM, VMEM, VMEM, VMEM],
        out_specs=(VMEM,) * 2,
        scratch_shapes=[pltpu.VMEM((rows, width), BF16), pltpu.SemaphoreType.DMA((1,))],
        compiler_params=pltpu.CompilerParams(vmem_limit_bytes=14 * MIB),
        cost_estimate=LIGHT,
        name="weight",
    )(flag, number, turned, stay(delta), came, *early)


def own_half(keep, got, bit):
    mine = (lax.axis_index("dp") >> bit) & 1

    def pick(which):
        return lax.dynamic_index_in_dim(keep, which, 0, keepdims=False) + lax.dynamic_index_in_dim(
            got, which, 0, keepdims=False
        ).astype(F32)

    return pick(1 - mine).astype(BF16), pick(mine)


def join_kernel(first, first_got, second, second_got, out):
    half = first.shape[1]
    out[:, :half] = first[...] + first_got[...].astype(F32)
    out[:, half:] = second[...] + second_got[...].astype(F32)


def join_call(keeps, gots):
    rows, half = keeps[0].shape
    return pl.pallas_call(
        join_kernel,
        out_shape=jax.ShapeDtypeStruct((rows, 2 * half), F32),
        in_specs=[VMEM] * 4,
        out_specs=VMEM,
        cost_estimate=LIGHT,
        name="join",
    )(keeps[0], gots[0], keeps[1], gots[1])


def scatter_sums(sends, keeps, table, orders, pairs_of):
    steps = len(orders[0])
    sends, keeps = list(sends), list(keeps)
    for n in range(steps):
        gots = [lax.ppermute(send, "dp", pairs_of(bits[n])) for send, bits in zip(sends, orders)]
        for c, bits in enumerate(orders):
            if n + 1 < steps:
                lead = (2, keeps[c].shape[0] // 2, keeps[c].shape[1])
                sends[c], keeps[c] = own_half(keeps[c].reshape(lead), gots[c].reshape(lead), bits[n + 1])
        if n + 2 == steps:
            table, _ = lax.optimization_barrier((table, tuple(sends)))
    blocks = lax.all_to_all(table.reshape(1 << steps, -1, table.shape[1]), "dp", 0, 0)
    return join_call(keeps, gots), jnp.sum(blocks.astype(F32), axis=0)


def body(activations, section_weights, cand_table, cand_index, cand_count, pooled_cotangent):
    sections = lax.axis_size("section")
    replicas = lax.axis_size("dp")
    position = lax.axis_index("section")
    replica = lax.axis_index("dp")
    last = sections - 1
    final_flag = position == last
    acts = activations[0]
    weight = section_weights[0]
    micro_count, row_count, model_width = acts.shape

    def flag(truth):
        return truth.astype(jnp.int32).reshape(1)

    number = replica.reshape(1)
    count = cand_count.reshape(1, micro_count)
    pooled = pooled_cotangent.reshape(micro_count, model_width)
    final = flag(final_flag)
    grads, shares, slants, highs = [], [], [], []
    delta = acts
    for m in range(micro_count):
        grad, delta, share, slant, high = first_call(
            m, final, count, acts, weight, cand_table, cand_index, pooled, delta
        )
        grads.append(grad)
        shares.append(share)
        slants.append(slant)
        highs.append(high)

    def pairs(bit):
        return [(i, i ^ (1 << bit)) for i in range(replicas)]

    for hop in range(last):
        source = last - hop
        received = [lax.ppermute(g, "section", [(source, source - 1)]) for g in grads]
        active = flag(position == source - 1)
        for m in range(micro_count):
            if hop + 1 < last:
                after = token if hop == 1 and m == 0 else acts
                grads[m], delta = hop_call(m, active, received[m], delta, weight, after, True)
            elif m + 1 < micro_count:
                (delta,) = hop_call(m, active, received[m], delta, weight, acts, False)
        if hop == 0:
            parts = table_call(
                final, cand_index, pooled, cand_table.shape[0], grads[-1], shares, slants, highs, sections
            )
            turned, token = turn_call(acts, grads[-1])

    spread = [lax.ppermute(parts[s], "section", [(last, s)]) for s in range(last)]
    table_part = jnp.where(final_flag, parts[last], sum(spread))

    orders = bit_orders(replicas)
    early = early_call(number, turned, delta, replicas)
    sends = weight_call(0, active, number, turned, delta, received[-1], early[::2], replicas)
    keeps = weight_call(1, active, number, turned, delta, received[-1], early[1::2], replicas)
    sums, table_sum = scatter_sums(sends, keeps, table_part, orders, pairs)
    return sums[None], table_sum


def solution(mesh):
    in_specs = (
        P("section", None, "dp", None),
        P("section", None, None),
        P(),
        P(None, "dp", None),
        P(None, "dp"),
        P(None, "dp", None),
    )
    out_specs = (P("section", "dp", None), P("dp", "section"))
    return jax.shard_map(body, mesh=mesh, in_specs=in_specs, out_specs=out_specs, check_vma=False)
```

```python
import functools
import math

import jax
import jax.numpy as jnp
from jax import lax
from jax.experimental import pallas as pl
from jax.experimental.pallas import tpu as pltpu
from jax.sharding import PartitionSpec as P

HEAD = 64
PAIR = 2 * HEAD
TILE = 256
MIB = 1024 * 1024
HBM = pl.BlockSpec(memory_space=pltpu.HBM)
VMEM = pl.BlockSpec(memory_space=pltpu.VMEM)
SMEM = pl.BlockSpec(memory_space=pltpu.SMEM)
BF16 = jnp.bfloat16
F32 = jnp.float32
LIGHT = pl.CostEstimate(flops=1024, bytes_accessed=1024, transcendentals=0)

NN = (((1,), (0,)), ((), ()))
NT = (((1,), (1,)), ((), ()))
TN = (((0,), (0,)), ((), ()))


def dot(left, right, dims):
    return lax.dot_general(left, right, dims, preferred_element_type=F32)


def gelu_parts(hidden):
    root = math.sqrt(2.0 / math.pi)
    square = hidden * hidden
    bent = jnp.tanh(root * hidden * (1.0 + 0.044715 * square))
    share = 0.5 + 0.5 * bent
    slope = share + (0.5 * root) * hidden * (1.0 - bent * bent) * (1.0 + (3 * 0.044715) * square)
    return hidden * share, slope


def high_low(values):
    high = values.astype(BF16)
    return high, (values - high.astype(F32)).astype(BF16)


def stay(array):
    return pltpu.with_memory_space_constraint(array, pltpu.HBM)


def own_heads(width):
    shift = HEAD.bit_length() - 1
    row = lax.broadcasted_iota(jnp.int32, (PAIR, width), 0) >> shift
    return row == ((lax.broadcasted_iota(jnp.int32, (PAIR, width), 1) >> shift) & 1)


def first_kernel(
    m, flag_ref, count_hbm, acts_in, weight_in, table_in, index_hbm, pooled_hbm, delta_in,
    grad_hbm, delta_hbm, share_hbm, slant_hbm, high_hbm,
    count_ref, acts_buf, weight_buf, table_buf, index_ref, pooled_ref, grad, aux, share_ref, slant_ref, high_ref, sems,
):
    micros, rows, width = acts_in.shape
    table_rows = table_in.shape[0]
    pairs = width // PAIR
    tiles = width // TILE
    tile = [slice(q * TILE, (q + 1) * TILE) for q in range(tiles)]
    pair = [slice(j * PAIR, (j + 1) * PAIR) for j in range(pairs)]

    def copy(source, target, at):
        started = pltpu.make_async_copy(source, target, sems.at[at])
        started.start()
        return started

    if m == 0:
        acts_ref, weight, table = acts_buf, weight_buf, table_buf

        @pl.when(flag_ref[0] == 0)
        def _():
            load_weight = copy(weight_in, weight, 0)
            loads = [copy(acts_in.at[k], acts_ref.at[k], 1 + k) for k in range(micros)]
            load_weight.wait()
            stores = []
            for k in range(micros):
                loads[k].wait()
                for cols in tile:
                    hidden = dot(acts_ref[k], weight[:, cols], NN)
                    aux[k, :, cols] = gelu_parts(hidden)[1].astype(BF16)
                stores.append(copy(aux.at[k], delta_hbm.at[k], 1 + micros + k))
            for store in stores:
                store.wait()

    else:
        acts_ref, weight, table = acts_in, weight_in, table_in

    @pl.when(flag_ref[0] == 1)
    def _():
        loads = [copy(index_hbm, index_ref, 0), copy(pooled_hbm, pooled_ref, 1), copy(count_hbm, count_ref, 2)]
        if m == 0:
            loads.append(copy(table_in, table, 3))
            load_weight = copy(weight_in, weight, 4)
            load_acts = copy(acts_in.at[0], acts_ref.at[0], 5)
            load_acts.wait()
            load_weight.wait()
        acts = acts_ref.at[m]
        slopes, lows = [], []
        for cols in tile:
            hidden = dot(acts[...], weight[:, cols], NN)
            bent, slope = gelu_parts(hidden)
            high, low = high_low(acts[:, cols].astype(F32) + bent)
            high_ref[:, cols] = high
            slopes.append(slope)
            lows.append(low)
        store_high = copy(high_ref, high_hbm, 6)
        for load in loads:
            load.wait()
        index = index_ref[m]
        index = jnp.concatenate([index, index], axis=1)
        onehot = (lax.broadcasted_iota(jnp.int32, (table_rows, PAIR), 0) == index).astype(BF16)
        gathered = dot(onehot, table[...], TN)
        own = own_heads(width)
        keys = jnp.where(own, gathered[:, :width] * (1.0 / math.sqrt(HEAD)), 0.0).astype(BF16)
        values = jnp.where(own, gathered[:, width:], 0.0).astype(BF16)
        allowed = lax.broadcasted_iota(jnp.int32, (2, HEAD, rows), 1) < count_ref[0, m]
        given_row = pooled_ref[m : m + 1].astype(F32) * (1.0 / rows)
        given = jnp.broadcast_to(given_row, (rows, width)).astype(BF16)
        scores = []
        for j, here in enumerate(pair):
            part = slice(j * PAIR % TILE, j * PAIR % TILE + PAIR)
            scores.append(
                dot(
                    jnp.concatenate([keys[:, here], keys[:, here]], axis=1),
                    jnp.concatenate([high_ref[:, here], lows[j * PAIR // TILE][:, part]], axis=1),
                    NT,
                )
            )
        slants = []
        for j, here in enumerate(pair):
            share, slant = soften(scores[j], dot(values[:, here], given[:, here], NT), allowed)
            share_ref[here] = share
            slant_ref[here] = slant
            slants.append(slant)
        store_share = copy(share_ref, share_hbm, 7)
        store_slant = copy(slant_ref, slant_hbm, 10)
        totals = []
        for j, here in enumerate(pair):
            part = slice(j * PAIR % TILE, j * PAIR % TILE + PAIR)
            total = given_row[:, here] + dot(slants[j], keys[:, here], TN)
            totals.append(total)
            aux[0, :, here] = (total * slopes[j * PAIR // TILE][:, part]).astype(BF16)
        store_aux = copy(aux.at[0], delta_hbm.at[m], 8)
        for q, cols in enumerate(tile):
            total = jnp.concatenate(totals[q * TILE // PAIR : (q + 1) * TILE // PAIR], axis=1)
            grad[:, cols] = (total + dot(aux[0], weight[cols, :], NT)).astype(BF16)
        store_grad = copy(grad, grad_hbm, 9)
        store_high.wait()
        store_share.wait()
        store_slant.wait()
        store_aux.wait()
        store_grad.wait()


def lean(share, worth):
    worth = worth.reshape(share.shape)
    centre = jnp.sum(share * worth, axis=1, keepdims=True)
    return (share * (worth - centre)).reshape(worth.shape[0] * worth.shape[1], -1).astype(BF16)


def soften(score, worth, allowed):
    score = jnp.where(allowed, score.reshape(allowed.shape), -1e30)
    raised = jnp.exp(score - jnp.max(score, axis=1, keepdims=True))
    share = raised * (1.0 / jnp.sum(raised, axis=1, keepdims=True))
    return share.reshape(worth.shape).astype(BF16), lean(share, worth)


def first_call(m, flag, count, acts, weight, table, index, pooled, delta):
    micros, rows, width = acts.shape
    turned = (width // HEAD * index.shape[2], rows)
    block = pltpu.HBM((rows, width), BF16)
    big = HBM if m == 0 else VMEM
    small = pltpu.VMEM((8, 128), BF16)
    return pl.pallas_call(
        functools.partial(first_kernel, m),
        out_shape=(block, pltpu.HBM(acts.shape, BF16), pltpu.HBM(turned, BF16), pltpu.HBM(turned, BF16), block),
        in_specs=[SMEM, HBM, big, big, big, HBM, HBM, HBM],
        out_specs=(HBM,) * 5,
        scratch_shapes=[
            pltpu.SMEM(count.shape, jnp.int32),
            pltpu.VMEM(acts.shape, BF16) if m == 0 else small,
            pltpu.VMEM(weight.shape, BF16) if m == 0 else small,
            pltpu.VMEM(table.shape, BF16) if m == 0 else small,
            pltpu.VMEM(index.shape, jnp.int32),
            pltpu.VMEM(pooled.shape, BF16),
            pltpu.VMEM((rows, width), BF16),
            pltpu.VMEM((micros if m == 0 else 1, rows, width), BF16),
            pltpu.VMEM(turned, BF16),
            pltpu.VMEM(turned, BF16),
            pltpu.VMEM((rows, width), BF16),
            pltpu.SemaphoreType.DMA((max(11, 1 + 2 * micros),)),
        ],
        input_output_aliases={} if m == 0 else {7: 1},
        compiler_params=pltpu.CompilerParams(vmem_limit_bytes=18 * MIB),
        cost_estimate=LIGHT,
        name="first",
    )(
        flag,
        stay(count),
        *(stay(array) if m == 0 else array for array in (acts, weight, table)),
        stay(index),
        stay(pooled),
        stay(delta),
    )


def table_kernel(flag_ref, index_ref, pooled_ref, after_hbm, *refs):
    share, slant, high, kv, sems = refs[-5:]
    count, rows, width = high.shape
    sections = (len(refs) - 5 - 3 * count) // 2
    sources, outs, parts = refs[: 3 * count], refs[3 * count : -5 - sections], refs[-5 - sections : -5]
    table_rows, span = parts[0].shape
    cands = index_ref.shape[2]

    @pl.when(flag_ref[0] == 1)
    def _():
        loads = []
        for m in range(count):
            for k, target in enumerate((share, slant, high)):
                loads.append(pltpu.make_async_copy(sources[k * count + m], target.at[m], sems.at[3 * m + k]))
        for load in loads:
            load.start()
        row = lax.broadcasted_iota(jnp.int32, (table_rows, cands), 0)
        head = lax.broadcasted_iota(jnp.int32, (cands, TILE), 1) >> (HEAD.bit_length() - 1)
        ones = jnp.ones((rows, PAIR), BF16)
        onehot = jnp.concatenate([(row == index_ref[m]).astype(BF16) for m in range(count)], axis=1)

        def by_head(blocks):
            chosen = blocks[0]
            for k in range(1, len(blocks)):
                chosen = jnp.where(head == k, blocks[k], chosen)
            return chosen

        for m in range(count):
            given = pooled_ref[m : m + 1].astype(F32) * (1.0 / rows)
            lines = slice(m * cands, (m + 1) * cands)
            for k in range(3):
                loads[3 * m + k].wait()
            column = dot(share[m], ones, NN)
            column = jnp.concatenate([column, column], axis=1)
            for q in range(width // TILE):
                cols = slice(q * TILE, (q + 1) * TILE)
                key = dot(slant[m, cols], high[m, :, cols], NN) * (1.0 / math.sqrt(HEAD))
                starts = range(0, TILE, cands)
                kv[lines, cols] = by_head([key[at : at + cands] for at in starts])
                value = by_head([column[q * TILE + at : q * TILE + at + cands] for at in starts])
                kv[lines, width + q * TILE : width + (q + 1) * TILE] = value * given[:, cols]
        stores = []
        for k, part in enumerate(parts):
            kv_high, kv_low = high_low(kv[:, k * span : (k + 1) * span])
            part[...] = (dot(onehot, kv_high, NN) + dot(onehot, kv_low, NN)).astype(BF16)
            stores.append(pltpu.make_async_copy(part, outs[k], sems.at[3 * count + k]))
            stores[k].start()
        for store in stores:
            store.wait()


def table_call(flag, index, pooled, table_rows, after, shares, slants, highs, sections):
    rows, width = highs[0].shape
    count = len(highs)
    part = (table_rows, 2 * width // sections)
    return pl.pallas_call(
        table_kernel,
        out_shape=(pltpu.HBM(part, BF16),) * sections,
        in_specs=[SMEM, VMEM, VMEM, HBM] + [HBM] * (3 * count),
        out_specs=(HBM,) * sections,
        scratch_shapes=[pltpu.VMEM(part, BF16)] * sections
        + [
            pltpu.VMEM((count,) + shares[0].shape, BF16),
            pltpu.VMEM((count,) + slants[0].shape, BF16),
            pltpu.VMEM((count,) + highs[0].shape, BF16),
            pltpu.VMEM((count * index.shape[2], 2 * width), F32),
            pltpu.SemaphoreType.DMA((3 * count + sections,)),
        ],
        compiler_params=pltpu.CompilerParams(vmem_limit_bytes=18 * MIB),
        cost_estimate=LIGHT,
        name="table",
    )(flag, index, pooled, stay(after), *map(stay, shares), *map(stay, slants), *map(stay, highs))


def hop_kernel(m, with_grad, flag_ref, came_hbm, delta_in, weight, after_hbm, *rest):
    if with_grad:
        grad_hbm, delta_hbm, came, aux, grad, sems = rest
    else:
        delta_hbm, came, aux, sems = rest
    width = came.shape[1]

    @pl.when(flag_ref[0] == 1)
    def _():
        first = pltpu.make_async_copy(came_hbm, came, sems.at[0])
        second = pltpu.make_async_copy(delta_in.at[m], aux, sems.at[1])
        first.start()
        second.start()
        first.wait()
        second.wait()
        aux[...] = (came[...].astype(F32) * aux[...].astype(F32)).astype(BF16)
        stores = [pltpu.make_async_copy(aux, delta_hbm.at[m], sems.at[2])]
        stores[0].start()
        if with_grad:
            for n in range(width // TILE):
                part = slice(n * TILE, (n + 1) * TILE)
                grad[:, part] = (came[:, part].astype(F32) + dot(aux[...], weight[part, :], NT)).astype(BF16)
            stores.append(pltpu.make_async_copy(grad, grad_hbm, sems.at[3]))
            stores[-1].start()
        for store in stores:
            store.wait()


def hop_call(m, flag, came, delta, weight, after, with_grad):
    rows, width = came.shape
    scratch = [pltpu.VMEM((rows, width), BF16)] * (3 if with_grad else 2)
    scratch.append(pltpu.SemaphoreType.DMA((4,)))
    outs = (pltpu.HBM(delta.shape, BF16),)
    if with_grad:
        outs = (pltpu.HBM((rows, width), BF16),) + outs
    return pl.pallas_call(
        functools.partial(hop_kernel, m, with_grad),
        out_shape=outs,
        in_specs=[SMEM, HBM, HBM, VMEM if with_grad else HBM, HBM],
        out_specs=(HBM,) * len(outs),
        scratch_shapes=scratch,
        input_output_aliases={2: len(outs) - 1},
        compiler_params=pltpu.CompilerParams(vmem_limit_bytes=12 * MIB),
        cost_estimate=LIGHT,
        name="hop" if with_grad else "end",
    )(flag, came, stay(delta), weight if with_grad else stay(weight), stay(after))


def bit_orders(replicas):
    bits = list(range(replicas.bit_length() - 1))
    return [bits, bits[1::-1] + bits[2:]]


def block_order(bits):
    rest = bits[1:]
    order = []
    for i in range(1 << len(rest)):
        order.append(sum(((i >> (len(rest) - 1 - k)) & 1) << bit for k, bit in enumerate(rest)))
    return order


def turn_kernel(acts_hbm, after_hbm, out, token_ref, acts, sems):
    count, rows, width = acts.shape
    token_ref[...] = jnp.zeros_like(token_ref)
    loads = [pltpu.make_async_copy(acts_hbm.at[m], acts.at[m], sems.at[m]) for m in range(count)]
    for load in loads:
        load.start()
    for m in range(count):
        loads[m].wait()
        out[:, m * rows : (m + 1) * rows] = acts[m].T


def turn_call(acts, after):
    count, rows, width = acts.shape
    return pl.pallas_call(
        turn_kernel,
        out_shape=(jax.ShapeDtypeStruct((width, count * rows), BF16), pltpu.HBM((16, 128), BF16)),
        in_specs=[HBM, HBM],
        out_specs=(VMEM,) * 2,
        scratch_shapes=[pltpu.VMEM(acts.shape, BF16), pltpu.SemaphoreType.DMA((count,))],
        compiler_params=pltpu.CompilerParams(vmem_limit_bytes=14 * MIB),
        cost_estimate=LIGHT,
        name="turn",
    )(stay(acts), stay(after))


def picked_rows(turned, number, bits, which, size, columns):
    mine = (number >> bits[0]) & 1
    base = (mine if which else 1 - mine) << bits[0]
    return jnp.concatenate(
        [turned[pl.ds(pl.multiple_of((base + block) * size, size), size), columns] for block in block_order(bits)],
        axis=0,
    )


def early_kernel(replicas, number_ref, turned, delta_hbm, *refs):
    outs, (delta, sems) = refs[:4], refs[4:]
    micros, rows, width = delta.shape
    half = width // 2
    loads = [pltpu.make_async_copy(delta_hbm.at[m], delta.at[m], sems.at[m]) for m in range(micros)]
    for load in loads:
        load.start()
    for load in loads:
        load.wait()
    flat = delta.reshape(micros * rows, width)
    for c, bits in enumerate(bit_orders(replicas)):
        for which in range(2):
            left = picked_rows(turned, number_ref[0], bits, which, width // replicas, slice(0, micros * rows))
            for at in range(0, half, TILE):
                outs[2 * c + which][:, at : at + TILE] = dot(
                    left, flat[:, c * half + at : c * half + at + TILE], NN
                )


def early_call(number, turned, delta, replicas):
    micros, rows, width = delta.shape
    half = jax.ShapeDtypeStruct((width // 2, width // 2), F32)
    return pl.pallas_call(
        functools.partial(early_kernel, replicas),
        out_shape=(half,) * 4,
        in_specs=[SMEM, VMEM, HBM],
        out_specs=(VMEM,) * 4,
        scratch_shapes=[
            pltpu.VMEM((micros - 1, rows, width), BF16),
            pltpu.SemaphoreType.DMA((micros - 1,)),
        ],
        compiler_params=pltpu.CompilerParams(vmem_limit_bytes=18 * MIB),
        cost_estimate=LIGHT,
        name="early",
    )(number, turned, stay(delta))


def weight_kernel(
    replicas, which, flag_ref, number_ref, turned, delta_hbm, came, early_first, early_second, *refs
):
    outs, (delta, sem) = refs[:2], refs[2:]
    rows, width = delta.shape
    half = width // 2
    last = delta_hbm.shape[0] - 1
    load = pltpu.make_async_copy(delta_hbm.at[last], delta, sem.at[0])
    load.start()
    load.wait()

    @pl.when(flag_ref[0] == 1)
    def _():
        delta[...] = (came[...].astype(F32) * delta[...].astype(F32)).astype(BF16)

    for c, (bits, early) in enumerate(zip(bit_orders(replicas), (early_first, early_second))):
        columns = slice(last * rows, (last + 1) * rows)
        left = picked_rows(turned, number_ref[0], bits, which, width // replicas, columns)
        for at in range(0, half, TILE):
            product = dot(left, delta[:, c * half + at : c * half + at + TILE], NN)
            outs[c][:, at : at + TILE] = (early[:, at : at + TILE] + product).astype(outs[c].dtype)


def weight_call(which, flag, number, turned, delta, came, early, replicas):
    micros, rows, width = delta.shape
    half = (width // 2, width // 2)
    return pl.pallas_call(
        functools.partial(weight_kernel, replicas, which),
        out_shape=(jax.ShapeDtypeStruct(half, F32) if which else pltpu.HBM(half, BF16),) * 2,
        in_specs=[SMEM, SMEM, VMEM, HBM, VMEM, VMEM, VMEM],
        out_specs=(VMEM,) * 2,
        scratch_shapes=[pltpu.VMEM((rows, width), BF16), pltpu.SemaphoreType.DMA((1,))],
        compiler_params=pltpu.CompilerParams(vmem_limit_bytes=14 * MIB),
        cost_estimate=LIGHT,
        name="weight",
    )(flag, number, turned, stay(delta), came, *early)


def own_half(keep, got, bit):
    mine = (lax.axis_index("dp") >> bit) & 1

    def pick(which):
        return lax.dynamic_index_in_dim(keep, which, 0, keepdims=False) + lax.dynamic_index_in_dim(
            got, which, 0, keepdims=False
        ).astype(F32)

    return pick(1 - mine).astype(BF16), pick(mine)


def scatter_sums(sends, keeps, table, orders, pairs_of):
    steps = len(orders[0])
    sends, keeps = list(sends), list(keeps)
    for n in range(steps):
        gots = [lax.ppermute(send, "dp", pairs_of(bits[n])) for send, bits in zip(sends, orders)]
        for c, bits in enumerate(orders):
            if n + 1 < steps:
                lead = (2, keeps[c].shape[0] // 2, keeps[c].shape[1])
                sends[c], keeps[c] = own_half(keeps[c].reshape(lead), gots[c].reshape(lead), bits[n + 1])
        if n == 0:
            table, _ = lax.optimization_barrier((table, tuple(sends)))
    blocks = lax.all_to_all(table.reshape(1 << steps, -1, table.shape[1]), "dp", 0, 0)
    sums = [keep + got.astype(F32) for keep, got in zip(keeps, gots)]
    return jnp.concatenate(sums, axis=1), jnp.sum(blocks.astype(F32), axis=0)


def body(activations, section_weights, cand_table, cand_index, cand_count, pooled_cotangent):
    sections = lax.axis_size("section")
    replicas = lax.axis_size("dp")
    position = lax.axis_index("section")
    replica = lax.axis_index("dp")
    last = sections - 1
    final_flag = position == last
    acts = activations[0]
    weight = section_weights[0]
    micro_count, row_count, model_width = acts.shape

    def flag(truth):
        return truth.astype(jnp.int32).reshape(1)

    number = replica.reshape(1)
    count = cand_count.reshape(1, micro_count)
    pooled = pooled_cotangent.reshape(micro_count, model_width)
    final = flag(final_flag)
    grads, shares, slants, highs = [], [], [], []
    delta = acts
    for m in range(micro_count):
        grad, delta, share, slant, high = first_call(
            m, final, count, acts, weight, cand_table, cand_index, pooled, delta
        )
        grads.append(grad)
        shares.append(share)
        slants.append(slant)
        highs.append(high)

    def pairs(bit):
        return [(i, i ^ (1 << bit)) for i in range(replicas)]

    for hop in range(last):
        source = last - hop
        received = [lax.ppermute(g, "section", [(source, source - 1)]) for g in grads]
        active = flag(position == source - 1)
        for m in range(micro_count):
            if hop + 1 < last:
                after = token if hop == 1 and m == 0 else acts
                grads[m], delta = hop_call(m, active, received[m], delta, weight, after, True)
            elif m + 1 < micro_count:
                (delta,) = hop_call(m, active, received[m], delta, weight, acts, False)
        if hop == 0:
            parts = table_call(
                final, cand_index, pooled, cand_table.shape[0], grads[-1], shares, slants, highs, sections
            )
            turned, token = turn_call(acts, grads[-1])

    spread = [lax.ppermute(parts[s], "section", [(last, s)]) for s in range(last)]
    table_part = jnp.where(final_flag, parts[last], sum(spread))

    orders = bit_orders(replicas)
    early = early_call(number, turned, delta, replicas)
    sends = weight_call(0, active, number, turned, delta, received[-1], early[::2], replicas)
    keeps = weight_call(1, active, number, turned, delta, received[-1], early[1::2], replicas)
    sums, table_sum = scatter_sums(sends, keeps, table_part, orders, pairs)
    return sums[None], table_sum


def solution(mesh):
    in_specs = (
        P("section", None, "dp", None),
        P("section", None, None),
        P(),
        P(None, "dp", None),
        P(None, "dp"),
        P(None, "dp", None),
    )
    out_specs = (P("section", "dp", None), P("dp", "section"))
    return jax.shard_map(body, mesh=mesh, in_specs=in_specs, out_specs=out_specs, check_vma=False)
```

```python
import functools
import math

import jax
import jax.numpy as jnp
from jax import lax
from jax.experimental import pallas as pl
from jax.experimental.pallas import tpu as pltpu
from jax.sharding import PartitionSpec as P

HEAD = 64
PAIR = 2 * HEAD
TILE = 256
MIB = 1024 * 1024
HBM = pl.BlockSpec(memory_space=pltpu.HBM)
VMEM = pl.BlockSpec(memory_space=pltpu.VMEM)
SMEM = pl.BlockSpec(memory_space=pltpu.SMEM)
BF16 = jnp.bfloat16
F32 = jnp.float32
LIGHT = pl.CostEstimate(flops=1024, bytes_accessed=1024, transcendentals=0)

NN = (((1,), (0,)), ((), ()))
NT = (((1,), (1,)), ((), ()))
TN = (((0,), (0,)), ((), ()))


def dot(left, right, dims):
    return lax.dot_general(left, right, dims, preferred_element_type=F32)


def gelu_parts(hidden):
    root = math.sqrt(2.0 / math.pi)
    square = hidden * hidden
    bent = jnp.tanh(root * hidden * (1.0 + 0.044715 * square))
    share = 0.5 + 0.5 * bent
    slope = share + (0.5 * root) * hidden * (1.0 - bent * bent) * (1.0 + (3 * 0.044715) * square)
    return hidden * share, slope


def high_low(values):
    high = values.astype(BF16)
    return high, (values - high.astype(F32)).astype(BF16)


def stay(array):
    return pltpu.with_memory_space_constraint(array, pltpu.HBM)


def own_heads(width):
    shift = HEAD.bit_length() - 1
    row = lax.broadcasted_iota(jnp.int32, (PAIR, width), 0) >> shift
    return row == ((lax.broadcasted_iota(jnp.int32, (PAIR, width), 1) >> shift) & 1)


def first_kernel(
    m, flag_ref, count_hbm, acts_in, weight_in, table_in, index_hbm, pooled_hbm, delta_in,
    grad_hbm, delta_hbm, share_hbm, slant_hbm, high_hbm,
    count_ref, acts_buf, weight_buf, table_buf, index_ref, pooled_ref, grad, aux, share_ref, slant_ref, high_ref, sems,
):
    micros, rows, width = acts_in.shape
    table_rows = table_in.shape[0]
    pairs = width // PAIR
    tiles = width // TILE
    tile = [slice(q * TILE, (q + 1) * TILE) for q in range(tiles)]
    pair = [slice(j * PAIR, (j + 1) * PAIR) for j in range(pairs)]

    def copy(source, target, at):
        started = pltpu.make_async_copy(source, target, sems.at[at])
        started.start()
        return started

    if m == 0:
        acts_ref, weight, table = acts_buf, weight_buf, table_buf

        @pl.when(flag_ref[0] == 0)
        def _():
            load_weight = copy(weight_in, weight, 0)
            loads = [copy(acts_in.at[k], acts_ref.at[k], 1 + k) for k in range(micros)]
            load_weight.wait()
            stores = []
            for k in range(micros):
                loads[k].wait()
                for cols in tile:
                    hidden = dot(acts_ref[k], weight[:, cols], NN)
                    aux[k, :, cols] = gelu_parts(hidden)[1].astype(BF16)
                stores.append(copy(aux.at[k], delta_hbm.at[k], 1 + micros + k))
            for store in stores:
                store.wait()

    else:
        acts_ref, weight, table = acts_in, weight_in, table_in

    @pl.when(flag_ref[0] == 1)
    def _():
        loads = [copy(index_hbm, index_ref, 0), copy(pooled_hbm, pooled_ref, 1), copy(count_hbm, count_ref, 2)]
        if m == 0:
            loads.append(copy(table_in, table, 3))
            load_weight = copy(weight_in, weight, 4)
            load_acts = copy(acts_in.at[0], acts_ref.at[0], 5)
            load_acts.wait()
            load_weight.wait()
        acts = acts_ref.at[m]
        slopes, lows = [], []
        for cols in tile:
            hidden = dot(acts[...], weight[:, cols], NN)
            bent, slope = gelu_parts(hidden)
            high, low = high_low(acts[:, cols].astype(F32) + bent)
            high_ref[:, cols] = high
            slopes.append(slope)
            lows.append(low)
        store_high = copy(high_ref, high_hbm, 6)
        for load in loads:
            load.wait()
        index = index_ref[m]
        index = jnp.concatenate([index, index], axis=1)
        onehot = (lax.broadcasted_iota(jnp.int32, (table_rows, PAIR), 0) == index).astype(BF16)
        gathered = dot(onehot, table[...], TN)
        own = own_heads(width)
        keys = jnp.where(own, gathered[:, :width] * (1.0 / math.sqrt(HEAD)), 0.0).astype(BF16)
        values = jnp.where(own, gathered[:, width:], 0.0).astype(BF16)
        allowed = lax.broadcasted_iota(jnp.int32, (2, HEAD, rows), 1) < count_ref[0, m]
        given_row = pooled_ref[m : m + 1].astype(F32) * (1.0 / rows)
        given = jnp.broadcast_to(given_row, (rows, width)).astype(BF16)
        scores = []
        for j, here in enumerate(pair):
            part = slice(j * PAIR % TILE, j * PAIR % TILE + PAIR)
            scores.append(
                dot(
                    jnp.concatenate([keys[:, here], keys[:, here]], axis=1),
                    jnp.concatenate([high_ref[:, here], lows[j * PAIR // TILE][:, part]], axis=1),
                    NT,
                )
            )
        slants = []
        for j, here in enumerate(pair):
            share, slant = soften(scores[j], dot(values[:, here], given[:, here], NT), allowed)
            share_ref[here] = share
            slant_ref[here] = slant
            slants.append(slant)
        store_share = copy(share_ref, share_hbm, 7)
        store_slant = copy(slant_ref, slant_hbm, 10)
        totals = []
        for j, here in enumerate(pair):
            part = slice(j * PAIR % TILE, j * PAIR % TILE + PAIR)
            total = given_row[:, here] + dot(slants[j], keys[:, here], TN)
            totals.append(total)
            aux[0, :, here] = (total * slopes[j * PAIR // TILE][:, part]).astype(BF16)
        store_aux = copy(aux.at[0], delta_hbm.at[m], 8)
        for q, cols in enumerate(tile):
            total = jnp.concatenate(totals[q * TILE // PAIR : (q + 1) * TILE // PAIR], axis=1)
            grad[:, cols] = (total + dot(aux[0], weight[cols, :], NT)).astype(BF16)
        store_grad = copy(grad, grad_hbm, 9)
        store_high.wait()
        store_share.wait()
        store_slant.wait()
        store_aux.wait()
        store_grad.wait()


def lean(share, worth):
    worth = worth.reshape(share.shape)
    centre = jnp.sum(share * worth, axis=1, keepdims=True)
    return (share * (worth - centre)).reshape(worth.shape[0] * worth.shape[1], -1).astype(BF16)


def soften(score, worth, allowed):
    score = jnp.where(allowed, score.reshape(allowed.shape), -1e30)
    raised = jnp.exp(score - jnp.max(score, axis=1, keepdims=True))
    share = raised * (1.0 / jnp.sum(raised, axis=1, keepdims=True))
    return share.reshape(worth.shape).astype(BF16), lean(share, worth)


def first_call(m, flag, count, acts, weight, table, index, pooled, delta):
    micros, rows, width = acts.shape
    turned = (width // HEAD * index.shape[2], rows)
    block = pltpu.HBM((rows, width), BF16)
    big = HBM if m == 0 else VMEM
    small = pltpu.VMEM((8, 128), BF16)
    return pl.pallas_call(
        functools.partial(first_kernel, m),
        out_shape=(block, pltpu.HBM(acts.shape, BF16), pltpu.HBM(turned, BF16), pltpu.HBM(turned, BF16), block),
        in_specs=[SMEM, HBM, big, big, big, HBM, HBM, HBM],
        out_specs=(HBM,) * 5,
        scratch_shapes=[
            pltpu.SMEM(count.shape, jnp.int32),
            pltpu.VMEM(acts.shape, BF16) if m == 0 else small,
            pltpu.VMEM(weight.shape, BF16) if m == 0 else small,
            pltpu.VMEM(table.shape, BF16) if m == 0 else small,
            pltpu.VMEM(index.shape, jnp.int32),
            pltpu.VMEM(pooled.shape, BF16),
            pltpu.VMEM((rows, width), BF16),
            pltpu.VMEM((micros if m == 0 else 1, rows, width), BF16),
            pltpu.VMEM(turned, BF16),
            pltpu.VMEM(turned, BF16),
            pltpu.VMEM((rows, width), BF16),
            pltpu.SemaphoreType.DMA((max(11, 1 + 2 * micros),)),
        ],
        input_output_aliases={} if m == 0 else {7: 1},
        compiler_params=pltpu.CompilerParams(vmem_limit_bytes=18 * MIB),
        cost_estimate=LIGHT,
        name="first",
    )(
        flag,
        stay(count),
        *(stay(array) if m == 0 else array for array in (acts, weight, table)),
        stay(index),
        stay(pooled),
        stay(delta),
    )


def table_kernel(flag_ref, index_ref, pooled_ref, after_hbm, *refs):
    share, slant, high, kv, sems = refs[-5:]
    count, rows, width = high.shape
    sections = (len(refs) - 5 - 3 * count) // 2
    sources, outs, parts = refs[: 3 * count], refs[3 * count : -5 - sections], refs[-5 - sections : -5]
    table_rows, span = parts[0].shape
    cands = index_ref.shape[2]

    @pl.when(flag_ref[0] == 1)
    def _():
        loads = []
        for m in range(count):
            for k, target in enumerate((share, slant, high)):
                loads.append(pltpu.make_async_copy(sources[k * count + m], target.at[m], sems.at[3 * m + k]))
        for load in loads:
            load.start()
        row = lax.broadcasted_iota(jnp.int32, (table_rows, cands), 0)
        head = lax.broadcasted_iota(jnp.int32, (cands, TILE), 1) >> (HEAD.bit_length() - 1)
        ones = jnp.ones((rows, PAIR), BF16)
        onehot = jnp.concatenate([(row == index_ref[m]).astype(BF16) for m in range(count)], axis=1)

        def by_head(blocks):
            chosen = blocks[0]
            for k in range(1, len(blocks)):
                chosen = jnp.where(head == k, blocks[k], chosen)
            return chosen

        for m in range(count):
            given = pooled_ref[m : m + 1].astype(F32) * (1.0 / rows)
            lines = slice(m * cands, (m + 1) * cands)
            for k in range(3):
                loads[3 * m + k].wait()
            column = dot(share[m], ones, NN)
            column = jnp.concatenate([column, column], axis=1)
            for q in range(width // TILE):
                cols = slice(q * TILE, (q + 1) * TILE)
                key = dot(slant[m, cols], high[m, :, cols], NN) * (1.0 / math.sqrt(HEAD))
                starts = range(0, TILE, cands)
                kv[lines, cols] = by_head([key[at : at + cands] for at in starts])
                value = by_head([column[q * TILE + at : q * TILE + at + cands] for at in starts])
                kv[lines, width + q * TILE : width + (q + 1) * TILE] = value * given[:, cols]
        stores = []
        for k, part in enumerate(parts):
            kv_high, kv_low = high_low(kv[:, k * span : (k + 1) * span])
            part[...] = (dot(onehot, kv_high, NN) + dot(onehot, kv_low, NN)).astype(BF16)
            stores.append(pltpu.make_async_copy(part, outs[k], sems.at[3 * count + k]))
            stores[k].start()
        for store in stores:
            store.wait()


def table_call(flag, index, pooled, table_rows, after, shares, slants, highs, sections):
    rows, width = highs[0].shape
    count = len(highs)
    part = (table_rows, 2 * width // sections)
    return pl.pallas_call(
        table_kernel,
        out_shape=(pltpu.HBM(part, BF16),) * sections,
        in_specs=[SMEM, VMEM, VMEM, HBM] + [HBM] * (3 * count),
        out_specs=(HBM,) * sections,
        scratch_shapes=[pltpu.VMEM(part, BF16)] * sections
        + [
            pltpu.VMEM((count,) + shares[0].shape, BF16),
            pltpu.VMEM((count,) + slants[0].shape, BF16),
            pltpu.VMEM((count,) + highs[0].shape, BF16),
            pltpu.VMEM((count * index.shape[2], 2 * width), F32),
            pltpu.SemaphoreType.DMA((3 * count + sections,)),
        ],
        compiler_params=pltpu.CompilerParams(vmem_limit_bytes=18 * MIB),
        cost_estimate=LIGHT,
        name="table",
    )(flag, index, pooled, stay(after), *map(stay, shares), *map(stay, slants), *map(stay, highs))


def hop_kernel(m, with_grad, flag_ref, came_hbm, delta_in, weight, after_hbm, *rest):
    if with_grad:
        grad_hbm, delta_hbm, came, aux, grad, sems = rest
    else:
        delta_hbm, came, aux, sems = rest
    width = came.shape[1]

    @pl.when(flag_ref[0] == 1)
    def _():
        first = pltpu.make_async_copy(came_hbm, came, sems.at[0])
        second = pltpu.make_async_copy(delta_in.at[m], aux, sems.at[1])
        first.start()
        second.start()
        first.wait()
        second.wait()
        aux[...] = (came[...].astype(F32) * aux[...].astype(F32)).astype(BF16)
        stores = [pltpu.make_async_copy(aux, delta_hbm.at[m], sems.at[2])]
        stores[0].start()
        if with_grad:
            for n in range(width // TILE):
                part = slice(n * TILE, (n + 1) * TILE)
                grad[:, part] = (came[:, part].astype(F32) + dot(aux[...], weight[part, :], NT)).astype(BF16)
            stores.append(pltpu.make_async_copy(grad, grad_hbm, sems.at[3]))
            stores[-1].start()
        for store in stores:
            store.wait()


def hop_call(m, flag, came, delta, weight, after, with_grad):
    rows, width = came.shape
    scratch = [pltpu.VMEM((rows, width), BF16)] * (3 if with_grad else 2)
    scratch.append(pltpu.SemaphoreType.DMA((4,)))
    outs = (pltpu.HBM(delta.shape, BF16),)
    if with_grad:
        outs = (pltpu.HBM((rows, width), BF16),) + outs
    return pl.pallas_call(
        functools.partial(hop_kernel, m, with_grad),
        out_shape=outs,
        in_specs=[SMEM, HBM, HBM, VMEM if with_grad else HBM, HBM],
        out_specs=(HBM,) * len(outs),
        scratch_shapes=scratch,
        input_output_aliases={2: len(outs) - 1},
        compiler_params=pltpu.CompilerParams(vmem_limit_bytes=12 * MIB),
        cost_estimate=LIGHT,
        name="hop" if with_grad else "end",
    )(flag, came, stay(delta), weight if with_grad else stay(weight), stay(after))


def bit_orders(replicas):
    bits = list(range(replicas.bit_length() - 1))
    return [bits, bits[1::-1] + bits[2:]]


def block_order(bits):
    rest = bits[1:]
    order = []
    for i in range(1 << len(rest)):
        order.append(sum(((i >> (len(rest) - 1 - k)) & 1) << bit for k, bit in enumerate(rest)))
    return order


def turn_kernel(acts_hbm, after_hbm, out, token_ref, acts, sems):
    count, rows, width = acts.shape
    token_ref[...] = jnp.zeros_like(token_ref)
    loads = [pltpu.make_async_copy(acts_hbm.at[m], acts.at[m], sems.at[m]) for m in range(count)]
    for load in loads:
        load.start()
    for m in range(count):
        loads[m].wait()
        out[:, m * rows : (m + 1) * rows] = acts[m].T


def turn_call(acts, after):
    count, rows, width = acts.shape
    return pl.pallas_call(
        turn_kernel,
        out_shape=(jax.ShapeDtypeStruct((width, count * rows), BF16), pltpu.HBM((16, 128), BF16)),
        in_specs=[HBM, HBM],
        out_specs=(VMEM,) * 2,
        scratch_shapes=[pltpu.VMEM(acts.shape, BF16), pltpu.SemaphoreType.DMA((count,))],
        compiler_params=pltpu.CompilerParams(vmem_limit_bytes=14 * MIB),
        cost_estimate=LIGHT,
        name="turn",
    )(stay(acts), stay(after))


def picked_rows(turned, number, bits, which, size, columns):
    mine = (number >> bits[0]) & 1
    base = (mine if which else 1 - mine) << bits[0]
    return jnp.concatenate(
        [turned[pl.ds(pl.multiple_of((base + block) * size, size), size), columns] for block in block_order(bits)],
        axis=0,
    )


def early_kernel(replicas, number_ref, turned, delta_hbm, *refs):
    outs, (delta, sems) = refs[:2], refs[2:]
    micros, rows, width = delta.shape
    half = width // 2
    loads = [pltpu.make_async_copy(delta_hbm.at[m], delta.at[m], sems.at[m]) for m in range(micros)]
    for load in loads:
        load.start()
    for load in loads:
        load.wait()
    flat = delta.reshape(micros * rows, width)
    for c, bits in enumerate(bit_orders(replicas)):
        left = picked_rows(turned, number_ref[0], bits, 0, width // replicas, slice(0, micros * rows))
        for at in range(0, half, TILE):
            outs[c][:, at : at + TILE] = dot(left, flat[:, c * half + at : c * half + at + TILE], NN)


def early_call(number, turned, delta, replicas):
    micros, rows, width = delta.shape
    half = jax.ShapeDtypeStruct((width // 2, width // 2), F32)
    return pl.pallas_call(
        functools.partial(early_kernel, replicas),
        out_shape=(half,) * 2,
        in_specs=[SMEM, VMEM, HBM],
        out_specs=(VMEM,) * 2,
        scratch_shapes=[
            pltpu.VMEM((micros - 1, rows, width), BF16),
            pltpu.SemaphoreType.DMA((micros - 1,)),
        ],
        compiler_params=pltpu.CompilerParams(vmem_limit_bytes=18 * MIB),
        cost_estimate=LIGHT,
        name="early",
    )(number, turned, stay(delta))


def weight_kernel(replicas, which, flag_ref, number_ref, turned, delta_hbm, came, *refs):
    early, outs, (delta, sems) = refs[:-4], refs[-4:-2], refs[-2:]
    micros, rows, width = delta_hbm.shape
    half = width // 2
    begin = micros - 1 if early else 0
    loads = [
        pltpu.make_async_copy(delta_hbm.at[m], delta.at[pl.ds((m - begin) * rows, rows)], sems.at[m - begin])
        for m in range(begin, micros)
    ]
    for load in loads:
        load.start()
    for load in loads:
        load.wait()

    @pl.when(flag_ref[0] == 1)
    def _():
        tail = pl.ds((micros - 1 - begin) * rows, rows)
        delta[tail] = (came[...].astype(F32) * delta[tail].astype(F32)).astype(BF16)

    for c, bits in enumerate(bit_orders(replicas)):
        columns = slice(begin * rows, micros * rows)
        left = picked_rows(turned, number_ref[0], bits, which, width // replicas, columns)
        for at in range(0, half, TILE):
            product = dot(left, delta[:, c * half + at : c * half + at + TILE], NN)
            if early:
                product = early[c][:, at : at + TILE] + product
            outs[c][:, at : at + TILE] = product.astype(outs[c].dtype)


def weight_call(which, flag, number, turned, delta, came, early, replicas):
    micros, rows, width = delta.shape
    half = (width // 2, width // 2)
    taken = 1 if early else micros
    return pl.pallas_call(
        functools.partial(weight_kernel, replicas, which),
        out_shape=(jax.ShapeDtypeStruct(half, F32) if which else pltpu.HBM(half, BF16),) * 2,
        in_specs=[SMEM, SMEM, VMEM, HBM] + [VMEM] * (1 + len(early)),
        out_specs=(VMEM,) * 2,
        scratch_shapes=[pltpu.VMEM((taken * rows, width), BF16), pltpu.SemaphoreType.DMA((taken,))],
        compiler_params=pltpu.CompilerParams(vmem_limit_bytes=18 * MIB),
        cost_estimate=LIGHT,
        name="weight",
    )(flag, number, turned, stay(delta), came, *early)


def own_half(keep, got, bit):
    mine = (lax.axis_index("dp") >> bit) & 1

    def pick(which):
        return lax.dynamic_index_in_dim(keep, which, 0, keepdims=False) + lax.dynamic_index_in_dim(
            got, which, 0, keepdims=False
        ).astype(F32)

    return pick(1 - mine).astype(BF16), pick(mine)


def scatter_sums(sends, keeps, table, orders, pairs_of):
    steps = len(orders[0])
    sends, keeps = list(sends), list(keeps)
    for n in range(steps):
        gots = [lax.ppermute(send, "dp", pairs_of(bits[n])) for send, bits in zip(sends, orders)]
        for c, bits in enumerate(orders):
            if n + 1 < steps:
                lead = (2, keeps[c].shape[0] // 2, keeps[c].shape[1])
                sends[c], keeps[c] = own_half(keeps[c].reshape(lead), gots[c].reshape(lead), bits[n + 1])
        if n == 0:
            table, _ = lax.optimization_barrier((table, tuple(sends)))
    blocks = lax.all_to_all(table.reshape(1 << steps, -1, table.shape[1]), "dp", 0, 0)
    sums = [keep + got.astype(F32) for keep, got in zip(keeps, gots)]
    return jnp.concatenate(sums, axis=1), jnp.sum(blocks.astype(F32), axis=0)


def body(activations, section_weights, cand_table, cand_index, cand_count, pooled_cotangent):
    sections = lax.axis_size("section")
    replicas = lax.axis_size("dp")
    position = lax.axis_index("section")
    replica = lax.axis_index("dp")
    last = sections - 1
    final_flag = position == last
    acts = activations[0]
    weight = section_weights[0]
    micro_count, row_count, model_width = acts.shape

    def flag(truth):
        return truth.astype(jnp.int32).reshape(1)

    number = replica.reshape(1)
    count = cand_count.reshape(1, micro_count)
    pooled = pooled_cotangent.reshape(micro_count, model_width)
    final = flag(final_flag)
    grads, shares, slants, highs = [], [], [], []
    delta = acts
    for m in range(micro_count):
        grad, delta, share, slant, high = first_call(
            m, final, count, acts, weight, cand_table, cand_index, pooled, delta
        )
        grads.append(grad)
        shares.append(share)
        slants.append(slant)
        highs.append(high)

    def pairs(bit):
        return [(i, i ^ (1 << bit)) for i in range(replicas)]

    for hop in range(last):
        source = last - hop
        received = [lax.ppermute(g, "section", [(source, source - 1)]) for g in grads]
        active = flag(position == source - 1)
        for m in range(micro_count):
            if hop + 1 < last:
                after = token if hop == 1 and m == 0 else acts
                grads[m], delta = hop_call(m, active, received[m], delta, weight, after, True)
            elif m + 1 < micro_count:
                (delta,) = hop_call(m, active, received[m], delta, weight, acts, False)
        if hop == 0:
            parts = table_call(
                final, cand_index, pooled, cand_table.shape[0], grads[-1], shares, slants, highs, sections
            )
            turned, token = turn_call(acts, grads[-1])

    spread = [lax.ppermute(parts[s], "section", [(last, s)]) for s in range(last)]
    table_part = jnp.where(final_flag, parts[last], sum(spread))

    orders = bit_orders(replicas)
    early = early_call(number, turned, delta, replicas)
    sends = weight_call(0, active, number, turned, delta, received[-1], early, replicas)
    keeps = weight_call(1, active, number, turned, delta, received[-1], (), replicas)
    sums, table_sum = scatter_sums(sends, keeps, table_part, orders, pairs)
    return sums[None], table_sum


def solution(mesh):
    in_specs = (
        P("section", None, "dp", None),
        P("section", None, None),
        P(),
        P(None, "dp", None),
        P(None, "dp"),
        P(None, "dp", None),
    )
    out_specs = (P("section", "dp", None), P("dp", "section"))
    return jax.shard_map(body, mesh=mesh, in_specs=in_specs, out_specs=out_specs, check_vma=False)
```

```python
import functools
import math

import jax
import jax.numpy as jnp
from jax import lax
from jax.experimental import pallas as pl
from jax.experimental.pallas import tpu as pltpu
from jax.sharding import PartitionSpec as P

HEAD = 64
PAIR = 2 * HEAD
TILE = 256
MIB = 1024 * 1024
HBM = pl.BlockSpec(memory_space=pltpu.HBM)
VMEM = pl.BlockSpec(memory_space=pltpu.VMEM)
SMEM = pl.BlockSpec(memory_space=pltpu.SMEM)
BF16 = jnp.bfloat16
F32 = jnp.float32
LIGHT = pl.CostEstimate(flops=1024, bytes_accessed=1024, transcendentals=0)

NN = (((1,), (0,)), ((), ()))
NT = (((1,), (1,)), ((), ()))
TN = (((0,), (0,)), ((), ()))


def dot(left, right, dims):
    return lax.dot_general(left, right, dims, preferred_element_type=F32)


def gelu_parts(hidden):
    root = math.sqrt(2.0 / math.pi)
    square = hidden * hidden
    bent = jnp.tanh(root * hidden * (1.0 + 0.044715 * square))
    share = 0.5 + 0.5 * bent
    slope = share + (0.5 * root) * hidden * (1.0 - bent * bent) * (1.0 + (3 * 0.044715) * square)
    return hidden * share, slope


def high_low(values):
    high = values.astype(BF16)
    return high, (values - high.astype(F32)).astype(BF16)


def stay(array):
    return pltpu.with_memory_space_constraint(array, pltpu.HBM)


def own_heads(width):
    shift = HEAD.bit_length() - 1
    row = lax.broadcasted_iota(jnp.int32, (PAIR, width), 0) >> shift
    return row == ((lax.broadcasted_iota(jnp.int32, (PAIR, width), 1) >> shift) & 1)


def first_kernel(
    m, flag_ref, count_hbm, acts_in, weight_in, table_in, index_hbm, pooled_hbm, delta_in,
    grad_hbm, delta_hbm, share_hbm, slant_hbm, high_hbm,
    count_ref, acts_buf, weight_buf, table_buf, index_ref, pooled_ref, grad, aux, share_ref, slant_ref, high_ref, sems,
):
    micros, rows, width = acts_in.shape
    table_rows = table_in.shape[0]
    pairs = width // PAIR
    tiles = width // TILE
    tile = [slice(q * TILE, (q + 1) * TILE) for q in range(tiles)]
    pair = [slice(j * PAIR, (j + 1) * PAIR) for j in range(pairs)]

    def copy(source, target, at):
        started = pltpu.make_async_copy(source, target, sems.at[at])
        started.start()
        return started

    if m == 0:
        acts_ref, weight, table = acts_buf, weight_buf, table_buf

        @pl.when(flag_ref[0] == 0)
        def _():
            load_weight = copy(weight_in, weight, 0)
            loads = [copy(acts_in.at[k], acts_ref.at[k], 1 + k) for k in range(micros)]
            load_weight.wait()
            stores = []
            for k in range(micros):
                loads[k].wait()
                for cols in tile:
                    hidden = dot(acts_ref[k], weight[:, cols], NN)
                    aux[k, :, cols] = gelu_parts(hidden)[1].astype(BF16)
                stores.append(copy(aux.at[k], delta_hbm.at[k], 1 + micros + k))
            for store in stores:
                store.wait()

    else:
        acts_ref, weight, table = acts_in, weight_in, table_in

    @pl.when(flag_ref[0] == 1)
    def _():
        loads = [copy(index_hbm, index_ref, 0), copy(pooled_hbm, pooled_ref, 1), copy(count_hbm, count_ref, 2)]
        if m == 0:
            loads.append(copy(table_in, table, 3))
            load_weight = copy(weight_in, weight, 4)
            load_acts = copy(acts_in.at[0], acts_ref.at[0], 5)
            load_acts.wait()
            load_weight.wait()
        acts = acts_ref.at[m]
        slopes, lows = [], []
        for cols in tile:
            hidden = dot(acts[...], weight[:, cols], NN)
            bent, slope = gelu_parts(hidden)
            high, low = high_low(acts[:, cols].astype(F32) + bent)
            high_ref[:, cols] = high
            slopes.append(slope)
            lows.append(low)
        store_high = copy(high_ref, high_hbm, 6)
        for load in loads:
            load.wait()
        index = index_ref[m]
        index = jnp.concatenate([index, index], axis=1)
        onehot = (lax.broadcasted_iota(jnp.int32, (table_rows, PAIR), 0) == index).astype(BF16)
        gathered = dot(onehot, table[...], TN)
        own = own_heads(width)
        keys = jnp.where(own, gathered[:, :width] * (1.0 / math.sqrt(HEAD)), 0.0).astype(BF16)
        values = jnp.where(own, gathered[:, width:], 0.0).astype(BF16)
        allowed = lax.broadcasted_iota(jnp.int32, (2, HEAD, rows), 1) < count_ref[0, m]
        given_row = pooled_ref[m : m + 1].astype(F32) * (1.0 / rows)
        given = jnp.broadcast_to(given_row, (rows, width)).astype(BF16)
        scores = []
        for j, here in enumerate(pair):
            part = slice(j * PAIR % TILE, j * PAIR % TILE + PAIR)
            scores.append(
                dot(
                    jnp.concatenate([keys[:, here], keys[:, here]], axis=1),
                    jnp.concatenate([high_ref[:, here], lows[j * PAIR // TILE][:, part]], axis=1),
                    NT,
                )
            )
        slants = []
        for j, here in enumerate(pair):
            share, slant = soften(scores[j], dot(values[:, here], given[:, here], NT), allowed)
            share_ref[here] = share
            slant_ref[here] = slant
            slants.append(slant)
        store_share = copy(share_ref, share_hbm, 7)
        store_slant = copy(slant_ref, slant_hbm, 10)
        totals = []
        for j, here in enumerate(pair):
            part = slice(j * PAIR % TILE, j * PAIR % TILE + PAIR)
            total = given_row[:, here] + dot(slants[j], keys[:, here], TN)
            totals.append(total)
            aux[0, :, here] = (total * slopes[j * PAIR // TILE][:, part]).astype(BF16)
        store_aux = copy(aux.at[0], delta_hbm.at[m], 8)
        for q, cols in enumerate(tile):
            total = jnp.concatenate(totals[q * TILE // PAIR : (q + 1) * TILE // PAIR], axis=1)
            grad[:, cols] = (total + dot(aux[0], weight[cols, :], NT)).astype(BF16)
        store_grad = copy(grad, grad_hbm, 9)
        store_high.wait()
        store_share.wait()
        store_slant.wait()
        store_aux.wait()
        store_grad.wait()


def lean(share, worth):
    worth = worth.reshape(share.shape)
    centre = jnp.sum(share * worth, axis=1, keepdims=True)
    return (share * (worth - centre)).reshape(worth.shape[0] * worth.shape[1], -1).astype(BF16)


def soften(score, worth, allowed):
    score = jnp.where(allowed, score.reshape(allowed.shape), -1e30)
    raised = jnp.exp(score - jnp.max(score, axis=1, keepdims=True))
    share = raised * (1.0 / jnp.sum(raised, axis=1, keepdims=True))
    return share.reshape(worth.shape).astype(BF16), lean(share, worth)


def first_call(m, flag, count, acts, weight, table, index, pooled, delta):
    micros, rows, width = acts.shape
    turned = (width // HEAD * index.shape[2], rows)
    block = pltpu.HBM((rows, width), BF16)
    big = HBM if m == 0 else VMEM
    small = pltpu.VMEM((8, 128), BF16)
    return pl.pallas_call(
        functools.partial(first_kernel, m),
        out_shape=(block, pltpu.HBM(acts.shape, BF16), pltpu.HBM(turned, BF16), pltpu.HBM(turned, BF16), block),
        in_specs=[SMEM, HBM, big, big, big, HBM, HBM, HBM],
        out_specs=(HBM,) * 5,
        scratch_shapes=[
            pltpu.SMEM(count.shape, jnp.int32),
            pltpu.VMEM(acts.shape, BF16) if m == 0 else small,
            pltpu.VMEM(weight.shape, BF16) if m == 0 else small,
            pltpu.VMEM(table.shape, BF16) if m == 0 else small,
            pltpu.VMEM(index.shape, jnp.int32),
            pltpu.VMEM(pooled.shape, BF16),
            pltpu.VMEM((rows, width), BF16),
            pltpu.VMEM((micros if m == 0 else 1, rows, width), BF16),
            pltpu.VMEM(turned, BF16),
            pltpu.VMEM(turned, BF16),
            pltpu.VMEM((rows, width), BF16),
            pltpu.SemaphoreType.DMA((max(11, 1 + 2 * micros),)),
        ],
        input_output_aliases={} if m == 0 else {7: 1},
        compiler_params=pltpu.CompilerParams(vmem_limit_bytes=18 * MIB),
        cost_estimate=LIGHT,
        name="first",
    )(
        flag,
        stay(count),
        *(stay(array) if m == 0 else array for array in (acts, weight, table)),
        stay(index),
        stay(pooled),
        stay(delta),
    )


def table_kernel(flag_ref, index_ref, pooled_ref, after_hbm, *refs):
    share, slant, high, kv, sems = refs[-5:]
    count, rows, width = high.shape
    sections = (len(refs) - 5 - 3 * count) // 2
    sources, outs, parts = refs[: 3 * count], refs[3 * count : -5 - sections], refs[-5 - sections : -5]
    table_rows, span = parts[0].shape
    cands = index_ref.shape[2]

    @pl.when(flag_ref[0] == 1)
    def _():
        loads = []
        for m in range(count):
            for k, target in enumerate((share, slant, high)):
                loads.append(pltpu.make_async_copy(sources[k * count + m], target.at[m], sems.at[3 * m + k]))
        for load in loads:
            load.start()
        row = lax.broadcasted_iota(jnp.int32, (table_rows, cands), 0)
        head = lax.broadcasted_iota(jnp.int32, (cands, TILE), 1) >> (HEAD.bit_length() - 1)
        ones = jnp.ones((rows, PAIR), BF16)
        onehot = jnp.concatenate([(row == index_ref[m]).astype(BF16) for m in range(count)], axis=1)

        def by_head(blocks):
            chosen = blocks[0]
            for k in range(1, len(blocks)):
                chosen = jnp.where(head == k, blocks[k], chosen)
            return chosen

        for m in range(count):
            given = pooled_ref[m : m + 1].astype(F32) * (1.0 / rows)
            lines = slice(m * cands, (m + 1) * cands)
            for k in range(3):
                loads[3 * m + k].wait()
            column = dot(share[m], ones, NN)
            column = jnp.concatenate([column, column], axis=1)
            for q in range(width // TILE):
                cols = slice(q * TILE, (q + 1) * TILE)
                key = dot(slant[m, cols], high[m, :, cols], NN) * (1.0 / math.sqrt(HEAD))
                starts = range(0, TILE, cands)
                kv[lines, cols] = by_head([key[at : at + cands] for at in starts])
                value = by_head([column[q * TILE + at : q * TILE + at + cands] for at in starts])
                kv[lines, width + q * TILE : width + (q + 1) * TILE] = value * given[:, cols]
        stores = []
        for k, part in enumerate(parts):
            kv_high, kv_low = high_low(kv[:, k * span : (k + 1) * span])
            part[...] = (dot(onehot, kv_high, NN) + dot(onehot, kv_low, NN)).astype(BF16)
            stores.append(pltpu.make_async_copy(part, outs[k], sems.at[3 * count + k]))
            stores[k].start()
        for store in stores:
            store.wait()


def table_call(flag, index, pooled, table_rows, after, shares, slants, highs, sections):
    rows, width = highs[0].shape
    count = len(highs)
    part = (table_rows, 2 * width // sections)
    return pl.pallas_call(
        table_kernel,
        out_shape=(pltpu.HBM(part, BF16),) * sections,
        in_specs=[SMEM, VMEM, VMEM, HBM] + [HBM] * (3 * count),
        out_specs=(HBM,) * sections,
        scratch_shapes=[pltpu.VMEM(part, BF16)] * sections
        + [
            pltpu.VMEM((count,) + shares[0].shape, BF16),
            pltpu.VMEM((count,) + slants[0].shape, BF16),
            pltpu.VMEM((count,) + highs[0].shape, BF16),
            pltpu.VMEM((count * index.shape[2], 2 * width), F32),
            pltpu.SemaphoreType.DMA((3 * count + sections,)),
        ],
        compiler_params=pltpu.CompilerParams(vmem_limit_bytes=18 * MIB),
        cost_estimate=LIGHT,
        name="table",
    )(flag, index, pooled, stay(after), *map(stay, shares), *map(stay, slants), *map(stay, highs))


def hop_kernel(m, with_grad, flag_ref, came_hbm, delta_in, weight, after_hbm, *rest):
    if with_grad:
        grad_hbm, delta_hbm, came, aux, grad, sems = rest
    else:
        delta_hbm, came, aux, sems = rest
    width = came.shape[1]

    @pl.when(flag_ref[0] == 1)
    def _():
        first = pltpu.make_async_copy(came_hbm, came, sems.at[0])
        second = pltpu.make_async_copy(delta_in.at[m], aux, sems.at[1])
        first.start()
        second.start()
        first.wait()
        second.wait()
        aux[...] = (came[...].astype(F32) * aux[...].astype(F32)).astype(BF16)
        stores = [pltpu.make_async_copy(aux, delta_hbm.at[m], sems.at[2])]
        stores[0].start()
        if with_grad:
            for n in range(width // TILE):
                part = slice(n * TILE, (n + 1) * TILE)
                grad[:, part] = (came[:, part].astype(F32) + dot(aux[...], weight[part, :], NT)).astype(BF16)
            stores.append(pltpu.make_async_copy(grad, grad_hbm, sems.at[3]))
            stores[-1].start()
        for store in stores:
            store.wait()


def hop_call(m, flag, came, delta, weight, after, with_grad):
    rows, width = came.shape
    scratch = [pltpu.VMEM((rows, width), BF16)] * (3 if with_grad else 2)
    scratch.append(pltpu.SemaphoreType.DMA((4,)))
    outs = (pltpu.HBM(delta.shape, BF16),)
    if with_grad:
        outs = (pltpu.HBM((rows, width), BF16),) + outs
    return pl.pallas_call(
        functools.partial(hop_kernel, m, with_grad),
        out_shape=outs,
        in_specs=[SMEM, HBM, HBM, VMEM if with_grad else HBM, HBM],
        out_specs=(HBM,) * len(outs),
        scratch_shapes=scratch,
        input_output_aliases={2: len(outs) - 1},
        compiler_params=pltpu.CompilerParams(vmem_limit_bytes=12 * MIB),
        cost_estimate=LIGHT,
        name="hop" if with_grad else "end",
    )(flag, came, stay(delta), weight if with_grad else stay(weight), stay(after))


def bit_orders(replicas):
    bits = list(range(replicas.bit_length() - 1))
    return [bits, bits[1::-1] + bits[2:]]


def block_order(bits):
    rest = bits[1:]
    order = []
    for i in range(1 << len(rest)):
        order.append(sum(((i >> (len(rest) - 1 - k)) & 1) << bit for k, bit in enumerate(rest)))
    return order


def turn_kernel(acts_hbm, after_hbm, out, token_ref, acts, sems):
    count, rows, width = acts.shape
    token_ref[...] = jnp.zeros_like(token_ref)
    loads = [pltpu.make_async_copy(acts_hbm.at[m], acts.at[m], sems.at[m]) for m in range(count)]
    for load in loads:
        load.start()
    for m in range(count):
        loads[m].wait()
        out[:, m * rows : (m + 1) * rows] = acts[m].T


def turn_call(acts, after):
    count, rows, width = acts.shape
    return pl.pallas_call(
        turn_kernel,
        out_shape=(pltpu.HBM((width, count * rows), BF16), pltpu.HBM((16, 128), BF16)),
        in_specs=[HBM, HBM],
        out_specs=(VMEM,) * 2,
        scratch_shapes=[pltpu.VMEM(acts.shape, BF16), pltpu.SemaphoreType.DMA((count,))],
        compiler_params=pltpu.CompilerParams(vmem_limit_bytes=14 * MIB),
        cost_estimate=LIGHT,
        name="turn",
    )(stay(acts), stay(after))


def picked_rows(turned, number, bits, which, size, columns):
    mine = (number >> bits[0]) & 1
    base = (mine if which else 1 - mine) << bits[0]
    return jnp.concatenate(
        [turned[pl.ds(pl.multiple_of((base + block) * size, size), size), columns] for block in block_order(bits)],
        axis=0,
    )


def early_kernel(replicas, number_ref, turned_hbm, delta_hbm, *refs):
    outs, (turned, delta, sems) = refs[:2], refs[2:]
    micros, rows, width = delta.shape
    half = width // 2
    loads = [pltpu.make_async_copy(delta_hbm.at[m], delta.at[m], sems.at[m]) for m in range(micros)]
    loads.append(pltpu.make_async_copy(turned_hbm.at[:, pl.ds(0, micros * rows)], turned, sems.at[micros]))
    for load in loads:
        load.start()
    for load in loads:
        load.wait()
    flat = delta.reshape(micros * rows, width)
    for c, bits in enumerate(bit_orders(replicas)):
        left = picked_rows(turned, number_ref[0], bits, 0, width // replicas, slice(0, micros * rows))
        for at in range(0, half, TILE):
            outs[c][:, at : at + TILE] = dot(left, flat[:, c * half + at : c * half + at + TILE], NN)


def early_call(number, turned, delta, replicas):
    micros, rows, width = delta.shape
    half = jax.ShapeDtypeStruct((width // 2, width // 2), F32)
    return pl.pallas_call(
        functools.partial(early_kernel, replicas),
        out_shape=(half,) * 2,
        in_specs=[SMEM, HBM, HBM],
        out_specs=(VMEM,) * 2,
        scratch_shapes=[
            pltpu.VMEM((width, (micros - 1) * rows), BF16),
            pltpu.VMEM((micros - 1, rows, width), BF16),
            pltpu.SemaphoreType.DMA((micros,)),
        ],
        compiler_params=pltpu.CompilerParams(vmem_limit_bytes=18 * MIB),
        cost_estimate=LIGHT,
        name="early",
    )(number, stay(turned), stay(delta))


def weight_kernel(replicas, which, flag_ref, number_ref, turned_hbm, delta_hbm, came, *refs):
    early, outs, (turned, delta, sems) = refs[:-5], refs[-5:-3], refs[-3:]
    micros, rows, width = delta_hbm.shape
    half = width // 2
    begin = micros - 1 if early else 0
    loads = [
        pltpu.make_async_copy(delta_hbm.at[m], delta.at[pl.ds((m - begin) * rows, rows)], sems.at[m - begin])
        for m in range(begin, micros)
    ]
    columns = pl.ds(begin * rows, (micros - begin) * rows)
    loads.append(pltpu.make_async_copy(turned_hbm.at[:, columns], turned, sems.at[micros - begin]))
    for load in loads:
        load.start()
    for load in loads:
        load.wait()

    @pl.when(flag_ref[0] == 1)
    def _():
        tail = pl.ds((micros - 1 - begin) * rows, rows)
        delta[tail] = (came[...].astype(F32) * delta[tail].astype(F32)).astype(BF16)

    for c, bits in enumerate(bit_orders(replicas)):
        left = picked_rows(turned, number_ref[0], bits, which, width // replicas, slice(None))
        for at in range(0, half, TILE):
            product = dot(left, delta[:, c * half + at : c * half + at + TILE], NN)
            if early:
                product = early[c][:, at : at + TILE] + product
            outs[c][:, at : at + TILE] = product.astype(outs[c].dtype)


def weight_call(which, flag, number, turned, delta, came, early, replicas):
    micros, rows, width = delta.shape
    half = (width // 2, width // 2)
    taken = 1 if early else micros
    return pl.pallas_call(
        functools.partial(weight_kernel, replicas, which),
        out_shape=(jax.ShapeDtypeStruct(half, F32) if which else pltpu.HBM(half, BF16),) * 2,
        in_specs=[SMEM, SMEM, HBM, HBM] + [VMEM] * (1 + len(early)),
        out_specs=(VMEM,) * 2,
        scratch_shapes=[
            pltpu.VMEM((width, taken * rows), BF16),
            pltpu.VMEM((taken * rows, width), BF16),
            pltpu.SemaphoreType.DMA((taken + 1,)),
        ],
        compiler_params=pltpu.CompilerParams(vmem_limit_bytes=18 * MIB),
        cost_estimate=LIGHT,
        name="weight",
    )(flag, number, stay(turned), stay(delta), came, *early)


def own_half(keep, got, bit):
    mine = (lax.axis_index("dp") >> bit) & 1

    def pick(which):
        return lax.dynamic_index_in_dim(keep, which, 0, keepdims=False) + lax.dynamic_index_in_dim(
            got, which, 0, keepdims=False
        ).astype(F32)

    return pick(1 - mine).astype(BF16), pick(mine)


def scatter_sums(sends, keeps, table, orders, pairs_of):
    steps = len(orders[0])
    sends, keeps = list(sends), list(keeps)
    for n in range(steps):
        gots = [lax.ppermute(send, "dp", pairs_of(bits[n])) for send, bits in zip(sends, orders)]
        for c, bits in enumerate(orders):
            if n + 1 < steps:
                lead = (2, keeps[c].shape[0] // 2, keeps[c].shape[1])
                sends[c], keeps[c] = own_half(keeps[c].reshape(lead), gots[c].reshape(lead), bits[n + 1])
        if n == 0:
            table, _ = lax.optimization_barrier((table, tuple(sends)))
    blocks = lax.all_to_all(table.reshape(1 << steps, -1, table.shape[1]), "dp", 0, 0)
    sums = [keep + got.astype(F32) for keep, got in zip(keeps, gots)]
    return jnp.concatenate(sums, axis=1), jnp.sum(blocks.astype(F32), axis=0)


def body(activations, section_weights, cand_table, cand_index, cand_count, pooled_cotangent):
    sections = lax.axis_size("section")
    replicas = lax.axis_size("dp")
    position = lax.axis_index("section")
    replica = lax.axis_index("dp")
    last = sections - 1
    final_flag = position == last
    acts = activations[0]
    weight = section_weights[0]
    micro_count, row_count, model_width = acts.shape

    def flag(truth):
        return truth.astype(jnp.int32).reshape(1)

    number = replica.reshape(1)
    count = cand_count.reshape(1, micro_count)
    pooled = pooled_cotangent.reshape(micro_count, model_width)
    final = flag(final_flag)
    grads, shares, slants, highs = [], [], [], []
    delta = acts
    for m in range(micro_count):
        grad, delta, share, slant, high = first_call(
            m, final, count, acts, weight, cand_table, cand_index, pooled, delta
        )
        grads.append(grad)
        shares.append(share)
        slants.append(slant)
        highs.append(high)

    def pairs(bit):
        return [(i, i ^ (1 << bit)) for i in range(replicas)]

    for hop in range(last):
        source = last - hop
        received = [lax.ppermute(g, "section", [(source, source - 1)]) for g in grads]
        active = flag(position == source - 1)
        for m in range(micro_count):
            if hop + 1 < last:
                after = token if hop == 1 and m == 0 else acts
                grads[m], delta = hop_call(m, active, received[m], delta, weight, after, True)
            elif m + 1 < micro_count:
                (delta,) = hop_call(m, active, received[m], delta, weight, acts, False)
        if hop == 0:
            parts = table_call(
                final, cand_index, pooled, cand_table.shape[0], grads[-1], shares, slants, highs, sections
            )
            turned, token = turn_call(acts, grads[-1])

    spread = [lax.ppermute(parts[s], "section", [(last, s)]) for s in range(last)]
    table_part = jnp.where(final_flag, parts[last], sum(spread))

    orders = bit_orders(replicas)
    early = early_call(number, turned, delta, replicas)
    sends = weight_call(0, active, number, turned, delta, received[-1], early, replicas)
    keeps = weight_call(1, active, number, turned, delta, received[-1], (), replicas)
    sums, table_sum = scatter_sums(sends, keeps, table_part, orders, pairs)
    return sums[None], table_sum


def solution(mesh):
    in_specs = (
        P("section", None, "dp", None),
        P("section", None, None),
        P(),
        P(None, "dp", None),
        P(None, "dp"),
        P(None, "dp", None),
    )
    out_specs = (P("section", "dp", None), P("dp", "section"))
    return jax.shard_map(body, mesh=mesh, in_specs=in_specs, out_specs=out_specs, check_vma=False)
```

```python
import functools
import math

import jax
import jax.numpy as jnp
from jax import lax
from jax.experimental import pallas as pl
from jax.experimental.pallas import tpu as pltpu
from jax.sharding import PartitionSpec as P

HEAD = 64
PAIR = 2 * HEAD
TILE = 256
MIB = 1024 * 1024
HBM = pl.BlockSpec(memory_space=pltpu.HBM)
VMEM = pl.BlockSpec(memory_space=pltpu.VMEM)
SMEM = pl.BlockSpec(memory_space=pltpu.SMEM)
BF16 = jnp.bfloat16
F32 = jnp.float32
LIGHT = pl.CostEstimate(flops=1024, bytes_accessed=1024, transcendentals=0)

NN = (((1,), (0,)), ((), ()))
NT = (((1,), (1,)), ((), ()))
TN = (((0,), (0,)), ((), ()))


def dot(left, right, dims):
    return lax.dot_general(left, right, dims, preferred_element_type=F32)


def gelu_parts(hidden):
    root = math.sqrt(2.0 / math.pi)
    square = hidden * hidden
    bent = jnp.tanh(root * hidden * (1.0 + 0.044715 * square))
    share = 0.5 + 0.5 * bent
    slope = share + (0.5 * root) * hidden * (1.0 - bent * bent) * (1.0 + (3 * 0.044715) * square)
    return hidden * share, slope


def high_low(values):
    high = values.astype(BF16)
    return high, (values - high.astype(F32)).astype(BF16)


def stay(array):
    return pltpu.with_memory_space_constraint(array, pltpu.HBM)


def own_heads(width):
    shift = HEAD.bit_length() - 1
    row = lax.broadcasted_iota(jnp.int32, (PAIR, width), 0) >> shift
    return row == ((lax.broadcasted_iota(jnp.int32, (PAIR, width), 1) >> shift) & 1)


def first_kernel(
    m, flag_ref, count_hbm, acts_in, weight_in, table_in, index_hbm, pooled_hbm, delta_in,
    grad_hbm, delta_hbm, share_hbm, slant_hbm, high_hbm,
    count_ref, acts_buf, weight_buf, table_buf, index_ref, pooled_ref, grad, aux, share_ref, slant_ref, high_ref, sems,
):
    micros, rows, width = acts_in.shape
    table_rows = table_in.shape[0]
    pairs = width // PAIR
    tiles = width // TILE
    tile = [slice(q * TILE, (q + 1) * TILE) for q in range(tiles)]
    pair = [slice(j * PAIR, (j + 1) * PAIR) for j in range(pairs)]

    def copy(source, target, at):
        started = pltpu.make_async_copy(source, target, sems.at[at])
        started.start()
        return started

    if m == 0:
        acts_ref, weight, table = acts_buf, weight_buf, table_buf

        @pl.when(flag_ref[0] == 0)
        def _():
            load_weight = copy(weight_in, weight, 0)
            loads = [copy(acts_in.at[k], acts_ref.at[k], 1 + k) for k in range(micros)]
            load_weight.wait()
            stores = []
            for k in range(micros):
                loads[k].wait()
                for cols in tile:
                    hidden = dot(acts_ref[k], weight[:, cols], NN)
                    aux[k, :, cols] = gelu_parts(hidden)[1].astype(BF16)
                stores.append(copy(aux.at[k], delta_hbm.at[k], 1 + micros + k))
            for store in stores:
                store.wait()

    else:
        acts_ref, weight, table = acts_in, weight_in, table_in

    @pl.when(flag_ref[0] == 1)
    def _():
        loads = [copy(index_hbm, index_ref, 0), copy(pooled_hbm, pooled_ref, 1), copy(count_hbm, count_ref, 2)]
        if m == 0:
            loads.append(copy(table_in, table, 3))
            load_weight = copy(weight_in, weight, 4)
            load_acts = copy(acts_in.at[0], acts_ref.at[0], 5)
            load_acts.wait()
            load_weight.wait()
        acts = acts_ref.at[m]
        slopes, lows = [], []
        for cols in tile:
            hidden = dot(acts[...], weight[:, cols], NN)
            bent, slope = gelu_parts(hidden)
            high, low = high_low(acts[:, cols].astype(F32) + bent)
            high_ref[:, cols] = high
            slopes.append(slope)
            lows.append(low)
        store_high = copy(high_ref, high_hbm, 6)
        for load in loads:
            load.wait()
        index = index_ref[m]
        index = jnp.concatenate([index, index], axis=1)
        onehot = (lax.broadcasted_iota(jnp.int32, (table_rows, PAIR), 0) == index).astype(BF16)
        gathered = dot(onehot, table[...], TN)
        own = own_heads(width)
        keys = jnp.where(own, gathered[:, :width] * (1.0 / math.sqrt(HEAD)), 0.0).astype(BF16)
        values = jnp.where(own, gathered[:, width:], 0.0).astype(BF16)
        allowed = lax.broadcasted_iota(jnp.int32, (2, HEAD, rows), 1) < count_ref[0, m]
        given_row = pooled_ref[m : m + 1].astype(F32) * (1.0 / rows)
        given = jnp.broadcast_to(given_row, (rows, width)).astype(BF16)
        scores = []
        for j, here in enumerate(pair):
            part = slice(j * PAIR % TILE, j * PAIR % TILE + PAIR)
            scores.append(
                dot(
                    jnp.concatenate([keys[:, here], keys[:, here]], axis=1),
                    jnp.concatenate([high_ref[:, here], lows[j * PAIR // TILE][:, part]], axis=1),
                    NT,
                )
            )
        slants = []
        for j, here in enumerate(pair):
            share, slant = soften(scores[j], dot(values[:, here], given[:, here], NT), allowed)
            share_ref[here] = share
            slant_ref[here] = slant
            slants.append(slant)
        store_share = copy(share_ref, share_hbm, 7)
        store_slant = copy(slant_ref, slant_hbm, 10)
        totals = []
        for j, here in enumerate(pair):
            part = slice(j * PAIR % TILE, j * PAIR % TILE + PAIR)
            total = given_row[:, here] + dot(slants[j], keys[:, here], TN)
            totals.append(total)
            aux[0, :, here] = (total * slopes[j * PAIR // TILE][:, part]).astype(BF16)
        store_aux = copy(aux.at[0], delta_hbm.at[m], 8)
        for q, cols in enumerate(tile):
            total = jnp.concatenate(totals[q * TILE // PAIR : (q + 1) * TILE // PAIR], axis=1)
            grad[:, cols] = (total + dot(aux[0], weight[cols, :], NT)).astype(BF16)
        store_grad = copy(grad, grad_hbm, 9)
        store_high.wait()
        store_share.wait()
        store_slant.wait()
        store_aux.wait()
        store_grad.wait()


def lean(share, worth):
    worth = worth.reshape(share.shape)
    centre = jnp.sum(share * worth, axis=1, keepdims=True)
    return (share * (worth - centre)).reshape(worth.shape[0] * worth.shape[1], -1).astype(BF16)


def soften(score, worth, allowed):
    score = jnp.where(allowed, score.reshape(allowed.shape), -1e30)
    raised = jnp.exp(score - jnp.max(score, axis=1, keepdims=True))
    share = raised * (1.0 / jnp.sum(raised, axis=1, keepdims=True))
    return share.reshape(worth.shape).astype(BF16), lean(share, worth)


def first_call(m, flag, count, acts, weight, table, index, pooled, delta):
    micros, rows, width = acts.shape
    turned = (width // HEAD * index.shape[2], rows)
    block = pltpu.HBM((rows, width), BF16)
    big = HBM if m == 0 else VMEM
    small = pltpu.VMEM((8, 128), BF16)
    return pl.pallas_call(
        functools.partial(first_kernel, m),
        out_shape=(block, pltpu.HBM(acts.shape, BF16), pltpu.HBM(turned, BF16), pltpu.HBM(turned, BF16), block),
        in_specs=[SMEM, HBM, big, big, big, HBM, HBM, HBM],
        out_specs=(HBM,) * 5,
        scratch_shapes=[
            pltpu.SMEM(count.shape, jnp.int32),
            pltpu.VMEM(acts.shape, BF16) if m == 0 else small,
            pltpu.VMEM(weight.shape, BF16) if m == 0 else small,
            pltpu.VMEM(table.shape, BF16) if m == 0 else small,
            pltpu.VMEM(index.shape, jnp.int32),
            pltpu.VMEM(pooled.shape, BF16),
            pltpu.VMEM((rows, width), BF16),
            pltpu.VMEM((micros if m == 0 else 1, rows, width), BF16),
            pltpu.VMEM(turned, BF16),
            pltpu.VMEM(turned, BF16),
            pltpu.VMEM((rows, width), BF16),
            pltpu.SemaphoreType.DMA((max(11, 1 + 2 * micros),)),
        ],
        input_output_aliases={} if m == 0 else {7: 1},
        compiler_params=pltpu.CompilerParams(vmem_limit_bytes=18 * MIB),
        cost_estimate=LIGHT,
        name="first",
    )(
        flag,
        stay(count),
        *(stay(array) if m == 0 else array for array in (acts, weight, table)),
        stay(index),
        stay(pooled),
        stay(delta),
    )


def table_kernel(flag_ref, index_ref, pooled_ref, after_hbm, *refs):
    share, slant, high, kv, sems = refs[-5:]
    count, rows, width = high.shape
    sections = (len(refs) - 5 - 3 * count) // 2
    sources, outs, parts = refs[: 3 * count], refs[3 * count : -5 - sections], refs[-5 - sections : -5]
    table_rows, span = parts[0].shape
    cands = index_ref.shape[2]

    @pl.when(flag_ref[0] == 1)
    def _():
        loads = []
        for m in range(count):
            for k, target in enumerate((share, slant, high)):
                loads.append(pltpu.make_async_copy(sources[k * count + m], target.at[m], sems.at[3 * m + k]))
        for load in loads:
            load.start()
        row = lax.broadcasted_iota(jnp.int32, (table_rows, cands), 0)
        head = lax.broadcasted_iota(jnp.int32, (cands, TILE), 1) >> (HEAD.bit_length() - 1)
        ones = jnp.ones((rows, PAIR), BF16)
        onehot = jnp.concatenate([(row == index_ref[m]).astype(BF16) for m in range(count)], axis=1)

        def by_head(blocks):
            chosen = blocks[0]
            for k in range(1, len(blocks)):
                chosen = jnp.where(head == k, blocks[k], chosen)
            return chosen

        for m in range(count):
            given = pooled_ref[m : m + 1].astype(F32) * (1.0 / rows)
            lines = slice(m * cands, (m + 1) * cands)
            for k in range(3):
                loads[3 * m + k].wait()
            column = dot(share[m], ones, NN)
            column = jnp.concatenate([column, column], axis=1)
            for q in range(width // TILE):
                cols = slice(q * TILE, (q + 1) * TILE)
                key = dot(slant[m, cols], high[m, :, cols], NN) * (1.0 / math.sqrt(HEAD))
                starts = range(0, TILE, cands)
                kv[lines, cols] = by_head([key[at : at + cands] for at in starts])
                value = by_head([column[q * TILE + at : q * TILE + at + cands] for at in starts])
                kv[lines, width + q * TILE : width + (q + 1) * TILE] = value * given[:, cols]
        stores = []
        for k, part in enumerate(parts):
            kv_high, kv_low = high_low(kv[:, k * span : (k + 1) * span])
            part[...] = (dot(onehot, kv_high, NN) + dot(onehot, kv_low, NN)).astype(BF16)
            stores.append(pltpu.make_async_copy(part, outs[k], sems.at[3 * count + k]))
            stores[k].start()
        for store in stores:
            store.wait()


def table_call(flag, index, pooled, table_rows, after, shares, slants, highs, sections):
    rows, width = highs[0].shape
    count = len(highs)
    part = (table_rows, 2 * width // sections)
    return pl.pallas_call(
        table_kernel,
        out_shape=(pltpu.HBM(part, BF16),) * sections,
        in_specs=[SMEM, VMEM, VMEM, HBM] + [HBM] * (3 * count),
        out_specs=(HBM,) * sections,
        scratch_shapes=[pltpu.VMEM(part, BF16)] * sections
        + [
            pltpu.VMEM((count,) + shares[0].shape, BF16),
            pltpu.VMEM((count,) + slants[0].shape, BF16),
            pltpu.VMEM((count,) + highs[0].shape, BF16),
            pltpu.VMEM((count * index.shape[2], 2 * width), F32),
            pltpu.SemaphoreType.DMA((3 * count + sections,)),
        ],
        compiler_params=pltpu.CompilerParams(vmem_limit_bytes=18 * MIB),
        cost_estimate=LIGHT,
        name="table",
    )(flag, index, pooled, stay(after), *map(stay, shares), *map(stay, slants), *map(stay, highs))


def hop_kernel(m, with_grad, fetch, flag_ref, came_hbm, delta_in, weight_in, after_hbm, *rest):
    weight = weight_in
    if fetch:
        rest, weight = rest[:-1], rest[-1]
    if with_grad:
        grad_hbm, delta_hbm, came, aux, grad, sems = rest
    else:
        delta_hbm, came, aux, sems = rest
    width = came.shape[1]

    @pl.when(flag_ref[0] == 1)
    def _():
        first = pltpu.make_async_copy(came_hbm, came, sems.at[0])
        third = pltpu.make_async_copy(weight_in, weight, sems.at[4]) if fetch else None
        second = pltpu.make_async_copy(delta_in.at[m], aux, sems.at[1])
        first.start()
        second.start()
        if fetch:
            third.start()
        first.wait()
        second.wait()
        aux[...] = (came[...].astype(F32) * aux[...].astype(F32)).astype(BF16)
        stores = [pltpu.make_async_copy(aux, delta_hbm.at[m], sems.at[2])]
        stores[0].start()
        if fetch:
            third.wait()
        if with_grad:
            for n in range(width // TILE):
                part = slice(n * TILE, (n + 1) * TILE)
                grad[:, part] = (came[:, part].astype(F32) + dot(aux[...], weight[part, :], NT)).astype(BF16)
            stores.append(pltpu.make_async_copy(grad, grad_hbm, sems.at[3]))
            stores[-1].start()
        for store in stores:
            store.wait()


def hop_call(m, flag, came, delta, weight, after, with_grad, fetch=False):
    rows, width = came.shape
    scratch = [pltpu.VMEM((rows, width), BF16)] * (3 if with_grad else 2)
    scratch.append(pltpu.SemaphoreType.DMA((5,)))
    if fetch:
        scratch.append(pltpu.VMEM(weight.shape, BF16))
    held = with_grad and not fetch
    outs = (pltpu.HBM(delta.shape, BF16),)
    if with_grad:
        outs = (pltpu.HBM((rows, width), BF16),) + outs
    return pl.pallas_call(
        functools.partial(hop_kernel, m, with_grad, fetch),
        out_shape=outs,
        in_specs=[SMEM, HBM, HBM, VMEM if held else HBM, HBM],
        out_specs=(HBM,) * len(outs),
        scratch_shapes=scratch,
        input_output_aliases={2: len(outs) - 1},
        compiler_params=pltpu.CompilerParams(vmem_limit_bytes=12 * MIB),
        cost_estimate=LIGHT,
        name="hop" if with_grad else "end",
    )(flag, came, stay(delta), weight if held else stay(weight), stay(after))


def bit_orders(replicas):
    bits = list(range(replicas.bit_length() - 1))
    return [bits, bits[1::-1] + bits[2:]]


def block_order(bits):
    rest = bits[1:]
    order = []
    for i in range(1 << len(rest)):
        order.append(sum(((i >> (len(rest) - 1 - k)) & 1) << bit for k, bit in enumerate(rest)))
    return order


def turn_kernel(acts_hbm, after_hbm, out, token_ref, acts, sems):
    count, rows, width = acts.shape
    token_ref[...] = jnp.zeros_like(token_ref)
    loads = [pltpu.make_async_copy(acts_hbm.at[m], acts.at[m], sems.at[m]) for m in range(count)]
    for load in loads:
        load.start()
    for m in range(count):
        loads[m].wait()
        out[:, m * rows : (m + 1) * rows] = acts[m].T


def turn_call(acts, after):
    count, rows, width = acts.shape
    return pl.pallas_call(
        turn_kernel,
        out_shape=(pltpu.HBM((width, count * rows), BF16), pltpu.HBM((16, 128), BF16)),
        in_specs=[HBM, HBM],
        out_specs=(VMEM,) * 2,
        scratch_shapes=[pltpu.VMEM(acts.shape, BF16), pltpu.SemaphoreType.DMA((count,))],
        compiler_params=pltpu.CompilerParams(vmem_limit_bytes=14 * MIB),
        cost_estimate=LIGHT,
        name="turn",
    )(stay(acts), stay(after))


def picked_rows(turned, number, bits, which, size, columns):
    mine = (number >> bits[0]) & 1
    base = (mine if which else 1 - mine) << bits[0]
    return jnp.concatenate(
        [turned[pl.ds(pl.multiple_of((base + block) * size, size), size), columns] for block in block_order(bits)],
        axis=0,
    )


def early_kernel(replicas, number_ref, turned_hbm, delta_hbm, *refs):
    outs, (turned, delta, sems) = refs[:2], refs[2:]
    micros, rows, width = delta.shape
    half = width // 2
    loads = [pltpu.make_async_copy(delta_hbm.at[m], delta.at[m], sems.at[m]) for m in range(micros)]
    loads.append(pltpu.make_async_copy(turned_hbm.at[:, pl.ds(0, micros * rows)], turned, sems.at[micros]))
    for load in loads:
        load.start()
    for load in loads:
        load.wait()
    flat = delta.reshape(micros * rows, width)
    for c, bits in enumerate(bit_orders(replicas)):
        left = picked_rows(turned, number_ref[0], bits, 0, width // replicas, slice(0, micros * rows))
        for at in range(0, half, TILE):
            outs[c][:, at : at + TILE] = dot(left, flat[:, c * half + at : c * half + at + TILE], NN)


def early_call(number, turned, delta, replicas):
    micros, rows, width = delta.shape
    half = jax.ShapeDtypeStruct((width // 2, width // 2), F32)
    return pl.pallas_call(
        functools.partial(early_kernel, replicas),
        out_shape=(half,) * 2,
        in_specs=[SMEM, HBM, HBM],
        out_specs=(VMEM,) * 2,
        scratch_shapes=[
            pltpu.VMEM((width, (micros - 1) * rows), BF16),
            pltpu.VMEM((micros - 1, rows, width), BF16),
            pltpu.SemaphoreType.DMA((micros,)),
        ],
        compiler_params=pltpu.CompilerParams(vmem_limit_bytes=18 * MIB),
        cost_estimate=LIGHT,
        name="early",
    )(number, stay(turned), stay(delta))


def weight_kernel(replicas, which, flag_ref, number_ref, turned_hbm, delta_hbm, came, *refs):
    early, outs, (turned, delta, sems) = refs[:-5], refs[-5:-3], refs[-3:]
    micros, rows, width = delta_hbm.shape
    half = width // 2
    begin = micros - 1 if early else 0
    loads = [
        pltpu.make_async_copy(delta_hbm.at[m], delta.at[pl.ds((m - begin) * rows, rows)], sems.at[m - begin])
        for m in range(begin, micros)
    ]
    columns = pl.ds(begin * rows, (micros - begin) * rows)
    loads.append(pltpu.make_async_copy(turned_hbm.at[:, columns], turned, sems.at[micros - begin]))
    for load in loads:
        load.start()
    for load in loads:
        load.wait()

    @pl.when(flag_ref[0] == 1)
    def _():
        tail = pl.ds((micros - 1 - begin) * rows, rows)
        delta[tail] = (came[...].astype(F32) * delta[tail].astype(F32)).astype(BF16)

    for c, bits in enumerate(bit_orders(replicas)):
        left = picked_rows(turned, number_ref[0], bits, which, width // replicas, slice(None))
        for at in range(0, half, TILE):
            product = dot(left, delta[:, c * half + at : c * half + at + TILE], NN)
            if early:
                product = early[c][:, at : at + TILE] + product
            outs[c][:, at : at + TILE] = product.astype(outs[c].dtype)


def weight_call(which, flag, number, turned, delta, came, early, replicas):
    micros, rows, width = delta.shape
    half = (width // 2, width // 2)
    taken = 1 if early else micros
    return pl.pallas_call(
        functools.partial(weight_kernel, replicas, which),
        out_shape=(jax.ShapeDtypeStruct(half, F32) if which else pltpu.HBM(half, BF16),) * 2,
        in_specs=[SMEM, SMEM, HBM, HBM] + [VMEM] * (1 + len(early)),
        out_specs=(VMEM,) * 2,
        scratch_shapes=[
            pltpu.VMEM((width, taken * rows), BF16),
            pltpu.VMEM((taken * rows, width), BF16),
            pltpu.SemaphoreType.DMA((taken + 1,)),
        ],
        compiler_params=pltpu.CompilerParams(vmem_limit_bytes=18 * MIB),
        cost_estimate=LIGHT,
        name="weight",
    )(flag, number, stay(turned), stay(delta), came, *early)


def own_half(keep, got, bit):
    mine = (lax.axis_index("dp") >> bit) & 1

    def pick(which):
        return lax.dynamic_index_in_dim(keep, which, 0, keepdims=False) + lax.dynamic_index_in_dim(
            got, which, 0, keepdims=False
        ).astype(F32)

    return pick(1 - mine).astype(BF16), pick(mine)


def scatter_sums(sends, keeps, table, orders, pairs_of):
    steps = len(orders[0])
    sends, keeps = list(sends), list(keeps)
    for n in range(steps):
        gots = [lax.ppermute(send, "dp", pairs_of(bits[n])) for send, bits in zip(sends, orders)]
        for c, bits in enumerate(orders):
            if n + 1 < steps:
                lead = (2, keeps[c].shape[0] // 2, keeps[c].shape[1])
                sends[c], keeps[c] = own_half(keeps[c].reshape(lead), gots[c].reshape(lead), bits[n + 1])
        if n == 0:
            table, _ = lax.optimization_barrier((table, tuple(sends)))
    blocks = lax.all_to_all(table.reshape(1 << steps, -1, table.shape[1]), "dp", 0, 0)
    sums = [keep + got.astype(F32) for keep, got in zip(keeps, gots)]
    return jnp.concatenate(sums, axis=1), jnp.sum(blocks.astype(F32), axis=0)


def body(activations, section_weights, cand_table, cand_index, cand_count, pooled_cotangent):
    sections = lax.axis_size("section")
    replicas = lax.axis_size("dp")
    position = lax.axis_index("section")
    replica = lax.axis_index("dp")
    last = sections - 1
    final_flag = position == last
    acts = activations[0]
    weight = section_weights[0]
    micro_count, row_count, model_width = acts.shape

    def flag(truth):
        return truth.astype(jnp.int32).reshape(1)

    number = replica.reshape(1)
    count = cand_count.reshape(1, micro_count)
    pooled = pooled_cotangent.reshape(micro_count, model_width)
    final = flag(final_flag)
    grads, shares, slants, highs = [], [], [], []
    delta = acts
    for m in range(micro_count):
        grad, delta, share, slant, high = first_call(
            m, final, count, acts, weight, cand_table, cand_index, pooled, delta
        )
        grads.append(grad)
        shares.append(share)
        slants.append(slant)
        highs.append(high)

    def pairs(bit):
        return [(i, i ^ (1 << bit)) for i in range(replicas)]

    for hop in range(last):
        source = last - hop
        received = [lax.ppermute(g, "section", [(source, source - 1)]) for g in grads]
        active = flag(position == source - 1)
        for m in range(micro_count):
            if hop + 1 < last:
                after = token if hop == 1 and m == 0 else acts
                grads[m], delta = hop_call(m, active, received[m], delta, weight, after, True, hop == 0 and m == 0)
            elif m + 1 < micro_count:
                (delta,) = hop_call(m, active, received[m], delta, weight, acts, False)
        if hop == 0:
            parts = table_call(
                final, cand_index, pooled, cand_table.shape[0], grads[-1], shares, slants, highs, sections
            )
            turned, token = turn_call(acts, grads[-1])

    spread = [lax.ppermute(parts[s], "section", [(last, s)]) for s in range(last)]
    table_part = jnp.where(final_flag, parts[last], sum(spread))

    orders = bit_orders(replicas)
    early = early_call(number, turned, delta, replicas)
    sends = weight_call(0, active, number, turned, delta, received[-1], early, replicas)
    keeps = weight_call(1, active, number, turned, delta, received[-1], (), replicas)
    sums, table_sum = scatter_sums(sends, keeps, table_part, orders, pairs)
    return sums[None], table_sum


def solution(mesh):
    in_specs = (
        P("section", None, "dp", None),
        P("section", None, None),
        P(),
        P(None, "dp", None),
        P(None, "dp"),
        P(None, "dp", None),
    )
    out_specs = (P("section", "dp", None), P("dp", "section"))
    return jax.shard_map(body, mesh=mesh, in_specs=in_specs, out_specs=out_specs, check_vma=False)
```
